32 devices in a mesh: grp: 2 (over y), tile: 4 (over z), row: 2 (over x), sub: 2 (over core).
Axes of the slice: x: 2, y: 2, z: 4, core: 2. Of those that a mesh axis runs over, the one named last changes fastest.
Arguments:
- velocity: float32 [2, 480, 960], P(None, ('grp', 'row'), ('tile', 'sub')), parts along dimension 1, may hold values from -10 to 10, as said below
- wet_bits: int32 [16, 960], P(('grp', 'row'), ('tile', 'sub')), parts along dimension 0, may hold values from 0 to 1073741823, as said below
- east_face: int32 [4], replicated, may hold values from 0 to 3, as said below
- seam_turn: int32 [4], replicated, may hold values from 0 to 3
Outputs:
- forcing: float32 [2, 120, 240], P(None, ('grp', 'row'), ('tile', 'sub')), parts along dimension 1
The draws below stay inside these ranges and needn't reach their ends.
There are 2 independent parts, one for each index of `grp`. The reference program is written for one: setup_inputs(seed, part) draws one part's arguments, and reference() takes and returns one part's arrays. A program takes and returns all parts, laid end to end along the dimension named above; an argument that names none is the same for every part. Nothing has to cross between parts.
Inputs may be any that keep to these rules, and one draw needn't show every extreme that they name: `velocity`: gentle combinations of a few waves plus independent cell-to-cell parts. Bit b of wet_bits[j, x] is 1 where cell (30 j + b, x) is wet and 0 on land. `east_face`: each face is east of exactly one face.
All inputs are finite; a program needn't handle non-finite values.
Results may differ from the reference program's by a relative error of at most 0.000098.
Values sent between devices are 32-bit elements; how exact they have to be, the bound alone decides.
No kernel may reach another device: no remote copies, remote signals or barrier semaphores. Data moves between devices by JAX's collectives and lax.ppermute only.
A program may use at most 64 MiB of HBM per device.

```python
import jax
import jax.numpy as jnp
from jax import lax

CX = 120
R = 32
FACES = 4
NY = 240
NX = 960
N_SUB = 2


def draw_velocity(key, part):
    keys = jax.random.split(key, 5)
    full_shape = (2, NY, NX)
    rough = jnp.clip(jax.random.normal(keys[0], full_shape, jnp.float32), -4.0, 4.0)
    row_index = jnp.arange(NY, dtype=jnp.float32)[:, None]
    col_index = jnp.arange(NX, dtype=jnp.float32)[None, :]
    wave_x = jax.random.randint(keys[1], (2, 4), 1, 5).astype(jnp.float32)
    wave_y = jax.random.randint(keys[2], (2, 4), 1, 5).astype(jnp.float32)
    phases = jax.random.uniform(keys[3], (2, 4), jnp.float32, -3.14159, 3.14159)
    amplitude = jax.random.uniform(keys[4], (2, 4), jnp.float32, -1.5, 1.5)
    smooth = jnp.zeros(full_shape, jnp.float32)
    for mode in range(4):
        angle = 6.2831853 * (wave_x[:, mode, None, None] * col_index / 256.0 + wave_y[:, mode, None, None] * row_index / 256.0) + phases[:, mode, None, None]
        smooth = smooth + amplitude[:, mode, None, None] * jnp.sin(angle)
    return (rough + smooth).astype(jnp.float32)


def draw_wet_bits(key, part):
    row_index = jnp.arange(NY, dtype=jnp.int32)[:, None]
    col_index = jnp.arange(NX, dtype=jnp.int32)[None, :]
    land = jax.random.randint(jax.random.fold_in(key, 99), (NY, NX), 0, 20) == 0
    for box_index in range(10):
        box_key = jax.random.split(jax.random.fold_in(key, box_index), 4)
        top = jax.random.randint(box_key[0], (), 0, NY)
        height = jax.random.randint(box_key[1], (), NY // 10, NY // 2)
        left = jax.random.randint(box_key[2], (), 0, NX)
        breadth = jax.random.randint(box_key[3], (), NX // 20, NX // 4)
        inside = (row_index >= top) & (row_index < top + height) & (col_index >= left) & (col_index < left + breadth)
        land = land | inside
    wet = jnp.where(land, 0, 1).astype(jnp.int32)
    shifts = jnp.left_shift(jnp.ones((30,), jnp.int32), jnp.arange(30, dtype=jnp.int32))
    packed = jnp.sum(wet.reshape(NY // 30, 30, NX) * shifts[None, :, None], axis=1)
    return packed.astype(jnp.int32)


def draw_east_face(key, part):
    keys = jax.random.split(key, 2)
    perm = jax.random.permutation(keys[0], FACES).astype(jnp.int32)
    start = jax.random.randint(keys[1], (), 0, FACES).astype(jnp.int32)
    target = ((start + FACES // 2) % FACES).astype(jnp.int32)
    positions = jnp.arange(FACES, dtype=jnp.int32)
    where_target = jnp.sum(jnp.where(perm == target, positions, 0)).astype(jnp.int32)
    previous = perm[start]
    return perm.at[where_target].set(previous).at[start].set(target).astype(jnp.int32)


def place_ends(values, rng, low, high):
    shape = values.shape
    index_at = [jax.random.randint(jax.random.fold_in(rng, axis), (), 0, shape[axis]) for axis in range(len(shape))]
    values = values.at[tuple(index_at)].set(low)
    longest = shape.index(max(shape))
    index_at[longest] = (index_at[longest] + 1) % shape[longest]
    return values.at[tuple(index_at)].set(high)


def setup_inputs(seed: int = 0, part: int = 0) -> dict:
    key_list = jax.random.split(jax.random.key(seed), 5)
    part_keys = jax.random.split(jax.random.fold_in(key_list[4], part), 5)
    return {
        "velocity": draw_velocity(jax.random.fold_in(jax.random.fold_in(key_list[4], part), 71), part),
        "wet_bits": draw_wet_bits(jax.random.fold_in(jax.random.fold_in(key_list[4], part), 71), part),
        "east_face": draw_east_face(jax.random.fold_in(key_list[4], 71), part),
        "seam_turn": place_ends(jax.random.randint(key_list[3], (FACES,), 0, 4), jax.random.fold_in(key_list[3], 1), 0, 3).astype(jnp.int32),
    }


deriv_scale = 8.0


def unpack(wet_bits):
    repeated = jnp.repeat(wet_bits, 30, axis=0)
    shifts = lax.broadcasted_iota(jnp.int32, repeated.shape, 0) % 30
    return (jnp.right_shift(repeated, shifts) & 1).astype(jnp.float32)


def banded(n_in, n_out):
    offset = jnp.arange(n_in, dtype=jnp.int32)[:, None] - jnp.arange(n_out, dtype=jnp.int32)[None, :]
    spread = R * 1.0
    centred = (offset - R).astype(jnp.float32)
    taps = (jnp.arange(2 * R + 1, dtype=jnp.int32) - R).astype(jnp.float32)
    weight_sum = jnp.sum(jnp.exp(-0.5 * (taps / spread) ** 2))
    inside = (offset >= 0) & (offset <= 2 * R)
    return jnp.where(inside, jnp.exp(-0.5 * (centred / spread) ** 2) / weight_sum, jnp.float32(0.0)).astype(jnp.float32)


def rotate(strip, turn):
    cosine = jnp.where(turn == 0, 1.0, jnp.where(turn == 2, -1.0, 0.0)).astype(jnp.float32)
    sine_part = jnp.where(turn == 1, 1.0, jnp.where(turn == 3, -1.0, 0.0)).astype(jnp.float32)
    return jnp.stack([cosine * strip[0] - sine_part * strip[1], sine_part * strip[0] + cosine * strip[1]])


def derive(padded):
    centre = padded[:, 1:-1, ..., 1:-1]
    grad_x = deriv_scale * (padded[:, 1:-1, ..., 2:] - padded[:, 1:-1, ..., :-2])
    grad_y = deriv_scale * (padded[:, 2:, ..., 1:-1] - padded[:, :-2, ..., 1:-1])
    advect = centre[0] * grad_x + centre[1] * grad_y
    return jnp.concatenate([centre, grad_x, grad_y, advect], axis=0)


def combine(smooth):
    east_part = smooth[6] - (smooth[0] * smooth[2] + smooth[1] * smooth[4])
    north_part = smooth[7] - (smooth[0] * smooth[3] + smooth[1] * smooth[5])
    return jnp.stack([east_part, north_part])


def reference(velocity, wet_bits, east_face, seam_turn):
    wet = unpack(wet_bits)
    field = velocity * wet[None]
    face_width = N_SUB * CX
    grid = field.reshape(2, NY, FACES, face_width)
    order = jnp.arange(FACES, dtype=jnp.int32)
    west_face = jnp.zeros((FACES,), jnp.int32).at[east_face].set(order)
    west_turn = (4 - seam_turn[west_face]) % 4
    rim_width = R + 1
    from_west = rotate(grid[:, :, west_face, face_width - rim_width:], west_turn[:, None])
    from_east = rotate(grid[:, :, east_face, :rim_width], seam_turn[:, None])
    padded = jnp.concatenate([from_west, grid, from_east], axis=3)
    padded = jnp.pad(padded, ((0, 0), (1, 1), (0, 0), (0, 0)))
    channels = derive(padded)
    along = jnp.einsum("cyfx,xj->cyfj", channels, banded(face_width + 2 * R, face_width), precision=lax.Precision.HIGHEST)
    along = jnp.pad(along, ((0, 0), (R, R), (0, 0), (0, 0)))
    smooth = jnp.einsum("ki,ckfx->cifx", banded(NY + 2 * R, NY), along, precision=lax.Precision.HIGHEST)
    fine = combine(smooth) * wet.reshape(NY, FACES, face_width)[None]
    coarse = fine.reshape(2, NY // 4, 4, FACES, face_width // 4, 4).mean(axis=(2, 5))
    return coarse.reshape(2, NY // 4, NX // 4)
```

```python
import functools
import itertools

import jax
import jax.numpy as jnp
import numpy as np
from jax import lax
from jax.experimental import pallas as pl
from jax.experimental.pallas import tpu as pltpu
from jax.sharding import PartitionSpec as P

R = 32
RIM = R + 1
BITS = 30
COARSE = 4
LANES = 128
HALF = LANES // 2
SUBLANES = 8
SWITCHED_FACES = 4

deriv_scale = 8.0

f32 = jnp.float32
bf16 = jnp.bfloat16


def up_to(value, step):
    return -(-value // step) * step


def iota(shape, dim):
    return lax.broadcasted_iota(jnp.int32, shape, dim)


def split(value):
    high = value.astype(bf16)
    return high, (value - high.astype(f32)).astype(bf16)


def dot(left, right):
    return jnp.dot(left, right, preferred_element_type=f32)


def taps_sum():
    taps = np.arange(-R, R + 1, dtype=np.float64)
    return float(np.sum(np.exp(-0.5 * (taps / R) ** 2)))


def gaussian(distance, inside):
    inside = inside & (distance >= -R) & (distance <= R)
    scaled = distance.astype(f32) * (1.0 / R)
    return jnp.where(inside, jnp.exp(-0.5 * scaled * scaled) * (1.0 / taps_sum()), 0.0)


def roll(value, shift):
    return pltpu.roll(value, shift % LANES, axis=1)


def place(value, columns):
    return jnp.pad(value, ((0, 0), (0, columns - value.shape[1])))


def mask_kernel(geom, velocity, wet_bits, east_face, seam_turn, field, rows, wet, turn):
    n_rows, n_cols, depth, row_count, _ = geom
    at = iota((n_rows, n_cols), 0)
    word = jnp.zeros((n_rows, n_cols), jnp.int32)
    for j in range(n_rows // BITS):
        line = jnp.broadcast_to(wet_bits[j : j + 1, :], (n_rows, n_cols))
        word = jnp.where((at >= j * BITS) & (at < (j + 1) * BITS), line, word)
    bits = jnp.right_shift(word, at % BITS) & 1
    mask = bits.astype(f32)
    wet[:, :n_cols] = mask
    wet[:, n_cols:] = jnp.zeros((n_rows, LANES - n_cols), f32)
    row_at = lax.axis_index("row")
    for c in range(2):
        value = place(velocity[c] * mask, LANES)
        field[c] = value
        if row_count == 2:
            rows[c] = jnp.where(row_at == 0, value[n_rows - depth :], value[:depth])
        elif row_count > 2:
            rows[c, :depth] = value[:depth]
            rows[c, depth:] = value[n_rows - depth :]
    tile_at = lax.axis_index("tile")
    faces = east_face.shape[0]
    back = jnp.int32(0)
    for w in range(faces):
        back = jnp.where(east_face[w] == tile_at, seam_turn[w], back)
    ahead = seam_turn[tile_at]
    quarter = jnp.where(lax.axis_index("sub") == 0, (4 - back) % 4, ahead)
    cosine = jnp.where(quarter == 0, 1.0, jnp.where(quarter == 2, -1.0, 0.0)).astype(f32)
    sine = jnp.where(quarter == 1, 1.0, jnp.where(quarter == 3, -1.0, 0.0)).astype(f32)
    row = iota((SUBLANES, LANES), 0)
    lane = iota((SUBLANES, LANES), 1)
    turn[...] = jnp.where(row == 0, cosine, jnp.where(lane < HALF, -sine, sine))


def extend_kernel(geom, field, before, after, extended, outer, inner):
    n_rows, n_cols, depth, row_count, window = geom
    row_at = lax.axis_index("row")
    lane = iota((window, LANES), 1)
    whole = []
    for c in range(2):
        mine = field[c]
        if row_count == 2:
            other = before[c]
            value = jnp.where(
                row_at == 0,
                jnp.concatenate([mine, other], axis=0),
                jnp.concatenate([other, mine], axis=0),
            )
        elif row_count > 2:
            value = jnp.concatenate([before[c], mine, after[c]], axis=0)
        else:
            value = mine
        extended[c] = value
        whole.append(value)
    west = jnp.where(lane < HALF, whole[0], roll(whole[1], HALF))
    east = jnp.where(
        lane < HALF, roll(whole[0], RIM - n_cols), roll(whole[1], HALF + RIM - n_cols)
    )
    first = lax.axis_index("sub") == 0
    outer[...] = jnp.where(first, west, east)
    inner[...] = jnp.where(first, east, west)


def filter_kernel(geom, extended, seam, beside, wet, turn, forcing, columns, padded, along):
    n_rows, n_cols, depth, row_count, window = geom
    first = lax.axis_index("sub") == 0
    row_at = lax.axis_index("row")
    wide = 2 * LANES
    lane = iota((wide, LANES), 0)
    target = iota((wide, LANES), 1)
    rim = lane - LANES
    column = jnp.where(
        lane < LANES, lane, jnp.where(rim < HALF, rim - RIM, rim - HALF + n_cols)
    )
    inside = (
        (lane < n_cols)
        | ((rim >= 1) & (rim < RIM))
        | ((rim >= HALF) & (rim < HALF + R))
    )
    x_high, x_low = split(gaussian(column - target, inside & (target < n_cols)))
    x_both = jnp.concatenate([x_high, x_low], axis=1)
    out_rows = up_to(n_rows, 2 * SUBLANES)
    source = iota((out_rows, window), 1)
    target = iota((out_rows, window), 0)
    if row_count == 2:
        start = jnp.where(row_at == 0, 0, depth)
    elif row_count > 2:
        start = jnp.int32(depth)
    else:
        start = jnp.int32(0)
    world = source - start + row_at * n_rows
    inside = (world >= 0) & (world < row_count * n_rows) & (target < n_rows)
    y_high, y_low = split(gaussian(source - start - target, inside))
    y_both = jnp.concatenate([y_high, y_low], axis=0)

    lane = iota((window, LANES), 1)
    low = lane < HALF
    cosine = turn[0:1, :]
    sine = turn[1:2, :]
    got = seam[...]
    turned = cosine * got + sine * roll(got, HALF)
    near = beside[...]
    west = jnp.where(first, turned, near)
    east = jnp.where(first, near, turned)
    west_far = roll(west, HALF)
    east_far = roll(east, HALF)
    blank = jnp.zeros((SUBLANES, wide), f32)
    for c in range(2):
        own = extended[c]
        if c == 0:
            rims = jnp.where(low, west, east_far)
        else:
            rims = jnp.where(low, west_far, east)
        rims = jnp.where(lane == RIM, roll(own, RIM), rims)
        rims = jnp.where(lane == HALF - 1, roll(own, HALF - n_cols), rims)
        own = jnp.where(
            lane < n_cols,
            own,
            jnp.where(lane == n_cols, roll(rims, n_cols - HALF), roll(rims, LANES - RIM)),
        )
        padded[c, :SUBLANES, :] = blank
        padded[c, SUBLANES + window :, :] = blank
        padded[c, SUBLANES : SUBLANES + window, :LANES] = own
        padded[c, SUBLANES : SUBLANES + window, LANES:] = rims

    def store(c, part, value):
        high, low_part = split(value)
        columns[0, c, :, part * LANES : (part + 1) * LANES] = high
        columns[1, c, :, part * LANES : (part + 1) * LANES] = low_part

    for part in range(2):
        at = slice(part * LANES, (part + 1) * LANES)
        vel = [padded[c, SUBLANES : SUBLANES + window, at] for c in range(2)]
        grad_x = [roll(vel[c], -1) - roll(vel[c], 1) for c in range(2)]
        grad_y = [
            padded[c, SUBLANES + 1 : SUBLANES + 1 + window, at]
            - padded[c, SUBLANES - 1 : SUBLANES - 1 + window, at]
            for c in range(2)
        ]
        for c in range(2):
            store(c, part, vel[c])
            store(2 + c, part, grad_x[c])
            store(4 + c, part, grad_y[c])
            store(6 + c, part, vel[0] * grad_x[c] + vel[1] * grad_y[c])
    smooth = []
    for c in range(8):
        main = dot(columns[0, c], x_both)
        value = main[:, :LANES] + (main[:, LANES:] + dot(columns[1, c], x_high))
        high, low_part = split(value)
        pair, side = divmod(c, 2)
        along[0, pair, :, side * LANES : (side + 1) * LANES] = high
        along[1, pair, :, side * LANES : (side + 1) * LANES] = low_part
    for pair in range(4):
        main = dot(y_both, along[0, pair])
        value = main[:out_rows] + (main[out_rows:] + dot(y_high, along[1, pair]))
        smooth += [value[:n_rows, :LANES], value[:n_rows, LANES:]]
    mask = wet[...]
    fine = [
        mask * (smooth[6 + c] - (smooth[0] * smooth[2 + c] + smooth[1] * smooth[4 + c]))
        for c in range(2)
    ]
    both = jnp.concatenate(fine, axis=1)
    both = jnp.pad(both, ((0, out_rows - n_rows), (0, 0)))
    coarse = n_rows // COARSE
    coarse_rows = up_to(coarse, 2 * SUBLANES)
    block = iota((coarse_rows, out_rows), 1) // COARSE == iota((coarse_rows, out_rows), 0)
    gather_y = jnp.where(block, 1.0, 0.0).astype(bf16)
    high, low_part = split(both)
    pooled = dot(gather_y, high) + dot(gather_y, low_part)
    block = iota((LANES, LANES), 0) // COARSE == iota((LANES, LANES), 1)
    gather_x = jnp.where(block, deriv_scale / (COARSE * COARSE), 0.0).astype(bf16)
    for c in range(2):
        high, low_part = split(pooled[:, c * LANES : (c + 1) * LANES])
        value = dot(high, gather_x) + dot(low_part, gather_x)
        forcing[c] = value[:coarse, : n_cols // COARSE]


VMEM_SPEC = pl.BlockSpec(memory_space=pltpu.VMEM)
SMEM_SPEC = pl.BlockSpec(memory_space=pltpu.SMEM)


def seam_order(east_face):
    count = east_face.shape[0]
    one = iota((count, count), 0)
    two = iota((count, count), 1)
    weight = jnp.zeros((count, count), jnp.int32)
    for i in range(count):
        weight = jnp.where(one == i, int(np.prod(np.arange(1, count - i))), weight)
    smaller = (east_face[None, :] < east_face[:, None]) & (two > one)
    return jnp.sum(jnp.where(smaller, weight, 0))


def exchange(east_face, outer, inner):
    faces = east_face.shape[0]
    subs = lax.axis_size("sub")
    beside = [(i, subs - 1 - i) for i in range(subs)]

    def swap(order, outer, inner):
        pairs = []
        for west, east in enumerate(order):
            pairs += [(west * subs + subs - 1, east * subs), (east * subs, west * subs + subs - 1)]
        return (
            lax.ppermute(outer, ("tile", "sub"), pairs),
            lax.ppermute(inner, "sub", beside),
        )

    if faces <= SWITCHED_FACES:
        orders = itertools.permutations(range(faces))
        branches = [functools.partial(swap, order) for order in orders]
        return lax.switch(seam_order(east_face), branches, outer, inner)
    tile_at = lax.axis_index("tile")
    sub_at = lax.axis_index("sub")
    west = jnp.sum(jnp.where(east_face == tile_at, jnp.arange(faces, dtype=jnp.int32), 0))
    east = lax.dynamic_index_in_dim(east_face, tile_at, 0, keepdims=False)
    gathered = lax.all_gather(lax.ppermute(outer, "sub", beside), "tile")
    partner = jnp.where(sub_at == 0, west, east)
    seam = lax.dynamic_index_in_dim(gathered, partner, 0, keepdims=False)
    return seam, lax.ppermute(inner, "sub", beside)


def on_device(velocity, wet_bits, east_face, seam_turn):
    _, n_rows, n_cols = velocity.shape
    row_count = lax.axis_size("row")
    depth = up_to(RIM, SUBLANES)
    sides = min(row_count - 1, 2)
    window = n_rows + sides * depth
    geom = (n_rows, n_cols, depth, row_count, window)
    sent = depth * max(sides, 1)
    params = pltpu.CompilerParams(vmem_limit_bytes=16 << 20)
    shape = jax.ShapeDtypeStruct
    field, rows, wet, turn = pl.pallas_call(
        functools.partial(mask_kernel, geom),
        out_shape=(
            shape((2, n_rows, LANES), f32),
            shape((2, sent, LANES), f32),
            shape((n_rows, LANES), f32),
            shape((SUBLANES, LANES), f32),
        ),
        in_specs=[VMEM_SPEC, VMEM_SPEC, SMEM_SPEC, SMEM_SPEC],
        out_specs=(VMEM_SPEC,) * 4,
        compiler_params=params,
        name="mask",
    )(velocity, wet_bits, east_face, seam_turn)
    if row_count == 2:
        before = lax.ppermute(rows, "row", [(0, 1), (1, 0)])
        after = before
    elif row_count > 2:
        up = [(i, i + 1) for i in range(row_count - 1)]
        before = lax.ppermute(rows[:, depth:], "row", up)
        after = lax.ppermute(rows[:, :depth], "row", [(j, i) for i, j in up])
    else:
        before = after = rows
    extended, outer, inner = pl.pallas_call(
        functools.partial(extend_kernel, geom),
        out_shape=(
            shape((2, window, LANES), f32),
            shape((window, LANES), f32),
            shape((window, LANES), f32),
        ),
        in_specs=[VMEM_SPEC] * 3,
        out_specs=(VMEM_SPEC,) * 3,
        compiler_params=params,
        name="extend",
    )(field, before, after)
    seam, beside = exchange(east_face, outer, inner)
    wide = 2 * LANES
    return pl.pallas_call(
        functools.partial(filter_kernel, geom),
        out_shape=shape((2, n_rows // COARSE, n_cols // COARSE), f32),
        in_specs=[VMEM_SPEC] * 5,
        out_specs=VMEM_SPEC,
        scratch_shapes=[
            pltpu.VMEM((2, 8, window, wide), bf16),
            pltpu.VMEM((2, window + 2 * SUBLANES, wide), f32),
            pltpu.VMEM((2, 4, window, wide), bf16),
        ],
        compiler_params=params,
        name="filter",
    )(extended, seam, beside, wet, turn)


def solution(mesh):
    placed = (
        P(None, ("grp", "row"), ("tile", "sub")),
        P(("grp", "row"), ("tile", "sub")),
        P(),
        P(),
    )
    return jax.shard_map(
        on_device,
        mesh=mesh,
        in_specs=placed,
        out_specs=P(None, ("grp", "row"), ("tile", "sub")),
        check_vma=False,
    )
```

```python
import functools
import itertools

import jax
import jax.numpy as jnp
import numpy as np
from jax import lax
from jax.experimental import pallas as pl
from jax.experimental.pallas import tpu as pltpu
from jax.sharding import PartitionSpec as P

R = 32
RIM = R + 1
BITS = 30
COARSE = 4
LANES = 128
HALF = LANES // 2
SUBLANES = 8
SWITCHED_FACES = 4

deriv_scale = 8.0

f32 = jnp.float32
bf16 = jnp.bfloat16


def up_to(value, step):
    return -(-value // step) * step


def iota(shape, dim):
    return lax.broadcasted_iota(jnp.int32, shape, dim)


def split(value):
    high = value.astype(bf16)
    return high, (value - high.astype(f32)).astype(bf16)


def dot(left, right):
    return jnp.dot(left, right, preferred_element_type=f32)


def taps_sum():
    taps = np.arange(-R, R + 1, dtype=np.float64)
    return float(np.sum(np.exp(-0.5 * (taps / R) ** 2)))


def gaussian(distance, inside):
    inside = inside & (distance >= -R) & (distance <= R)
    scaled = distance.astype(f32) * (1.0 / R)
    return jnp.where(inside, jnp.exp(-0.5 * scaled * scaled) * (1.0 / taps_sum()), 0.0)


def roll(value, shift):
    return pltpu.roll(value, shift % LANES, axis=1)


def fetch(pairs, sems):
    copies = [pltpu.make_async_copy(a, b, sems.at[i]) for i, (a, b) in enumerate(pairs)]
    for copy in copies:
        copy.start()
    for copy in copies:
        copy.wait()


def mask_kernel(geom, velocity, wet_bits, field, rows, wet, vel, packed, sems):
    n_rows, n_cols, depth, row_count, _ = geom
    fetch(((velocity, vel), (wet_bits, packed)), sems)
    at = iota((n_rows, n_cols), 0)
    word = jnp.broadcast_to(packed[0:1, :], (n_rows, n_cols))
    shift = at
    for j in range(1, n_rows // BITS):
        line = jnp.broadcast_to(packed[j : j + 1, :], (n_rows, n_cols))
        later = at >= j * BITS
        word = jnp.where(later, line, word)
        shift = jnp.where(later, at - j * BITS, shift)
    mask = (jnp.right_shift(word, shift) & 1).astype(f32)
    margin = jnp.zeros((n_rows, LANES - n_cols), f32)
    wet[:, :n_cols] = mask
    wet[:, n_cols:] = margin
    row_at = lax.axis_index("row")
    for c in range(2):
        value = jnp.concatenate([vel[c] * mask, margin], axis=1)
        field[c] = value
        if row_count == 2:
            rows[c] = jnp.where(row_at == 0, value[n_rows - depth :], value[:depth])
        elif row_count > 2:
            rows[c, :depth] = value[:depth]
            rows[c, depth:] = value[n_rows - depth :]


def seam_order(faces):
    count = faces.shape[0]
    order = jnp.int32(0)
    for i in range(count):
        smaller = jnp.int32(0)
        for j in range(i + 1, count):
            smaller = smaller + jnp.where(faces[j] < faces[i], 1, 0)
        order = order * (count - i) + smaller
    return order


def prepare_kernel(
    geom, east_face, seam_turn, order, turn, x_taps, y_taps, faces, turns, sems
):
    n_rows, n_cols, depth, row_count, window = geom
    copies = [
        pltpu.make_async_copy(east_face, faces, sems.at[0]),
        pltpu.make_async_copy(seam_turn, turns, sems.at[1]),
    ]
    for copy in copies:
        copy.start()
    row_at = lax.axis_index("row")
    lane = iota((2 * LANES, LANES), 0)
    target = iota((2 * LANES, LANES), 1)
    rim = lane - LANES
    column = jnp.where(
        lane < LANES, lane, jnp.where(rim < HALF, rim - RIM, rim - HALF + n_cols)
    )
    inside = (
        (lane < n_cols)
        | ((rim >= 0) & (rim < RIM))
        | ((rim >= HALF) & (rim < HALF + RIM))
    )
    inside = inside & (target < n_cols)
    away = column - target
    value = split(gaussian(away, inside))
    slope = split(gaussian(away - 1, inside) - gaussian(away + 1, inside))
    for i, taps in enumerate((slope[1], value[1], value[0], slope[0])):
        x_taps[:, i * LANES : (i + 1) * LANES] = taps
    out_rows = up_to(n_rows, 2 * SUBLANES)
    source = iota((out_rows, window), 1)
    target = iota((out_rows, window), 0)
    start = row_start(geom, row_at)
    world = source - start + row_at * n_rows
    last = row_count * n_rows

    def taps_at(step):
        at = world + step
        inside = (at >= 0) & (at < last) & (target < n_rows)
        return gaussian(source + step - start - target, inside)

    value = split(taps_at(0))
    slope = split(taps_at(-1) - taps_at(1))
    for i, taps in enumerate((slope[1], slope[0], value[0], value[1])):
        y_taps[i * out_rows : (i + 1) * out_rows, :] = taps
    for copy in copies:
        copy.wait()
    order[0] = seam_order(faces) if faces.shape[0] <= SWITCHED_FACES else jnp.int32(0)
    tile_at = lax.axis_index("tile")
    back = jnp.int32(0)
    for w in range(faces.shape[0]):
        back = jnp.where(faces[w] == tile_at, turns[w], back)
    quarter = jnp.where(lax.axis_index("sub") == 0, (4 - back) % 4, turns[tile_at])
    cosine = jnp.where(quarter == 0, 1.0, jnp.where(quarter == 2, -1.0, 0.0)).astype(f32)
    sine = jnp.where(quarter == 1, 1.0, jnp.where(quarter == 3, -1.0, 0.0)).astype(f32)
    row = iota((SUBLANES, LANES), 0)
    lane = iota((SUBLANES, LANES), 1)
    turn[...] = jnp.where(row == 0, cosine, jnp.where(lane < HALF, -sine, sine))


def row_start(geom, row_at):
    _, _, depth, row_count, _ = geom
    if row_count == 2:
        return jnp.where(row_at == 0, 0, depth)
    return jnp.int32(depth if row_count > 2 else 0)


def extend_kernel(geom, field, before, after, extended, outer, inner):
    n_rows, n_cols, depth, row_count, window = geom
    row_at = lax.axis_index("row")
    lane = iota((window, LANES), 1)
    whole = []
    for c in range(2):
        mine = field[c]
        if row_count == 2:
            other = before[c]
            value = jnp.where(
                row_at == 0,
                jnp.concatenate([mine, other], axis=0),
                jnp.concatenate([other, mine], axis=0),
            )
        elif row_count > 2:
            value = jnp.concatenate([before[c], mine, after[c]], axis=0)
        else:
            value = mine
        extended[c] = value
        whole.append(value)
    west = jnp.where(lane < HALF, whole[0], roll(whole[1], HALF))
    east = jnp.where(
        lane < HALF, roll(whole[0], RIM - n_cols), roll(whole[1], HALF + RIM - n_cols)
    )
    first = lax.axis_index("sub") == 0
    outer[...] = jnp.where(first, west, east)
    inner[...] = jnp.where(first, east, west)


def filter_kernel(
    geom, extended, seam, beside, wet, turn, x_taps, y_taps, forcing, columns, padded, along
):
    n_rows, n_cols, depth, row_count, window = geom
    first = lax.axis_index("sub") == 0
    wide = 2 * LANES
    out_rows = up_to(n_rows, 2 * SUBLANES)
    lane = iota((window, LANES), 1)
    low = lane < HALF
    cosine = turn[0:1, :]
    sine = turn[1:2, :]
    got = seam[...]
    turned = cosine * got + sine * roll(got, HALF)
    near = beside[...]
    west = jnp.where(first, turned, near)
    east = jnp.where(first, near, turned)
    west_far = roll(west, HALF)
    east_far = roll(east, HALF)
    blank = jnp.zeros((SUBLANES, wide), f32)
    for c in range(2):
        own = extended[c]
        if c == 0:
            rims = jnp.where(low, west, east_far)
        else:
            rims = jnp.where(low, west_far, east)
        rims = jnp.where(lane == RIM, roll(own, RIM), rims)
        rims = jnp.where(lane == HALF - 1, roll(own, HALF - n_cols), rims)
        own = jnp.where(
            lane < n_cols,
            own,
            jnp.where(lane == n_cols, roll(rims, n_cols - HALF), roll(rims, LANES - RIM)),
        )
        padded[c, :SUBLANES, :] = blank
        padded[c, SUBLANES + window :, :] = blank
        padded[c, SUBLANES : SUBLANES + window, :LANES] = own
        padded[c, SUBLANES : SUBLANES + window, LANES:] = rims

    def store(c, part, value):
        high, low_part = split(value)
        columns[0, c, :, part * LANES : (part + 1) * LANES] = high
        columns[1, c, :, part * LANES : (part + 1) * LANES] = low_part

    for part in range(2):
        at = slice(part * LANES, (part + 1) * LANES)
        vel = [padded[c, SUBLANES : SUBLANES + window, at] for c in range(2)]
        for c in range(2):
            grad_x = roll(vel[c], -1) - roll(vel[c], 1)
            grad_y = (
                padded[c, SUBLANES + 1 : SUBLANES + 1 + window, at]
                - padded[c, SUBLANES - 1 : SUBLANES - 1 + window, at]
            )
            store(c, part, vel[c])
            store(2 + c, part, vel[0] * grad_x + vel[1] * grad_y)

    def keep(pair, side, value):
        high, low_part = split(value)
        along[0, pair, :, side * LANES : (side + 1) * LANES] = high
        along[1, pair, :, side * LANES : (side + 1) * LANES] = low_part

    x_high = x_taps[:, wide:]
    x_low = x_taps[:, :wide]
    x_both = x_taps[:, LANES : LANES + wide]
    for c in range(2):
        main = dot(columns[0, c], x_high)
        more = dot(columns[1, c], x_high)
        rest = dot(columns[0, c], x_low)
        keep(0, c, main[:, :LANES] + (more[:, :LANES] + rest[:, LANES:]))
        keep(1, c, main[:, LANES:] + (more[:, LANES:] + rest[:, :LANES]))
    for c in range(2):
        main = dot(columns[0, 2 + c], x_both)
        more = dot(columns[1, 2 + c], x_both[:, LANES:])
        keep(2, c, main[:, LANES:] + (more + main[:, :LANES]))

    main = dot(y_taps[...], along[0, 0])
    more = dot(y_taps[out_rows : 3 * out_rows, :], along[1, 0])
    slope_y = main[out_rows : 2 * out_rows] + (main[:out_rows] + more[:out_rows])
    mean = main[2 * out_rows : 3 * out_rows] + (main[3 * out_rows :] + more[out_rows:])

    def across(pair):
        main = dot(y_taps[2 * out_rows :, :], along[0, pair])
        more = dot(y_taps[2 * out_rows : 3 * out_rows, :], along[1, pair])
        return main[:out_rows] + (main[out_rows:] + more)

    slope_x = across(1)
    flux = across(2)
    mean_u = mean[:, :LANES]
    mean_v = mean[:, LANES:]
    mask = jnp.pad(wet[...], ((0, out_rows - n_rows), (0, 0)))
    coarse = n_rows // COARSE
    coarse_rows = up_to(2 * coarse, 2 * SUBLANES)
    block = iota((coarse_rows, out_rows), 1) // COARSE * 2
    pooled = jnp.zeros((coarse_rows, LANES), f32)
    for c in range(2):
        at = slice(c * LANES, (c + 1) * LANES)
        fine = mask * (flux[:, at] - (mean_u * slope_x[:, at] + mean_v * slope_y[:, at]))
        gather = jnp.where(block + c == iota((coarse_rows, out_rows), 0), 1.0, 0.0).astype(bf16)
        high, low_part = split(fine)
        pooled = pooled + (dot(gather, high) + dot(gather, low_part))
    block = iota((LANES, LANES), 0) // COARSE == iota((LANES, LANES), 1)
    gather = jnp.where(block, deriv_scale / (COARSE * COARSE), 0.0).astype(bf16)
    high, low_part = split(pooled)
    value = dot(high, gather) + dot(low_part, gather)
    forcing[...] = value[: 2 * coarse, : n_cols // COARSE]


VMEM_SPEC = pl.BlockSpec(memory_space=pltpu.VMEM)
SMEM_SPEC = pl.BlockSpec(memory_space=pltpu.SMEM)
HBM_SPEC = pl.BlockSpec(memory_space=pltpu.HBM)


def exchange(order, east_face, outer, inner, finish):
    faces = east_face.shape[0]
    subs = lax.axis_size("sub")
    beside = [(i, subs - 1 - i) for i in range(subs)]

    def swap(order, outer, inner):
        pairs = []
        for west, east in enumerate(order):
            pairs += [(west * subs + subs - 1, east * subs), (east * subs, west * subs + subs - 1)]
        seam = lax.ppermute(outer, ("tile", "sub"), pairs)
        return finish(seam, lax.ppermute(inner, "sub", beside))

    if faces <= SWITCHED_FACES:
        orders = itertools.permutations(range(faces))
        branches = [functools.partial(swap, order) for order in orders]
        return lax.switch(order[0], branches, outer, inner)
    tile_at = lax.axis_index("tile")
    sub_at = lax.axis_index("sub")
    west = jnp.sum(jnp.where(east_face == tile_at, jnp.arange(faces, dtype=jnp.int32), 0))
    east = lax.dynamic_index_in_dim(east_face, tile_at, 0, keepdims=False)
    gathered = lax.all_gather(lax.ppermute(outer, "sub", beside), "tile")
    partner = jnp.where(sub_at == 0, west, east)
    seam = lax.dynamic_index_in_dim(gathered, partner, 0, keepdims=False)
    return finish(seam, lax.ppermute(inner, "sub", beside))


def on_device(velocity, wet_bits, east_face, seam_turn):
    _, n_rows, n_cols = velocity.shape
    row_count = lax.axis_size("row")
    depth = up_to(RIM, SUBLANES)
    sides = min(row_count - 1, 2)
    window = n_rows + sides * depth
    geom = (n_rows, n_cols, depth, row_count, window)
    sent = depth * max(sides, 1)
    wide = 2 * LANES
    out_rows = up_to(n_rows, 2 * SUBLANES)
    params = pltpu.CompilerParams(vmem_limit_bytes=16 << 20)
    shape = jax.ShapeDtypeStruct
    field, rows, wet = pl.pallas_call(
        functools.partial(mask_kernel, geom),
        out_shape=(
            shape((2, n_rows, LANES), f32),
            shape((2, sent, LANES), f32),
            shape((n_rows, LANES), f32),
        ),
        in_specs=[HBM_SPEC] * 2,
        out_specs=(VMEM_SPEC,) * 3,
        scratch_shapes=[
            pltpu.VMEM(velocity.shape, f32),
            pltpu.VMEM(wet_bits.shape, jnp.int32),
            pltpu.SemaphoreType.DMA((2,)),
        ],
        compiler_params=params,
        name="mask",
    )(
        pltpu.with_memory_space_constraint(velocity, pltpu.HBM),
        pltpu.with_memory_space_constraint(wet_bits, pltpu.HBM),
    )
    order, turn, x_taps, y_taps = pl.pallas_call(
        functools.partial(prepare_kernel, geom),
        out_shape=(
            shape((1,), jnp.int32),
            shape((SUBLANES, LANES), f32),
            shape((wide, 2 * wide), bf16),
            shape((4 * out_rows, window), bf16),
        ),
        in_specs=[HBM_SPEC] * 2,
        out_specs=(SMEM_SPEC,) + (VMEM_SPEC,) * 3,
        scratch_shapes=[
            pltpu.SMEM(east_face.shape, jnp.int32),
            pltpu.SMEM(seam_turn.shape, jnp.int32),
            pltpu.SemaphoreType.DMA((2,)),
        ],
        compiler_params=params,
        name="prepare",
    )(
        pltpu.with_memory_space_constraint(east_face, pltpu.HBM),
        pltpu.with_memory_space_constraint(seam_turn, pltpu.HBM),
    )
    if row_count == 2:
        before = lax.ppermute(rows, "row", [(0, 1), (1, 0)])
        after = before
    elif row_count > 2:
        up = [(i, i + 1) for i in range(row_count - 1)]
        before = lax.ppermute(rows[:, depth:], "row", up)
        after = lax.ppermute(rows[:, :depth], "row", [(j, i) for i, j in up])
    else:
        before = after = rows
    extended, outer, inner = pl.pallas_call(
        functools.partial(extend_kernel, geom),
        out_shape=(
            shape((2, window, LANES), f32),
            shape((window, LANES), f32),
            shape((window, LANES), f32),
        ),
        in_specs=[VMEM_SPEC] * 3,
        out_specs=(VMEM_SPEC,) * 3,
        compiler_params=params,
        name="extend",
    )(field, before, after)

    def finish(seam, beside):
        return pl.pallas_call(
            functools.partial(filter_kernel, geom),
            out_shape=shape((2 * (n_rows // COARSE), n_cols // COARSE), f32),
            in_specs=[VMEM_SPEC] * 7,
            out_specs=VMEM_SPEC,
            scratch_shapes=[
                pltpu.VMEM((2, 4, window, wide), bf16),
                pltpu.VMEM((2, window + 2 * SUBLANES, wide), f32),
                pltpu.VMEM((2, 3, window, wide), bf16),
            ],
            compiler_params=params,
            name="filter",
        )(extended, seam, beside, wet, turn, x_taps, y_taps)

    forcing = exchange(order, east_face, outer, inner, finish)
    return jnp.transpose(
        forcing.reshape(n_rows // COARSE, 2, n_cols // COARSE), (1, 0, 2)
    )


def solution(mesh):
    placed = (
        P(None, ("grp", "row"), ("tile", "sub")),
        P(("grp", "row"), ("tile", "sub")),
        P(),
        P(),
    )
    return jax.shard_map(
        on_device,
        mesh=mesh,
        in_specs=placed,
        out_specs=P(None, ("grp", "row"), ("tile", "sub")),
        check_vma=False,
    )
```

```python
import functools
import itertools

import jax
import jax.numpy as jnp
import numpy as np
from jax import lax
from jax.experimental import pallas as pl
from jax.experimental.pallas import tpu as pltpu
from jax.sharding import PartitionSpec as P

R = 32
RIM = R + 1
BITS = 30
COARSE = 4
LANES = 128
HALF = LANES // 2
GROUPS = 3
GROUP = 40
SUBLANES = 8
SWITCHED_FACES = 4

deriv_scale = 8.0

f32 = jnp.float32
bf16 = jnp.bfloat16


def up_to(value, step):
    return -(-value // step) * step


def iota(shape, dim):
    return lax.broadcasted_iota(jnp.int32, shape, dim)


def split(value):
    high = value.astype(bf16)
    return high, (value - high.astype(f32)).astype(bf16)


def dot(left, right):
    return jnp.dot(left, right, preferred_element_type=f32)


def taps_sum():
    taps = np.arange(-R, R + 1, dtype=np.float64)
    return float(np.sum(np.exp(-0.5 * (taps / R) ** 2)))


def gaussian(distance, inside):
    inside = inside & (distance >= -R) & (distance <= R)
    scaled = distance.astype(f32) * (1.0 / R)
    return jnp.where(inside, jnp.exp(-0.5 * scaled * scaled) * (1.0 / taps_sum()), 0.0)


def roll(value, shift):
    return pltpu.roll(value, shift % LANES, axis=1)


def fetch(pairs, sems):
    copies = [pltpu.make_async_copy(a, b, sems.at[i]) for i, (a, b) in enumerate(pairs)]
    for copy in copies:
        copy.start()
    for copy in copies:
        copy.wait()


def mask_kernel(geom, velocity, wet_bits, field, rows, wet, vel, packed, sems):
    n_rows, n_cols, depth, row_count, _ = geom
    fetch(((velocity, vel), (wet_bits, packed)), sems)
    at = iota((n_rows, n_cols), 0)
    word = jnp.broadcast_to(packed[0:1, :], (n_rows, n_cols))
    shift = at
    for j in range(1, n_rows // BITS):
        line = jnp.broadcast_to(packed[j : j + 1, :], (n_rows, n_cols))
        later = at >= j * BITS
        word = jnp.where(later, line, word)
        shift = jnp.where(later, at - j * BITS, shift)
    mask = (jnp.right_shift(word, shift) & 1).astype(f32)
    margin = jnp.zeros((n_rows, LANES - n_cols), f32)
    wet[:, :n_cols] = mask
    wet[:, n_cols:] = margin
    row_at = lax.axis_index("row")
    for c in range(2):
        value = jnp.concatenate([vel[c] * mask, margin], axis=1)
        field[c] = value
        if row_count == 2:
            rows[c] = jnp.where(row_at == 0, value[n_rows - depth :], value[:depth])
        elif row_count > 2:
            rows[c, :depth] = value[:depth]
            rows[c, depth:] = value[n_rows - depth :]


def seam_order(faces):
    count = faces.shape[0]
    order = jnp.int32(0)
    for i in range(count):
        smaller = jnp.int32(0)
        for j in range(i + 1, count):
            smaller = smaller + jnp.where(faces[j] < faces[i], 1, 0)
        order = order * (count - i) + smaller
    return order


def prepare_kernel(
    geom, east_face, seam_turn, order, turn, x_taps, y_taps, faces, turns, sems
):
    n_rows, n_cols, depth, row_count, window = geom
    copies = [
        pltpu.make_async_copy(east_face, faces, sems.at[0]),
        pltpu.make_async_copy(seam_turn, turns, sems.at[1]),
    ]
    for copy in copies:
        copy.start()
    row_at = lax.axis_index("row")
    lane = iota((2 * LANES, LANES), 0)
    target = iota((2 * LANES, LANES), 1)
    rim = lane - LANES
    column = jnp.where(
        lane < LANES, lane, jnp.where(rim < HALF - 1, rim - RIM, rim - HALF + n_cols)
    )
    inside = (
        ((lane >= 1) & (lane < n_cols - 1))
        | ((rim >= 0) & (rim <= RIM))
        | ((rim >= HALF - 1) & (rim < HALF + RIM))
    )
    inside = inside & (target < n_cols)
    away = column - target
    value = split(gaussian(away, inside))
    slope = split(gaussian(away - 1, inside) - gaussian(away + 1, inside))
    for i, taps in enumerate((slope[1], value[1], value[0], slope[0])):
        x_taps[:, i * LANES : (i + 1) * LANES] = taps
    out_rows = up_to(n_rows, 2 * SUBLANES)
    source = iota((out_rows, window), 1)
    target = iota((out_rows, window), 0)
    start = row_start(geom, row_at)
    world = source - start + row_at * n_rows
    last = row_count * n_rows

    def taps_at(step):
        at = world + step
        inside = (at >= 0) & (at < last) & (target < n_rows)
        return gaussian(source + step - start - target, inside)

    value = split(taps_at(0))
    slope = split(taps_at(-1) - taps_at(1))
    for i, taps in enumerate((slope[1], slope[0], value[0], value[1])):
        y_taps[i * out_rows : (i + 1) * out_rows, :] = taps
    for copy in copies:
        copy.wait()
    order[0] = seam_order(faces) if faces.shape[0] <= SWITCHED_FACES else jnp.int32(0)
    tile_at = lax.axis_index("tile")
    back = jnp.int32(0)
    for w in range(faces.shape[0]):
        back = jnp.where(faces[w] == tile_at, turns[w], back)
    sub_at = lax.axis_index("sub")
    quarter = jnp.where(sub_at == 0, (4 - back) % 4, turns[tile_at])
    cosine = jnp.where(quarter == 0, 1.0, jnp.where(quarter == 2, -1.0, 0.0)).astype(f32)
    sine = jnp.where(quarter == 1, 1.0, jnp.where(quarter == 3, -1.0, 0.0)).astype(f32)
    row = iota((SUBLANES, LANES), 0)
    lane = iota((SUBLANES, LANES), 1)
    seam_lane = seam_side(lane, sub_at)
    turn[...] = jnp.where(
        row == 0, jnp.where(seam_lane, cosine, 1.0), jnp.where(seam_lane, sine, 0.0)
    )


def seam_side(lane, sub_at):
    edge = jnp.where(sub_at == 0, RIM, LANES)
    start = jnp.where(sub_at == 0, 0, HALF)
    return (lane >= start) & (lane < edge)


def packed_rows(window):
    return up_to(-(-2 * window // GROUPS), SUBLANES)


def pieces(window):
    size = packed_rows(window)
    cuts = sorted({0, window, 2 * window, *(size * g for g in range(1, GROUPS))})
    return [
        (a // window, a % window, a // size, a % size, b - a) for a, b in zip(cuts, cuts[1:])
    ]


def row_start(geom, row_at):
    _, _, depth, row_count, _ = geom
    if row_count == 2:
        return jnp.where(row_at == 0, 0, depth)
    return jnp.int32(depth if row_count > 2 else 0)


def extend_kernel(geom, field, before, after, extended, outer, inner):
    n_rows, n_cols, depth, row_count, window = geom
    row_at = lax.axis_index("row")
    whole = []
    for c in range(2):
        mine = field[c]
        if row_count == 2:
            other = before[c]
            value = jnp.where(
                row_at == 0,
                jnp.concatenate([mine, other], axis=0),
                jnp.concatenate([other, mine], axis=0),
            )
        elif row_count > 2:
            value = jnp.concatenate([before[c], mine, after[c]], axis=0)
        else:
            value = mine
        extended[c] = value
        whole.append(value)
    first = lax.axis_index("sub") == 0
    size = packed_rows(window)
    lane = iota((size, LANES), 1)
    groups = [[] for _ in range(GROUPS)]
    for c, row, group, _, count in pieces(window):
        groups[group].append(whole[c][row : row + count])
    spare = GROUPS * size - 2 * window
    if spare:
        groups[-1].append(jnp.zeros((spare, LANES), f32))
    groups = [jnp.concatenate(group, axis=0) for group in groups]
    for to, base in ((outer, jnp.where(first, 0, RIM - n_cols)), (inner, jnp.where(first, RIM - n_cols, 0))):
        value = roll(groups[-1], base + (GROUPS - 1) * GROUP)
        for g in reversed(range(GROUPS - 1)):
            value = jnp.where(lane < (g + 1) * GROUP, roll(groups[g], base + g * GROUP), value)
        to[...] = value


def pad_rows(padded, c, window, value):
    blank = jnp.zeros((SUBLANES, LANES), f32)
    padded[c, :SUBLANES, :] = blank
    padded[c, SUBLANES + window :, :] = blank
    padded[c, SUBLANES : SUBLANES + window, :] = value


def channels(padded, columns, window):
    vel = [padded[c, SUBLANES : SUBLANES + window, :] for c in range(2)]
    for c in range(2):
        grad_x = roll(vel[c], -1) - roll(vel[c], 1)
        grad_y = (
            padded[c, SUBLANES + 1 : SUBLANES + 1 + window, :]
            - padded[c, SUBLANES - 1 : SUBLANES - 1 + window, :]
        )
        advect = vel[0] * grad_x + vel[1] * grad_y
        for at, value in ((c, vel[c]), (2 + c, advect)):
            high, low_part = split(value)
            columns[0, at * window : (at + 1) * window, :] = high
            columns[1, at * window : (at + 1) * window, :] = low_part


def across_x(columns, x_taps, window):
    wide = 2 * LANES
    high = x_taps[:, wide:]
    low_part = x_taps[:, :wide]
    both = x_taps[:, LANES : LANES + wide]
    main = dot(columns[0, : 2 * window, :], high)
    more = dot(columns[1, : 2 * window, :], high)
    rest = dot(columns[0, : 2 * window, :], low_part)
    flux = dot(columns[0, 2 * window :, :], both)
    flux_more = dot(columns[1, 2 * window :, :], both[:, LANES:])
    means = main[:, :LANES] + (more[:, :LANES] + rest[:, LANES:])
    slopes = main[:, LANES:] + (more[:, LANES:] + rest[:, :LANES])
    fluxes = flux[:, LANES:] + (flux_more + flux[:, :LANES])
    return means, slopes, fluxes


def inner_kernel(geom, extended, x_taps, partial, edges, padded, columns):
    n_rows, n_cols, depth, row_count, window = geom
    lane = iota((window, LANES), 1)
    for c in range(2):
        own = extended[c]
        pad_rows(padded, c, window, own)
        near = jnp.where(lane < RIM + 2, roll(own, RIM), roll(own, HALF - n_cols))
        edges[c] = near
    channels(padded, columns, window)
    for pair, value in enumerate(across_x(columns, x_taps[:LANES, :], window)):
        partial[pair] = value


def filter_kernel(
    geom,
    seam,
    beside,
    edges,
    partial,
    wet,
    turn,
    x_taps,
    y_taps,
    forcing,
    padded,
    columns,
    along,
    pools,
):
    n_rows, n_cols, depth, row_count, window = geom
    sub_at = lax.axis_index("sub")
    out_rows = up_to(n_rows, 2 * SUBLANES)
    near = jnp.where(sub_at == 0, 0, HALF)
    parts = [[], []]
    for c, _, group, row, count in pieces(window):
        lane = iota((count, LANES), 1)
        parts[c].append(
            jnp.where(
                seam_side(lane, sub_at),
                roll(seam[row : row + count, :], near - group * GROUP),
                roll(beside[row : row + count, :], HALF - near - group * GROUP),
            )
        )
    east, north = (jnp.concatenate(part, axis=0) for part in parts)
    cosine = turn[0:1, :]
    sine = turn[1:2, :]
    turned = (cosine * east - sine * north, sine * east + cosine * north)
    lane = iota((window, LANES), 1)
    own = (lane >= RIM) & (lane < HALF)
    for c in range(2):
        pad_rows(padded, c, window, jnp.where(own, edges[c], turned[c]))
    channels(padded, columns, window)
    for pair, value in enumerate(across_x(columns, x_taps[LANES:, :], window)):
        value = value + partial[pair]
        high, low_part = split(value)
        for c in range(2):
            at = slice(c * LANES, (c + 1) * LANES)
            along[0, pair, :, at] = high[c * window : (c + 1) * window]
            along[1, pair, :, at] = low_part[c * window : (c + 1) * window]

    main = dot(y_taps[...], along[0, 0])
    more = dot(y_taps[out_rows : 3 * out_rows, :], along[1, 0])
    slope_y = main[out_rows : 2 * out_rows] + (main[:out_rows] + more[:out_rows])
    mean = main[2 * out_rows : 3 * out_rows] + (main[3 * out_rows :] + more[out_rows:])

    def across(pair):
        main = dot(y_taps[2 * out_rows :, :], along[0, pair])
        more = dot(y_taps[2 * out_rows : 3 * out_rows, :], along[1, pair])
        return main[:out_rows] + (main[out_rows:] + more)

    slope_x = across(1)
    flux = across(2)
    mean_u = mean[:n_rows, :LANES]
    mean_v = mean[:n_rows, LANES:]
    mask = wet[...]
    coarse = n_rows // COARSE
    for c in range(2):
        at = slice(c * LANES, (c + 1) * LANES)
        pools[c] = mask * (
            flux[:n_rows, at] - (mean_u * slope_x[:n_rows, at] + mean_v * slope_y[:n_rows, at])
        )
    block = iota((LANES, LANES), 0) // COARSE == iota((LANES, LANES), 1)
    gather = jnp.where(block, deriv_scale / (COARSE * COARSE), 0.0).astype(bf16)
    for c in range(2):
        rows = [pools[c, pl.ds(k, coarse, stride=COARSE), :] for k in range(COARSE)]
        high, low_part = split((rows[0] + rows[1]) + (rows[2] + rows[3]))
        value = dot(high, gather) + dot(low_part, gather)
        forcing[:, c, :] = value[:, : n_cols // COARSE]


VMEM_SPEC = pl.BlockSpec(memory_space=pltpu.VMEM)
SMEM_SPEC = pl.BlockSpec(memory_space=pltpu.SMEM)
HBM_SPEC = pl.BlockSpec(memory_space=pltpu.HBM)


def exchange(order, east_face, outer, inner, finish):
    faces = east_face.shape[0]
    subs = lax.axis_size("sub")
    beside = [(i, subs - 1 - i) for i in range(subs)]

    def swap(order, outer, inner):
        pairs = []
        for west, east in enumerate(order):
            pairs += [(west * subs + subs - 1, east * subs), (east * subs, west * subs + subs - 1)]
        seam = lax.ppermute(outer, ("tile", "sub"), pairs)
        return finish(seam, lax.ppermute(inner, "sub", beside))

    if faces <= SWITCHED_FACES:
        orders = itertools.permutations(range(faces))
        branches = [functools.partial(swap, order) for order in orders]
        return lax.switch(order[0], branches, outer, inner)
    tile_at = lax.axis_index("tile")
    sub_at = lax.axis_index("sub")
    west = jnp.sum(jnp.where(east_face == tile_at, jnp.arange(faces, dtype=jnp.int32), 0))
    east = lax.dynamic_index_in_dim(east_face, tile_at, 0, keepdims=False)
    gathered = lax.all_gather(lax.ppermute(outer, "sub", beside), "tile")
    partner = jnp.where(sub_at == 0, west, east)
    seam = lax.dynamic_index_in_dim(gathered, partner, 0, keepdims=False)
    return finish(seam, lax.ppermute(inner, "sub", beside))


def on_device(velocity, wet_bits, east_face, seam_turn):
    _, n_rows, n_cols = velocity.shape
    row_count = lax.axis_size("row")
    depth = up_to(RIM, SUBLANES)
    sides = min(row_count - 1, 2)
    window = n_rows + sides * depth
    geom = (n_rows, n_cols, depth, row_count, window)
    sent = depth * max(sides, 1)
    wide = 2 * LANES
    out_rows = up_to(n_rows, 2 * SUBLANES)
    params = pltpu.CompilerParams(vmem_limit_bytes=16 << 20)
    shape = jax.ShapeDtypeStruct
    field, rows, wet = pl.pallas_call(
        functools.partial(mask_kernel, geom),
        out_shape=(
            shape((2, n_rows, LANES), f32),
            shape((2, sent, LANES), f32),
            shape((n_rows, LANES), f32),
        ),
        in_specs=[HBM_SPEC] * 2,
        out_specs=(VMEM_SPEC,) * 3,
        scratch_shapes=[
            pltpu.VMEM(velocity.shape, f32),
            pltpu.VMEM(wet_bits.shape, jnp.int32),
            pltpu.SemaphoreType.DMA((2,)),
        ],
        compiler_params=params,
        name="mask",
    )(
        pltpu.with_memory_space_constraint(velocity, pltpu.HBM),
        pltpu.with_memory_space_constraint(wet_bits, pltpu.HBM),
    )
    order, turn, x_taps, y_taps = pl.pallas_call(
        functools.partial(prepare_kernel, geom),
        out_shape=(
            shape((1,), jnp.int32),
            shape((SUBLANES, LANES), f32),
            shape((wide, 2 * wide), bf16),
            shape((4 * out_rows, window), bf16),
        ),
        in_specs=[HBM_SPEC] * 2,
        out_specs=(SMEM_SPEC,) + (VMEM_SPEC,) * 3,
        scratch_shapes=[
            pltpu.SMEM(east_face.shape, jnp.int32),
            pltpu.SMEM(seam_turn.shape, jnp.int32),
            pltpu.SemaphoreType.DMA((2,)),
        ],
        compiler_params=params,
        name="prepare",
    )(
        pltpu.with_memory_space_constraint(east_face, pltpu.HBM),
        pltpu.with_memory_space_constraint(seam_turn, pltpu.HBM),
    )
    if row_count == 2:
        before = lax.ppermute(rows, "row", [(0, 1), (1, 0)])
        after = before
    elif row_count > 2:
        up = [(i, i + 1) for i in range(row_count - 1)]
        before = lax.ppermute(rows[:, depth:], "row", up)
        after = lax.ppermute(rows[:, :depth], "row", [(j, i) for i, j in up])
    else:
        before = after = rows
    extended, outer, inner = pl.pallas_call(
        functools.partial(extend_kernel, geom),
        out_shape=(
            shape((2, window, LANES), f32),
            shape((packed_rows(window), LANES), f32),
            shape((packed_rows(window), LANES), f32),
        ),
        in_specs=[VMEM_SPEC] * 3,
        out_specs=(VMEM_SPEC,) * 3,
        compiler_params=params,
        name="extend",
    )(field, before, after)

    def finish(seam, beside):
        partial, edges = pl.pallas_call(
            functools.partial(inner_kernel, geom),
            out_shape=(
                shape((3, 2 * window, LANES), f32),
                shape((2, window, LANES), f32),
            ),
            in_specs=[VMEM_SPEC] * 2,
            out_specs=(VMEM_SPEC,) * 2,
            scratch_shapes=[
                pltpu.VMEM((2, window + 2 * SUBLANES, LANES), f32),
                pltpu.VMEM((2, 4 * window, LANES), bf16),
            ],
            compiler_params=params,
            name="inner",
        )(extended, x_taps)
        return pl.pallas_call(
            functools.partial(filter_kernel, geom),
            out_shape=shape((n_rows // COARSE, 2, n_cols // COARSE), f32),
            in_specs=[VMEM_SPEC] * 8,
            out_specs=VMEM_SPEC,
            scratch_shapes=[
                pltpu.VMEM((2, window + 2 * SUBLANES, LANES), f32),
                pltpu.VMEM((2, 4 * window, LANES), bf16),
                pltpu.VMEM((2, 3, window, wide), bf16),
                pltpu.VMEM((2, n_rows, LANES), f32),
            ],
            compiler_params=params,
            name="filter",
        )(seam, beside, edges, partial, wet, turn, x_taps, y_taps)

    forcing = exchange(order, east_face, outer, inner, finish)
    return jnp.transpose(forcing, (1, 0, 2))


def solution(mesh):
    placed = (
        P(None, ("grp", "row"), ("tile", "sub")),
        P(("grp", "row"), ("tile", "sub")),
        P(),
        P(),
    )
    return jax.shard_map(
        on_device,
        mesh=mesh,
        in_specs=placed,
        out_specs=P(None, ("grp", "row"), ("tile", "sub")),
        check_vma=False,
    )
```

```python
import functools
import itertools

import jax
import jax.numpy as jnp
import numpy as np
from jax import lax
from jax.experimental import pallas as pl
from jax.experimental.pallas import tpu as pltpu
from jax.sharding import PartitionSpec as P

R = 32
RIM = R + 1
BITS = 30
COARSE = 4
LANES = 128
HALF = LANES // 2
GROUPS = 3
GROUP = 40
SUBLANES = 8
SWITCHED_FACES = 4

deriv_scale = 8.0

f32 = jnp.float32
bf16 = jnp.bfloat16


def up_to(value, step):
    return -(-value // step) * step


def iota(shape, dim):
    return lax.broadcasted_iota(jnp.int32, shape, dim)


def split(value):
    high = value.astype(bf16)
    return high, (value - high.astype(f32)).astype(bf16)


def dot(left, right):
    return jnp.dot(left, right, preferred_element_type=f32)


def taps_sum():
    taps = np.arange(-R, R + 1, dtype=np.float64)
    return float(np.sum(np.exp(-0.5 * (taps / R) ** 2)))


def gaussian(distance, inside):
    inside = inside & (distance >= -R) & (distance <= R)
    scaled = distance.astype(f32) * (1.0 / R)
    return jnp.where(inside, jnp.exp(-0.5 * scaled * scaled) * (1.0 / taps_sum()), 0.0)


def roll(value, shift):
    return pltpu.roll(value, shift % LANES, axis=1)


def fetch(pairs, sems):
    copies = [pltpu.make_async_copy(a, b, sems.at[i]) for i, (a, b) in enumerate(pairs)]
    for copy in copies:
        copy.start()
    for copy in copies:
        copy.wait()


def mask_kernel(geom, velocity, wet_bits, field, rows, wet, vel, packed, sems):
    n_rows, n_cols, depth, row_count, _ = geom
    fetch(((velocity, vel), (wet_bits, packed)), sems)
    at = iota((n_rows, n_cols), 0)
    word = jnp.broadcast_to(packed[0:1, :], (n_rows, n_cols))
    shift = at
    for j in range(1, n_rows // BITS):
        line = jnp.broadcast_to(packed[j : j + 1, :], (n_rows, n_cols))
        later = at >= j * BITS
        word = jnp.where(later, line, word)
        shift = jnp.where(later, at - j * BITS, shift)
    mask = (jnp.right_shift(word, shift) & 1).astype(f32)
    margin = jnp.zeros((n_rows, LANES - n_cols), f32)
    wet[:, :n_cols] = mask
    wet[:, n_cols:] = margin
    row_at = lax.axis_index("row")
    for c in range(2):
        value = jnp.concatenate([vel[c] * mask, margin], axis=1)
        field[c] = value
        if row_count == 2:
            rows[c] = jnp.where(row_at == 0, value[n_rows - depth :], value[:depth])
        elif row_count > 2:
            rows[c, :depth] = value[:depth]
            rows[c, depth:] = value[n_rows - depth :]


def seam_order(faces):
    count = faces.shape[0]
    order = jnp.int32(0)
    for i in range(count):
        smaller = jnp.int32(0)
        for j in range(i + 1, count):
            smaller = smaller + jnp.where(faces[j] < faces[i], 1, 0)
        order = order * (count - i) + smaller
    return order


def prepare_kernel(
    geom, east_face, seam_turn, order, turn, x_taps, y_taps, faces, turns, sems
):
    n_rows, n_cols, depth, row_count, window = geom
    copies = [
        pltpu.make_async_copy(east_face, faces, sems.at[0]),
        pltpu.make_async_copy(seam_turn, turns, sems.at[1]),
    ]
    for copy in copies:
        copy.start()
    row_at = lax.axis_index("row")
    lane = iota((2 * LANES, LANES), 0)
    target = iota((2 * LANES, LANES), 1)
    rim = lane - LANES
    column = jnp.where(
        lane < LANES, lane, jnp.where(rim < HALF - 1, rim - RIM, rim - HALF + n_cols)
    )
    inside = (
        ((lane >= 1) & (lane < n_cols - 1))
        | ((rim >= 0) & (rim <= RIM))
        | ((rim >= HALF - 1) & (rim < HALF + RIM))
    )
    inside = inside & (target < n_cols)
    away = column - target
    value = split(gaussian(away, inside))
    slope = split(gaussian(away - 1, inside) - gaussian(away + 1, inside))
    for i, taps in enumerate((slope[1], value[1], value[0], slope[0])):
        x_taps[:, i * LANES : (i + 1) * LANES] = taps
    out_rows = up_to(n_rows, 2 * SUBLANES)
    source = iota((out_rows, window), 1)
    target = iota((out_rows, window), 0)
    start = row_start(geom, row_at)
    world = source - start + row_at * n_rows
    last = row_count * n_rows

    def taps_at(step):
        at = world + step
        inside = (at >= 0) & (at < last) & (target < n_rows)
        return gaussian(source + step - start - target, inside)

    value = split(taps_at(0))
    slope = split(taps_at(-1) - taps_at(1))
    for i, taps in enumerate((slope[1], slope[0], value[0], value[1])):
        y_taps[i * out_rows : (i + 1) * out_rows, :] = taps
    for copy in copies:
        copy.wait()
    order[0] = seam_order(faces) if faces.shape[0] <= SWITCHED_FACES else jnp.int32(0)
    write_turn(faces, turns, turn)


def write_turn(faces, turns, turn):
    tile_at = lax.axis_index("tile")
    back = jnp.int32(0)
    for w in range(faces.shape[0]):
        back = jnp.where(faces[w] == tile_at, turns[w], back)
    sub_at = lax.axis_index("sub")
    quarter = jnp.where(sub_at == 0, (4 - back) % 4, turns[tile_at])
    cosine = jnp.where(quarter == 0, 1.0, jnp.where(quarter == 2, -1.0, 0.0)).astype(f32)
    sine = jnp.where(quarter == 1, 1.0, jnp.where(quarter == 3, -1.0, 0.0)).astype(f32)
    row = iota((SUBLANES, LANES), 0)
    lane = iota((SUBLANES, LANES), 1)
    seam_lane = seam_side(lane, sub_at)
    turn[...] = jnp.where(
        row == 0, jnp.where(seam_lane, cosine, 1.0), jnp.where(seam_lane, sine, 0.0)
    )


def seam_side(lane, sub_at):
    edge = jnp.where(sub_at == 0, RIM, LANES)
    start = jnp.where(sub_at == 0, 0, HALF)
    return (lane >= start) & (lane < edge)


def packed_rows(window):
    return up_to(-(-2 * window // GROUPS), SUBLANES)


def pieces(window):
    size = packed_rows(window)
    cuts = sorted({0, window, 2 * window, *(size * g for g in range(1, GROUPS))})
    return [
        (a // window, a % window, a // size, a % size, b - a) for a, b in zip(cuts, cuts[1:])
    ]


def row_start(geom, row_at):
    _, _, depth, row_count, _ = geom
    if row_count == 2:
        return jnp.where(row_at == 0, 0, depth)
    return jnp.int32(depth if row_count > 2 else 0)


def extend_kernel(geom, field, before, after, extended, outer, inner):
    n_rows, n_cols, depth, row_count, window = geom
    row_at = lax.axis_index("row")
    whole = []
    for c in range(2):
        mine = field[c]
        if row_count == 2:
            other = before[c]
            value = jnp.where(
                row_at == 0,
                jnp.concatenate([mine, other], axis=0),
                jnp.concatenate([other, mine], axis=0),
            )
        elif row_count > 2:
            value = jnp.concatenate([before[c], mine, after[c]], axis=0)
        else:
            value = mine
        extended[c] = value
        whole.append(value)
    first = lax.axis_index("sub") == 0
    far = RIM - n_cols
    pack(whole, window, jnp.where(first, 0, far), outer)
    pack(whole, window, jnp.where(first, far, 0), inner)


def pad_rows(padded, c, window, value):
    blank = jnp.zeros((SUBLANES, LANES), f32)
    padded[c, :SUBLANES, :] = blank
    padded[c, SUBLANES + window :, :] = blank
    padded[c, SUBLANES : SUBLANES + window, :] = value


def channels(padded, columns, window):
    vel = [padded[c, SUBLANES : SUBLANES + window, :] for c in range(2)]
    for c in range(2):
        grad_x = roll(vel[c], -1) - roll(vel[c], 1)
        grad_y = (
            padded[c, SUBLANES + 1 : SUBLANES + 1 + window, :]
            - padded[c, SUBLANES - 1 : SUBLANES - 1 + window, :]
        )
        advect = vel[0] * grad_x + vel[1] * grad_y
        for at, value in ((c, vel[c]), (2 + c, advect)):
            high, low_part = split(value)
            columns[0, at * window : (at + 1) * window, :] = high
            columns[1, at * window : (at + 1) * window, :] = low_part


def across_x(columns, x_taps, window):
    wide = 2 * LANES
    high = x_taps[:, wide:]
    low_part = x_taps[:, :wide]
    both = x_taps[:, LANES : LANES + wide]
    main = dot(columns[0, : 2 * window, :], high)
    more = dot(columns[1, : 2 * window, :], high)
    rest = dot(columns[0, : 2 * window, :], low_part)
    flux = dot(columns[0, 2 * window :, :], both)
    flux_more = dot(columns[1, 2 * window :, :], both[:, LANES:])
    means = main[:, :LANES] + (more[:, :LANES] + rest[:, LANES:])
    slopes = main[:, LANES:] + (more[:, LANES:] + rest[:, :LANES])
    fluxes = flux[:, LANES:] + (flux_more + flux[:, :LANES])
    return means, slopes, fluxes


def inner_kernel(geom, extended, x_taps, partial, edges, padded, columns):
    n_rows, n_cols, depth, row_count, window = geom
    lane = iota((window, LANES), 1)
    for c in range(2):
        own = extended[c]
        pad_rows(padded, c, window, own)
        near = jnp.where(lane < RIM + 2, roll(own, RIM), roll(own, HALF - n_cols))
        edges[c] = near
    channels(padded, columns, window)
    for pair, value in enumerate(across_x(columns, x_taps[:LANES, :], window)):
        partial[pair] = value


def filter_kernel(
    geom,
    seam,
    beside,
    edges,
    partial,
    wet,
    turn,
    x_taps,
    y_taps,
    forcing,
    padded,
    columns,
    along,
    pools,
):
    n_rows, n_cols, depth, row_count, window = geom
    sub_at = lax.axis_index("sub")
    out_rows = up_to(n_rows, 2 * SUBLANES)
    turned = unpack(seam, beside, window, turn, sub_at)
    lane = iota((window, LANES), 1)
    own = (lane >= RIM) & (lane < HALF)
    for c in range(2):
        pad_rows(padded, c, window, jnp.where(own, edges[c], turned[c]))
    channels(padded, columns, window)
    for pair, value in enumerate(across_x(columns, x_taps[LANES:, :], window)):
        value = value + partial[pair]
        high, low_part = split(value)
        for c in range(2):
            at = slice(c * LANES, (c + 1) * LANES)
            along[0, pair, :, at] = high[c * window : (c + 1) * window]
            along[1, pair, :, at] = low_part[c * window : (c + 1) * window]

    main = dot(y_taps[...], along[0, 0])
    more = dot(y_taps[out_rows : 3 * out_rows, :], along[1, 0])
    slope_y = main[out_rows : 2 * out_rows] + (main[:out_rows] + more[:out_rows])
    mean = main[2 * out_rows : 3 * out_rows] + (main[3 * out_rows :] + more[out_rows:])

    def across(pair):
        main = dot(y_taps[2 * out_rows :, :], along[0, pair])
        more = dot(y_taps[2 * out_rows : 3 * out_rows, :], along[1, pair])
        return main[:out_rows] + (main[out_rows:] + more)

    slope_x = across(1)
    flux = across(2)
    mean_u = mean[:n_rows, :LANES]
    mean_v = mean[:n_rows, LANES:]
    mask = wet[...]
    coarse = n_rows // COARSE
    for c in range(2):
        at = slice(c * LANES, (c + 1) * LANES)
        pools[c] = mask * (
            flux[:n_rows, at] - (mean_u * slope_x[:n_rows, at] + mean_v * slope_y[:n_rows, at])
        )
    block = iota((LANES, LANES), 0) // COARSE == iota((LANES, LANES), 1)
    gather = jnp.where(block, deriv_scale / (COARSE * COARSE), 0.0).astype(bf16)
    for c in range(2):
        rows = [pools[c, pl.ds(k, coarse, stride=COARSE), :] for k in range(COARSE)]
        high, low_part = split((rows[0] + rows[1]) + (rows[2] + rows[3]))
        value = dot(high, gather) + dot(low_part, gather)
        forcing[:, c, :] = value[:, : n_cols // COARSE]


EDGE = 4


def np_split(value):
    high = value.astype(bf16)
    return high, (value - high.astype(np.float64)).astype(bf16)


def np_gaussian(distance):
    inside = np.abs(distance) <= R
    return np.where(inside, np.exp(-0.5 * (distance / R) ** 2) / taps_sum(), 0.0)


def x_constant(n_cols):
    lane = np.arange(2 * LANES)[:, None]
    target = np.arange(LANES)[None, :]
    rim = lane - LANES
    column = np.where(
        lane < LANES, lane, np.where(rim < HALF - 1, rim - RIM, rim - HALF + n_cols)
    )
    inside = (
        ((lane >= 1) & (lane < n_cols - 1))
        | ((rim >= 0) & (rim <= RIM))
        | ((rim >= HALF - 1) & (rim < HALF + RIM))
    )
    inside = inside & (target < n_cols)
    away = column - target
    value = np_split(np.where(inside, np_gaussian(away), 0.0))
    slope = np_split(np.where(inside, np_gaussian(away - 1) - np_gaussian(away + 1), 0.0))
    return np.concatenate([slope[1], value[1], value[0], slope[0]], axis=1)


def y_constant(target, source, used, first_row, last_row):
    def step(by):
        at = source + by
        inside = used & (at >= first_row) & (at < last_row)
        return np.where(inside[None, :], np_gaussian(at[None, :] - target[:, None]), 0.0)

    value = np_split(step(0))
    slope = np_split(step(-1) - step(1))
    pad = ((0, up_to(target.shape[0], 2 * SUBLANES) - target.shape[0]), (0, 0))
    return np.concatenate(
        [np.pad(taps, pad) for taps in (slope[1], slope[0], value[0], value[1])], axis=0
    )


def y_constants(n_rows, depth, near):
    own, tail = [], []
    for row_at in range(2):
        bounds = (-row_at * n_rows, (2 - row_at) * n_rows)
        source = np.arange(up_to(n_rows, 2 * SUBLANES))
        late = source >= n_rows - EDGE if row_at == 0 else source < EDGE
        used = ~late & (source < n_rows)
        own.append(y_constant(np.arange(n_rows), source, used, *bounds))
        source = np.arange(near + depth)
        source = source + n_rows - near if row_at == 0 else source - depth
        late = source >= n_rows - EDGE if row_at == 0 else source < EDGE
        target = np.arange(depth) + (n_rows - depth if row_at == 0 else 0)
        tail.append(y_constant(target, source, late, *bounds))
    return np.stack(own), np.stack(tail)


def start_all(pairs, sems):
    copies = [pltpu.make_async_copy(a, b, sems.at[i]) for i, (a, b) in enumerate(pairs)]
    for copy in copies:
        copy.start()
    return copies


def pack(whole, rows, base, to):
    size = packed_rows(rows)
    lane = iota((size, LANES), 1)
    groups = [[] for _ in range(GROUPS)]
    for c, row, group, _, count in pieces(rows):
        groups[group].append(whole[c][row : row + count])
    spare = GROUPS * size - 2 * rows
    if spare:
        groups[-1].append(jnp.zeros((spare, LANES), f32))
    groups = [jnp.concatenate(group, axis=0) for group in groups]
    value = roll(groups[-1], base + (GROUPS - 1) * GROUP)
    for g in reversed(range(GROUPS - 1)):
        value = jnp.where(lane < (g + 1) * GROUP, roll(groups[g], base + g * GROUP), value)
    to[...] = value


def unpack(seam, beside, rows, turn, sub_at):
    near = jnp.where(sub_at == 0, 0, HALF)
    parts = [[], []]
    for c, _, group, row, count in pieces(rows):
        lane = iota((count, LANES), 1)
        parts[c].append(
            jnp.where(
                seam_side(lane, sub_at),
                roll(seam[row : row + count, :], near - group * GROUP),
                roll(beside[row : row + count, :], HALF - near - group * GROUP),
            )
        )
    east, north = (jnp.concatenate(part, axis=0) for part in parts)
    cosine = turn[0:1, :]
    sine = turn[1:2, :]
    return cosine * east - sine * north, sine * east + cosine * north


def open_kernel(
    geom,
    velocity,
    wet_bits,
    east_face,
    seam_turn,
    field,
    rows,
    outer,
    inner,
    wet,
    turn,
    order,
    vel,
    packed,
    faces,
    turns,
    sems,
):
    n_rows, n_cols, depth, _ = geom
    copies = start_all(
        ((east_face, faces), (seam_turn, turns), (wet_bits, packed), (velocity, vel)), sems
    )
    for copy in copies[:2]:
        copy.wait()
    order[0] = seam_order(faces)
    sub_at = lax.axis_index("sub")
    write_turn(faces, turns, turn)
    copies[2].wait()
    at = iota((n_rows, n_cols), 0)
    word = jnp.broadcast_to(packed[0:1, :], (n_rows, n_cols))
    shift = at
    for j in range(1, n_rows // BITS):
        line = jnp.broadcast_to(packed[j : j + 1, :], (n_rows, n_cols))
        later = at >= j * BITS
        word = jnp.where(later, line, word)
        shift = jnp.where(later, at - j * BITS, shift)
    mask = (jnp.right_shift(word, shift) & 1).astype(f32)
    margin = jnp.zeros((n_rows, LANES - n_cols), f32)
    wet[:, :n_cols] = mask
    wet[:, n_cols:] = margin
    copies[3].wait()
    row_at = lax.axis_index("row")
    whole = []
    for c in range(2):
        value = jnp.concatenate([vel[c] * mask, margin], axis=1)
        field[c] = value
        rows[c] = jnp.where(row_at == 0, value[n_rows - depth :], value[:depth])
        whole.append(value)
    far = RIM - n_cols
    pack(whole, n_rows, jnp.where(sub_at == 0, 0, far), outer)
    pack(whole, n_rows, jnp.where(sub_at == 0, far, 0), inner)


def rims_kernel(geom, seam, beside, other, field, turn, rims, corner, halo):
    n_rows, n_cols, depth, _ = geom
    turned = unpack(seam, beside, n_rows, turn, lax.axis_index("sub"))
    row_at = lax.axis_index("row")
    lane = iota((n_rows, LANES), 1)
    own = (lane >= RIM) & (lane < HALF)
    for c in range(2):
        mine = field[c]
        near = jnp.where(lane < RIM + 2, roll(mine, RIM), roll(mine, HALF - n_cols))
        value = jnp.where(own, near, turned[c])
        rims[c] = value
        corner[c] = jnp.where(row_at == 0, value[n_rows - depth :], value[:depth])
        halo[c] = other[c]


def edge_rows(row_at, own, other, near):
    n_rows = own.shape[0]
    return jnp.where(
        row_at == 0,
        jnp.concatenate([own[n_rows - near :], other], axis=0),
        jnp.concatenate([other, own[:near]], axis=0),
    )


def keep_along(along, pair, value, rows):
    high, low_part = split(value)
    for c in range(2):
        at = slice(c * LANES, (c + 1) * LANES)
        along[0, pair, :, at] = high[c * rows : (c + 1) * rows]
        along[1, pair, :, at] = low_part[c * rows : (c + 1) * rows]


def across_y(y_taps, along, size):
    main = dot(y_taps[...], along[0, 0])
    more = dot(y_taps[size : 3 * size, :], along[1, 0])
    slope_y = main[size : 2 * size] + (main[:size] + more[:size])
    mean = main[2 * size : 3 * size] + (main[3 * size :] + more[size:])

    def plain(pair):
        main = dot(y_taps[2 * size :, :], along[0, pair])
        more = dot(y_taps[2 * size : 3 * size, :], along[1, pair])
        return main[:size] + (main[size:] + more)

    return slope_y, mean, plain(1), plain(2)


def pool(smooth, mask, pools):
    slope_y, mean, slope_x, flux = smooth
    count = mask.shape[0]
    mean_u = mean[:, :LANES]
    mean_v = mean[:, LANES:]
    block = iota((LANES, LANES), 0) // COARSE == iota((LANES, LANES), 1)
    gather = jnp.where(block, deriv_scale / (COARSE * COARSE), 0.0).astype(bf16)
    out = []
    for c in range(2):
        at = slice(c * LANES, (c + 1) * LANES)
        pools[c] = mask * (flux[:, at] - (mean_u * slope_x[:, at] + mean_v * slope_y[:, at]))
        rows = [
            pools[c, pl.ds(k, count // COARSE, stride=COARSE), :] for k in range(COARSE)
        ]
        high, low_part = split((rows[0] + rows[1]) + (rows[2] + rows[3]))
        out.append(dot(high, gather) + dot(low_part, gather))
    return out


def own_kernel(
    geom,
    field,
    rims,
    halo,
    wet,
    x_source,
    y_source,
    tail_source,
    part,
    tail,
    tail_wet,
    partial,
    x_taps,
    tail_taps,
    padded,
    columns,
    along,
    pools,
    tail_padded,
    tail_columns,
    y_taps,
    sems,
):
    n_rows, n_cols, depth, near = geom
    row_at = lax.axis_index("row")
    copies = start_all(
        (
            (x_source, x_taps),
            (y_source.at[row_at], y_taps),
            (tail_source.at[row_at], tail_taps),
        ),
        sems,
    )
    size = up_to(n_rows, 2 * SUBLANES)
    blank = jnp.zeros((size - n_rows, LANES), f32)
    for half, source in enumerate((field, rims)):
        for c in range(2):
            value = source[c]
            if size > n_rows:
                value = jnp.concatenate([value, blank], axis=0)
            pad_rows(padded.at[half], c, size, value)
        channels(
            padded.at[half], columns.at[:, :, half * LANES : (half + 1) * LANES], size
        )
    for c in range(2):
        pad_rows(tail_padded, c, near + depth, edge_rows(row_at, field[c], halo[c], near))
    channels(tail_padded, tail_columns, near + depth)
    for copy in copies:
        copy.wait()
    for pair, value in enumerate(across_x(columns, x_taps, size)):
        keep_along(along, pair, value, size)
    for pair, value in enumerate(across_x(tail_columns, x_taps[:LANES, :], near + depth)):
        partial[pair] = value
    smooth = [value[:n_rows] for value in across_y(y_taps, along, size)]
    mask = wet[...]
    for i, value in enumerate(smooth):
        tail[i] = jnp.where(row_at == 0, value[n_rows - depth :], value[:depth])
    tail_wet[...] = jnp.where(row_at == 0, mask[n_rows - depth :], mask[:depth])
    for c, value in enumerate(pool(smooth, mask, pools)):
        part[:, c, :] = value[:, : n_cols // COARSE]


def close_kernel(
    geom,
    corner,
    rims,
    part,
    tail,
    tail_wet,
    partial,
    x_taps,
    tail_taps,
    forcing,
    padded,
    columns,
    along,
    pools,
):
    n_rows, n_cols, depth, near = geom
    row_at = lax.axis_index("row")
    size = near + depth
    for c in range(2):
        pad_rows(padded, c, size, edge_rows(row_at, rims[c], corner[c], near))
    channels(padded, columns, size)
    for pair, value in enumerate(across_x(columns, x_taps[LANES:, :], size)):
        keep_along(along, pair, value + partial[pair], size)
    smooth = across_y(tail_taps, along, up_to(depth, 2 * SUBLANES))
    smooth = [value[:depth] + tail[i] for i, value in enumerate(smooth)]
    forcing[...] = part[...]
    start = jnp.where(row_at == 0, (n_rows - depth) // COARSE, 0)
    for c, value in enumerate(pool(smooth, tail_wet[...], pools)):
        forcing[pl.ds(start, depth // COARSE), c, :] = value[:, : n_cols // COARSE]


VMEM_SPEC = pl.BlockSpec(memory_space=pltpu.VMEM)
SMEM_SPEC = pl.BlockSpec(memory_space=pltpu.SMEM)
HBM_SPEC = pl.BlockSpec(memory_space=pltpu.HBM)


def choose(index, branches, *operands):
    closed = jax.make_jaxpr(lambda i, *rest: lax.switch(i, branches, *rest))(index, *operands)
    values = dict(zip(closed.jaxpr.constvars, closed.consts))
    values.update(zip(closed.jaxpr.invars, jax.tree.leaves((index, *operands))))

    def read(atom):
        return atom.val if hasattr(atom, "val") else values[atom]

    for eqn in closed.jaxpr.eqns:
        taken = [read(atom) for atom in eqn.invars]
        if eqn.primitive is lax.clamp_p:
            given = taken[1]
        else:
            given = eqn.primitive.bind(*taken, **eqn.params)
        if not eqn.primitive.multiple_results:
            given = [given]
        values.update(zip(eqn.outvars, given))
    return [read(atom) for atom in closed.jaxpr.outvars]


def seam_pairs(order, subs):
    pairs = []
    for west, east in enumerate(order):
        pairs += [(west * subs + subs - 1, east * subs), (east * subs, west * subs + subs - 1)]
    return pairs


def beside_pairs(subs):
    return [(i, subs - 1 - i) for i in range(subs)]


def exchange(order, east_face, outer, inner, finish):
    faces = east_face.shape[0]
    subs = lax.axis_size("sub")
    beside = beside_pairs(subs)

    def swap(order, outer, inner):
        seam = lax.ppermute(outer, ("tile", "sub"), seam_pairs(order, subs))
        return finish(seam, lax.ppermute(inner, "sub", beside))

    if faces <= SWITCHED_FACES:
        orders = itertools.permutations(range(faces))
        branches = [functools.partial(swap, order) for order in orders]
        return lax.switch(order[0], branches, outer, inner)
    tile_at = lax.axis_index("tile")
    sub_at = lax.axis_index("sub")
    west = jnp.sum(jnp.where(east_face == tile_at, jnp.arange(faces, dtype=jnp.int32), 0))
    east = lax.dynamic_index_in_dim(east_face, tile_at, 0, keepdims=False)
    gathered = lax.all_gather(lax.ppermute(outer, "sub", beside), "tile")
    partner = jnp.where(sub_at == 0, west, east)
    seam = lax.dynamic_index_in_dim(gathered, partner, 0, keepdims=False)
    return finish(seam, lax.ppermute(inner, "sub", beside))


def in_hbm(value):
    return pltpu.with_memory_space_constraint(value, pltpu.HBM)


def paired(velocity, wet_bits, east_face, seam_turn):
    _, n_rows, n_cols = velocity.shape
    depth = up_to(RIM, SUBLANES)
    near = up_to(depth + SUBLANES, 2 * SUBLANES) + 2 * SUBLANES - depth
    geom = (n_rows, n_cols, depth, near)
    size = up_to(n_rows, 2 * SUBLANES)
    tail_size = up_to(depth, 2 * SUBLANES)
    end = near + depth
    wide = 2 * LANES
    coarse = n_rows // COARSE
    params = pltpu.CompilerParams(vmem_limit_bytes=16 << 20)
    shape = jax.ShapeDtypeStruct
    kernel = lambda body, name, **rest: pl.pallas_call(
        functools.partial(body, geom), name=name, compiler_params=params, **rest
    )
    packed = shape((packed_rows(n_rows), LANES), f32)
    field, rows, outer, inner, wet, turn, order = kernel(
        open_kernel,
        "open",
        out_shape=(
            shape((2, n_rows, LANES), f32),
            shape((2, depth, LANES), f32),
            packed,
            packed,
            shape((n_rows, LANES), f32),
            shape((SUBLANES, LANES), f32),
            shape((1,), jnp.int32),
        ),
        in_specs=[HBM_SPEC] * 4,
        out_specs=(VMEM_SPEC,) * 6 + (SMEM_SPEC,),
        scratch_shapes=[
            pltpu.VMEM(velocity.shape, f32),
            pltpu.VMEM(wet_bits.shape, jnp.int32),
            pltpu.SMEM(east_face.shape, jnp.int32),
            pltpu.SMEM(seam_turn.shape, jnp.int32),
            pltpu.SemaphoreType.DMA((4,)),
        ],
    )(in_hbm(velocity), in_hbm(wet_bits), in_hbm(east_face), in_hbm(seam_turn))
    subs = lax.axis_size("sub")

    def swap(order, outer, inner, rows, field, turn):
        seam = lax.ppermute(outer, ("tile", "sub"), seam_pairs(order, subs))
        other = lax.ppermute(rows, "row", [(0, 1), (1, 0)])
        beside = lax.ppermute(inner, "sub", beside_pairs(subs))
        return kernel(
            rims_kernel,
            "rims",
            out_shape=(
                shape((2, n_rows, LANES), f32),
                shape((2, depth, LANES), f32),
                shape((2, depth, LANES), f32),
            ),
            in_specs=[VMEM_SPEC] * 5,
            out_specs=(VMEM_SPEC,) * 3,
        )(seam, beside, other, field, turn)

    orders = itertools.permutations(range(east_face.shape[0]))
    branches = [functools.partial(swap, order) for order in orders]
    rims, corner, halo = choose(order[0], branches, outer, inner, rows, field, turn)
    corner = lax.ppermute(corner, "row", [(0, 1), (1, 0)])
    own_taps, tail_taps = y_constants(n_rows, depth, near)
    x_taps = jnp.asarray(x_constant(n_cols))
    part, tail, tail_wet, partial, x_taps, tail_taps = kernel(
        own_kernel,
        "own",
        out_shape=(
            shape((coarse, 2, n_cols // COARSE), f32),
            shape((4, depth, wide), f32),
            shape((depth, LANES), f32),
            shape((3, 2 * end, LANES), f32),
            shape(x_taps.shape, bf16),
            shape(tail_taps.shape[1:], bf16),
        ),
        in_specs=[VMEM_SPEC] * 4 + [HBM_SPEC] * 3,
        out_specs=(VMEM_SPEC,) * 6,
        scratch_shapes=[
            pltpu.VMEM((2, 2, size + 2 * SUBLANES, LANES), f32),
            pltpu.VMEM((2, 4 * size, wide), bf16),
            pltpu.VMEM((2, 3, size, wide), bf16),
            pltpu.VMEM((2, n_rows, LANES), f32),
            pltpu.VMEM((2, end + 2 * SUBLANES, LANES), f32),
            pltpu.VMEM((2, 4 * end, LANES), bf16),
            pltpu.VMEM(own_taps.shape[1:], bf16),
            pltpu.SemaphoreType.DMA((3,)),
        ],
        cost_estimate=pl.CostEstimate(
            flops=1 << 30, bytes_accessed=1 << 22, transcendentals=0
        ),
    )(
        field,
        rims,
        halo,
        wet,
        in_hbm(x_taps),
        in_hbm(jnp.asarray(own_taps)),
        in_hbm(jnp.asarray(tail_taps)),
    )
    forcing = kernel(
        close_kernel,
        "close",
        out_shape=shape((coarse, 2, n_cols // COARSE), f32),
        in_specs=[VMEM_SPEC] * 8,
        out_specs=VMEM_SPEC,
        scratch_shapes=[
            pltpu.VMEM((2, end + 2 * SUBLANES, LANES), f32),
            pltpu.VMEM((2, 4 * end, LANES), bf16),
            pltpu.VMEM((2, 3, end, wide), bf16),
            pltpu.VMEM((2, depth, LANES), f32),
        ],
    )(corner, rims, part, tail, tail_wet, partial, x_taps, tail_taps)
    return jnp.transpose(forcing, (1, 0, 2))


def on_device(velocity, wet_bits, east_face, seam_turn):
    _, n_rows, n_cols = velocity.shape
    row_count = lax.axis_size("row")
    if row_count == 2 and east_face.shape[0] <= SWITCHED_FACES:
        return paired(velocity, wet_bits, east_face, seam_turn)
    depth = up_to(RIM, SUBLANES)
    sides = min(row_count - 1, 2)
    window = n_rows + sides * depth
    geom = (n_rows, n_cols, depth, row_count, window)
    sent = depth * max(sides, 1)
    wide = 2 * LANES
    out_rows = up_to(n_rows, 2 * SUBLANES)
    params = pltpu.CompilerParams(vmem_limit_bytes=16 << 20)
    shape = jax.ShapeDtypeStruct
    field, rows, wet = pl.pallas_call(
        functools.partial(mask_kernel, geom),
        out_shape=(
            shape((2, n_rows, LANES), f32),
            shape((2, sent, LANES), f32),
            shape((n_rows, LANES), f32),
        ),
        in_specs=[HBM_SPEC] * 2,
        out_specs=(VMEM_SPEC,) * 3,
        scratch_shapes=[
            pltpu.VMEM(velocity.shape, f32),
            pltpu.VMEM(wet_bits.shape, jnp.int32),
            pltpu.SemaphoreType.DMA((2,)),
        ],
        compiler_params=params,
        name="mask",
    )(
        pltpu.with_memory_space_constraint(velocity, pltpu.HBM),
        pltpu.with_memory_space_constraint(wet_bits, pltpu.HBM),
    )
    order, turn, x_taps, y_taps = pl.pallas_call(
        functools.partial(prepare_kernel, geom),
        out_shape=(
            shape((1,), jnp.int32),
            shape((SUBLANES, LANES), f32),
            shape((wide, 2 * wide), bf16),
            shape((4 * out_rows, window), bf16),
        ),
        in_specs=[HBM_SPEC] * 2,
        out_specs=(SMEM_SPEC,) + (VMEM_SPEC,) * 3,
        scratch_shapes=[
            pltpu.SMEM(east_face.shape, jnp.int32),
            pltpu.SMEM(seam_turn.shape, jnp.int32),
            pltpu.SemaphoreType.DMA((2,)),
        ],
        compiler_params=params,
        name="prepare",
    )(
        pltpu.with_memory_space_constraint(east_face, pltpu.HBM),
        pltpu.with_memory_space_constraint(seam_turn, pltpu.HBM),
    )
    if row_count == 2:
        before = lax.ppermute(rows, "row", [(0, 1), (1, 0)])
        after = before
    elif row_count > 2:
        up = [(i, i + 1) for i in range(row_count - 1)]
        before = lax.ppermute(rows[:, depth:], "row", up)
        after = lax.ppermute(rows[:, :depth], "row", [(j, i) for i, j in up])
    else:
        before = after = rows
    extended, outer, inner = pl.pallas_call(
        functools.partial(extend_kernel, geom),
        out_shape=(
            shape((2, window, LANES), f32),
            shape((packed_rows(window), LANES), f32),
            shape((packed_rows(window), LANES), f32),
        ),
        in_specs=[VMEM_SPEC] * 3,
        out_specs=(VMEM_SPEC,) * 3,
        compiler_params=params,
        name="extend",
    )(field, before, after)

    def finish(seam, beside):
        partial, edges = pl.pallas_call(
            functools.partial(inner_kernel, geom),
            out_shape=(
                shape((3, 2 * window, LANES), f32),
                shape((2, window, LANES), f32),
            ),
            in_specs=[VMEM_SPEC] * 2,
            out_specs=(VMEM_SPEC,) * 2,
            scratch_shapes=[
                pltpu.VMEM((2, window + 2 * SUBLANES, LANES), f32),
                pltpu.VMEM((2, 4 * window, LANES), bf16),
            ],
            compiler_params=params,
            name="inner",
        )(extended, x_taps)
        return pl.pallas_call(
            functools.partial(filter_kernel, geom),
            out_shape=shape((n_rows // COARSE, 2, n_cols // COARSE), f32),
            in_specs=[VMEM_SPEC] * 8,
            out_specs=VMEM_SPEC,
            scratch_shapes=[
                pltpu.VMEM((2, window + 2 * SUBLANES, LANES), f32),
                pltpu.VMEM((2, 4 * window, LANES), bf16),
                pltpu.VMEM((2, 3, window, wide), bf16),
                pltpu.VMEM((2, n_rows, LANES), f32),
            ],
            compiler_params=params,
            name="filter",
        )(seam, beside, edges, partial, wet, turn, x_taps, y_taps)

    forcing = exchange(order, east_face, outer, inner, finish)
    return jnp.transpose(forcing, (1, 0, 2))


def solution(mesh):
    placed = (
        P(None, ("grp", "row"), ("tile", "sub")),
        P(("grp", "row"), ("tile", "sub")),
        P(),
        P(),
    )
    return jax.shard_map(
        on_device,
        mesh=mesh,
        in_specs=placed,
        out_specs=P(None, ("grp", "row"), ("tile", "sub")),
        check_vma=False,
    )
```

```python
import functools
import itertools

import jax
import jax.numpy as jnp
import numpy as np
from jax import lax
from jax.experimental import pallas as pl
from jax.experimental.pallas import tpu as pltpu
from jax.sharding import PartitionSpec as P

R = 32
RIM = R + 1
BITS = 30
COARSE = 4
LANES = 128
HALF = LANES // 2
GROUPS = 3
GROUP = 40
SUBLANES = 8
SWITCHED_FACES = 4

deriv_scale = 8.0

f32 = jnp.float32
bf16 = jnp.bfloat16


def up_to(value, step):
    return -(-value // step) * step


def iota(shape, dim):
    return lax.broadcasted_iota(jnp.int32, shape, dim)


def split(value):
    high = value.astype(bf16)
    return high, (value - high.astype(f32)).astype(bf16)


def dot(left, right):
    return jnp.dot(left, right, preferred_element_type=f32)


def taps_sum():
    taps = np.arange(-R, R + 1, dtype=np.float64)
    return float(np.sum(np.exp(-0.5 * (taps / R) ** 2)))


def gaussian(distance, inside):
    inside = inside & (distance >= -R) & (distance <= R)
    scaled = distance.astype(f32) * (1.0 / R)
    return jnp.where(inside, jnp.exp(-0.5 * scaled * scaled) * (1.0 / taps_sum()), 0.0)


def roll(value, shift):
    return pltpu.roll(value, shift % LANES, axis=1)


def fetch(pairs, sems):
    copies = [pltpu.make_async_copy(a, b, sems.at[i]) for i, (a, b) in enumerate(pairs)]
    for copy in copies:
        copy.start()
    for copy in copies:
        copy.wait()


def mask_kernel(geom, velocity, wet_bits, field, rows, wet, vel, packed, sems):
    n_rows, n_cols, depth, row_count, _ = geom
    fetch(((velocity, vel), (wet_bits, packed)), sems)
    at = iota((n_rows, n_cols), 0)
    word = jnp.broadcast_to(packed[0:1, :], (n_rows, n_cols))
    shift = at
    for j in range(1, n_rows // BITS):
        line = jnp.broadcast_to(packed[j : j + 1, :], (n_rows, n_cols))
        later = at >= j * BITS
        word = jnp.where(later, line, word)
        shift = jnp.where(later, at - j * BITS, shift)
    mask = (jnp.right_shift(word, shift) & 1).astype(f32)
    margin = jnp.zeros((n_rows, LANES - n_cols), f32)
    wet[:, :n_cols] = mask
    wet[:, n_cols:] = margin
    row_at = lax.axis_index("row")
    for c in range(2):
        value = jnp.concatenate([vel[c] * mask, margin], axis=1)
        field[c] = value
        if row_count == 2:
            rows[c] = jnp.where(row_at == 0, value[n_rows - depth :], value[:depth])
        elif row_count > 2:
            rows[c, :depth] = value[:depth]
            rows[c, depth:] = value[n_rows - depth :]


def seam_order(faces):
    count = faces.shape[0]
    order = jnp.int32(0)
    for i in range(count):
        smaller = jnp.int32(0)
        for j in range(i + 1, count):
            smaller = smaller + jnp.where(faces[j] < faces[i], 1, 0)
        order = order * (count - i) + smaller
    return order


def prepare_kernel(
    geom, east_face, seam_turn, order, turn, x_taps, y_taps, faces, turns, sems
):
    n_rows, n_cols, depth, row_count, window = geom
    copies = [
        pltpu.make_async_copy(east_face, faces, sems.at[0]),
        pltpu.make_async_copy(seam_turn, turns, sems.at[1]),
    ]
    for copy in copies:
        copy.start()
    row_at = lax.axis_index("row")
    lane = iota((2 * LANES, LANES), 0)
    target = iota((2 * LANES, LANES), 1)
    rim = lane - LANES
    column = jnp.where(
        lane < LANES, lane, jnp.where(rim < HALF - 1, rim - RIM, rim - HALF + n_cols)
    )
    inside = (
        ((lane >= 1) & (lane < n_cols - 1))
        | ((rim >= 0) & (rim <= RIM))
        | ((rim >= HALF - 1) & (rim < HALF + RIM))
    )
    inside = inside & (target < n_cols)
    away = column - target
    value = split(gaussian(away, inside))
    slope = split(gaussian(away - 1, inside) - gaussian(away + 1, inside))
    for i, taps in enumerate((slope[1], value[1], value[0], slope[0])):
        x_taps[:, i * LANES : (i + 1) * LANES] = taps
    out_rows = up_to(n_rows, 2 * SUBLANES)
    source = iota((out_rows, window), 1)
    target = iota((out_rows, window), 0)
    start = row_start(geom, row_at)
    world = source - start + row_at * n_rows
    last = row_count * n_rows

    def taps_at(step):
        at = world + step
        inside = (at >= 0) & (at < last) & (target < n_rows)
        return gaussian(source + step - start - target, inside)

    value = split(taps_at(0))
    slope = split(taps_at(-1) - taps_at(1))
    for i, taps in enumerate((slope[1], slope[0], value[0], value[1])):
        y_taps[i * out_rows : (i + 1) * out_rows, :] = taps
    for copy in copies:
        copy.wait()
    order[0] = seam_order(faces) if faces.shape[0] <= SWITCHED_FACES else jnp.int32(0)
    write_turn(faces, turns, turn)


def write_turn(faces, turns, turn):
    tile_at = lax.axis_index("tile")
    back = jnp.int32(0)
    for w in range(faces.shape[0]):
        back = jnp.where(faces[w] == tile_at, turns[w], back)
    sub_at = lax.axis_index("sub")
    quarter = jnp.where(sub_at == 0, (4 - back) % 4, turns[tile_at])
    cosine = jnp.where(quarter == 0, 1.0, jnp.where(quarter == 2, -1.0, 0.0)).astype(f32)
    sine = jnp.where(quarter == 1, 1.0, jnp.where(quarter == 3, -1.0, 0.0)).astype(f32)
    row = iota((SUBLANES, LANES), 0)
    lane = iota((SUBLANES, LANES), 1)
    seam_lane = seam_side(lane, sub_at)
    turn[...] = jnp.where(
        row == 0, jnp.where(seam_lane, cosine, 1.0), jnp.where(seam_lane, sine, 0.0)
    )


def seam_side(lane, sub_at):
    edge = jnp.where(sub_at == 0, RIM, LANES)
    start = jnp.where(sub_at == 0, 0, HALF)
    return (lane >= start) & (lane < edge)


def packed_rows(window):
    return up_to(-(-2 * window // GROUPS), SUBLANES)


def pieces(window):
    size = packed_rows(window)
    cuts = sorted({0, window, 2 * window, *(size * g for g in range(1, GROUPS))})
    return [
        (a // window, a % window, a // size, a % size, b - a) for a, b in zip(cuts, cuts[1:])
    ]


def row_start(geom, row_at):
    _, _, depth, row_count, _ = geom
    if row_count == 2:
        return jnp.where(row_at == 0, 0, depth)
    return jnp.int32(depth if row_count > 2 else 0)


def extend_kernel(geom, field, before, after, extended, outer, inner):
    n_rows, n_cols, depth, row_count, window = geom
    row_at = lax.axis_index("row")
    whole = []
    for c in range(2):
        mine = field[c]
        if row_count == 2:
            other = before[c]
            value = jnp.where(
                row_at == 0,
                jnp.concatenate([mine, other], axis=0),
                jnp.concatenate([other, mine], axis=0),
            )
        elif row_count > 2:
            value = jnp.concatenate([before[c], mine, after[c]], axis=0)
        else:
            value = mine
        extended[c] = value
        whole.append(value)
    first = lax.axis_index("sub") == 0
    far = RIM - n_cols
    pack(whole, window, jnp.where(first, 0, far), outer)
    pack(whole, window, jnp.where(first, far, 0), inner)


def pad_rows(padded, c, window, value):
    blank = jnp.zeros((SUBLANES, LANES), f32)
    padded[c, :SUBLANES, :] = blank
    padded[c, SUBLANES + window :, :] = blank
    padded[c, SUBLANES : SUBLANES + window, :] = value


def channels(padded, columns, window):
    vel = [padded[c, SUBLANES : SUBLANES + window, :] for c in range(2)]
    for c in range(2):
        grad_x = roll(vel[c], -1) - roll(vel[c], 1)
        grad_y = (
            padded[c, SUBLANES + 1 : SUBLANES + 1 + window, :]
            - padded[c, SUBLANES - 1 : SUBLANES - 1 + window, :]
        )
        advect = vel[0] * grad_x + vel[1] * grad_y
        for at, value in ((c, vel[c]), (2 + c, advect)):
            high, low_part = split(value)
            columns[0, at * window : (at + 1) * window, :] = high
            columns[1, at * window : (at + 1) * window, :] = low_part


def across_x(columns, x_taps, window):
    wide = 2 * LANES
    high = x_taps[:, wide:]
    low_part = x_taps[:, :wide]
    both = x_taps[:, LANES : LANES + wide]
    main = dot(columns[0, : 2 * window, :], high)
    more = dot(columns[1, : 2 * window, :], high)
    rest = dot(columns[0, : 2 * window, :], low_part)
    flux = dot(columns[0, 2 * window :, :], both)
    flux_more = dot(columns[1, 2 * window :, :], both[:, LANES:])
    means = main[:, :LANES] + (more[:, :LANES] + rest[:, LANES:])
    slopes = main[:, LANES:] + (more[:, LANES:] + rest[:, :LANES])
    fluxes = flux[:, LANES:] + (flux_more + flux[:, :LANES])
    return means, slopes, fluxes


def inner_kernel(geom, extended, x_taps, partial, edges, padded, columns):
    n_rows, n_cols, depth, row_count, window = geom
    lane = iota((window, LANES), 1)
    for c in range(2):
        own = extended[c]
        pad_rows(padded, c, window, own)
        near = jnp.where(lane < RIM + 2, roll(own, RIM), roll(own, HALF - n_cols))
        edges[c] = near
    channels(padded, columns, window)
    for pair, value in enumerate(across_x(columns, x_taps[:LANES, :], window)):
        partial[pair] = value


def filter_kernel(
    geom,
    seam,
    beside,
    edges,
    partial,
    wet,
    turn,
    x_taps,
    y_taps,
    forcing,
    padded,
    columns,
    along,
    pools,
):
    n_rows, n_cols, depth, row_count, window = geom
    sub_at = lax.axis_index("sub")
    out_rows = up_to(n_rows, 2 * SUBLANES)
    turned = unpack(seam, beside, window, turn, sub_at)
    lane = iota((window, LANES), 1)
    own = (lane >= RIM) & (lane < HALF)
    for c in range(2):
        pad_rows(padded, c, window, jnp.where(own, edges[c], turned[c]))
    channels(padded, columns, window)
    for pair, value in enumerate(across_x(columns, x_taps[LANES:, :], window)):
        value = value + partial[pair]
        high, low_part = split(value)
        for c in range(2):
            at = slice(c * LANES, (c + 1) * LANES)
            along[0, pair, :, at] = high[c * window : (c + 1) * window]
            along[1, pair, :, at] = low_part[c * window : (c + 1) * window]

    main = dot(y_taps[...], along[0, 0])
    more = dot(y_taps[out_rows : 3 * out_rows, :], along[1, 0])
    slope_y = main[out_rows : 2 * out_rows] + (main[:out_rows] + more[:out_rows])
    mean = main[2 * out_rows : 3 * out_rows] + (main[3 * out_rows :] + more[out_rows:])

    def across(pair):
        main = dot(y_taps[2 * out_rows :, :], along[0, pair])
        more = dot(y_taps[2 * out_rows : 3 * out_rows, :], along[1, pair])
        return main[:out_rows] + (main[out_rows:] + more)

    slope_x = across(1)
    flux = across(2)
    mean_u = mean[:n_rows, :LANES]
    mean_v = mean[:n_rows, LANES:]
    mask = wet[...]
    coarse = n_rows // COARSE
    for c in range(2):
        at = slice(c * LANES, (c + 1) * LANES)
        pools[c] = mask * (
            flux[:n_rows, at] - (mean_u * slope_x[:n_rows, at] + mean_v * slope_y[:n_rows, at])
        )
    block = iota((LANES, LANES), 0) // COARSE == iota((LANES, LANES), 1)
    gather = jnp.where(block, deriv_scale / (COARSE * COARSE), 0.0).astype(bf16)
    for c in range(2):
        rows = [pools[c, pl.ds(k, coarse, stride=COARSE), :] for k in range(COARSE)]
        high, low_part = split((rows[0] + rows[1]) + (rows[2] + rows[3]))
        value = dot(high, gather) + dot(low_part, gather)
        forcing[:, c, :] = value[:, : n_cols // COARSE]


EDGE = 4


def np_split(value):
    high = value.astype(bf16)
    return high, (value - high.astype(np.float64)).astype(bf16)


def np_gaussian(distance):
    inside = np.abs(distance) <= R
    return np.where(inside, np.exp(-0.5 * (distance / R) ** 2) / taps_sum(), 0.0)


def x_constant(n_cols):
    lane = np.arange(2 * LANES)[:, None]
    target = np.arange(LANES)[None, :]
    rim = lane - LANES
    column = np.where(
        lane < LANES, lane, np.where(rim < HALF - 1, rim - RIM, rim - HALF + n_cols)
    )
    inside = (
        ((lane >= 1) & (lane < n_cols - 1))
        | ((rim >= 0) & (rim <= RIM))
        | ((rim >= HALF - 1) & (rim < HALF + RIM))
    )
    inside = inside & (target < n_cols)
    away = column - target
    value = np_split(np.where(inside, np_gaussian(away), 0.0))
    slope = np_split(np.where(inside, np_gaussian(away - 1) - np_gaussian(away + 1), 0.0))
    return np.concatenate([slope[1], value[1], value[0], slope[0]], axis=1)


def y_constant(target, source, used, first_row, last_row):
    def step(by):
        at = source + by
        inside = used & (at >= first_row) & (at < last_row)
        return np.where(inside[None, :], np_gaussian(at[None, :] - target[:, None]), 0.0)

    value = np_split(step(0))
    slope = np_split(step(-1) - step(1))
    pad = ((0, up_to(target.shape[0], 2 * SUBLANES) - target.shape[0]), (0, 0))
    return np.concatenate(
        [np.pad(taps, pad) for taps in (slope[1], slope[0], value[0], value[1])], axis=0
    )


def y_constants(n_rows, depth, near):
    own, tail = [], []
    for row_at in range(2):
        bounds = (-row_at * n_rows, (2 - row_at) * n_rows)
        source = np.arange(up_to(n_rows, 2 * SUBLANES))
        late = source >= n_rows - EDGE if row_at == 0 else source < EDGE
        used = ~late & (source < n_rows)
        own.append(y_constant(np.arange(n_rows), source, used, *bounds))
        source = np.arange(near + depth)
        source = source + n_rows - near if row_at == 0 else source - depth
        late = source >= n_rows - EDGE if row_at == 0 else source < EDGE
        target = np.arange(depth) + (n_rows - depth if row_at == 0 else 0)
        tail.append(y_constant(target, source, late, *bounds))
    return np.stack(own), np.stack(tail)


def start_all(pairs, sems):
    copies = [pltpu.make_async_copy(a, b, sems.at[i]) for i, (a, b) in enumerate(pairs)]
    for copy in copies:
        copy.start()
    return copies


def pack(whole, rows, base, to):
    size = packed_rows(rows)
    lane = iota((size, LANES), 1)
    groups = [[] for _ in range(GROUPS)]
    for c, row, group, _, count in pieces(rows):
        groups[group].append(whole[c][row : row + count])
    spare = GROUPS * size - 2 * rows
    if spare:
        groups[-1].append(jnp.zeros((spare, LANES), f32))
    groups = [jnp.concatenate(group, axis=0) for group in groups]
    value = roll(groups[-1], base + (GROUPS - 1) * GROUP)
    for g in reversed(range(GROUPS - 1)):
        value = jnp.where(lane < (g + 1) * GROUP, roll(groups[g], base + g * GROUP), value)
    to[...] = value


def unpack(seam, beside, rows, turn, sub_at):
    near = jnp.where(sub_at == 0, 0, HALF)
    parts = [[], []]
    for c, _, group, row, count in pieces(rows):
        lane = iota((count, LANES), 1)
        parts[c].append(
            jnp.where(
                seam_side(lane, sub_at),
                roll(seam[row : row + count, :], near - group * GROUP),
                roll(beside[row : row + count, :], HALF - near - group * GROUP),
            )
        )
    east, north = (jnp.concatenate(part, axis=0) for part in parts)
    cosine = turn[0:1, :]
    sine = turn[1:2, :]
    return cosine * east - sine * north, sine * east + cosine * north


def open_kernel(
    geom,
    velocity,
    wet_bits,
    east_face,
    seam_turn,
    field,
    outer,
    inner,
    wet,
    turn,
    order,
    vel,
    packed,
    faces,
    turns,
    sems,
):
    n_rows, n_cols, depth, _ = geom
    copies = start_all(
        ((east_face, faces), (seam_turn, turns), (wet_bits, packed), (velocity, vel)), sems
    )
    for copy in copies[:2]:
        copy.wait()
    order[0] = seam_order(faces)
    sub_at = lax.axis_index("sub")
    write_turn(faces, turns, turn)
    copies[2].wait()
    at = iota((n_rows, n_cols), 0)
    word = jnp.broadcast_to(packed[0:1, :], (n_rows, n_cols))
    shift = at
    for j in range(1, n_rows // BITS):
        line = jnp.broadcast_to(packed[j : j + 1, :], (n_rows, n_cols))
        later = at >= j * BITS
        word = jnp.where(later, line, word)
        shift = jnp.where(later, at - j * BITS, shift)
    mask = (jnp.right_shift(word, shift) & 1).astype(f32)
    margin = jnp.zeros((n_rows, LANES - n_cols), f32)
    wet[:, :n_cols] = mask
    wet[:, n_cols:] = margin
    copies[3].wait()
    whole = []
    for c in range(2):
        value = jnp.concatenate([vel[c] * mask, margin], axis=1)
        field[c] = value
        whole.append(value)
    far = RIM - n_cols
    pack(whole, n_rows, jnp.where(sub_at == 0, 0, far), outer)
    pack(whole, n_rows, jnp.where(sub_at == 0, far, 0), inner)


def corner_pieces(depth):
    size = corner_rows(depth)
    cuts = sorted({*range(0, 5 * depth, depth), *(size * g for g in range(1, GROUPS))})
    return [
        (a // (2 * depth), a // depth % 2, a % depth, a // size, a % size, b - a)
        for a, b in zip(cuts, cuts[1:])
    ]


def corner_rows(depth):
    return up_to(-(-4 * depth // GROUPS), SUBLANES)


def pack_corners(rims, depth):
    size = corner_rows(depth)
    groups = [[] for _ in range(GROUPS)]
    for c, side, row, group, _, count in corner_pieces(depth):
        groups[group].append(roll(rims[c][row : row + count], group * GROUP - side * (HALF - 2)))
    spare = GROUPS * size - 4 * depth
    if spare:
        groups[-1].append(jnp.zeros((spare, LANES), f32))
    groups = [jnp.concatenate(group, axis=0) for group in groups]
    lane = iota((size, LANES), 1)
    value = groups[-1]
    for g in reversed(range(GROUPS - 1)):
        value = jnp.where(lane < (g + 1) * GROUP, groups[g], value)
    return value


def unpack_corners(value, depth):
    parts = {}
    for c, side, _, group, row, count in corner_pieces(depth):
        piece = roll(value[row : row + count, :], side * (HALF - 2) - group * GROUP)
        parts.setdefault((c, side), []).append(piece)
    lane = iota((depth, LANES), 1)
    sides = {key: jnp.concatenate(part, axis=0) for key, part in parts.items()}
    return [jnp.where(lane < RIM + 2, sides[c, 0], sides[c, 1]) for c in range(2)]


def rims_kernel(geom, seam, beside, field, turn, rims, edge):
    n_rows, n_cols, depth, _ = geom
    turned = unpack(seam, beside, n_rows, turn, lax.axis_index("sub"))
    row_at = lax.axis_index("row")
    lane = iota((n_rows, LANES), 1)
    own = (lane >= RIM) & (lane < HALF)
    ends = []
    for c in range(2):
        mine = field[c]
        near = jnp.where(lane < RIM + 2, roll(mine, RIM), roll(mine, HALF - n_cols))
        value = jnp.where(own, near, turned[c])
        rims[c] = value
        edge[c * depth : (c + 1) * depth, :] = facing(row_at, mine, depth)
        ends.append(facing(row_at, value, depth))
    edge[2 * depth :, :] = pack_corners(ends, depth)


def facing(row_at, value, depth):
    return jnp.where(row_at == 0, value[value.shape[0] - depth :], value[:depth])


def edge_rows(row_at, own, other, near):
    n_rows = own.shape[0]
    return jnp.where(
        row_at == 0,
        jnp.concatenate([own[n_rows - near :], other], axis=0),
        jnp.concatenate([other, own[:near]], axis=0),
    )


def keep_along(along, pair, value, rows):
    high, low_part = split(value)
    for c in range(2):
        at = slice(c * LANES, (c + 1) * LANES)
        along[0, pair, :, at] = high[c * rows : (c + 1) * rows]
        along[1, pair, :, at] = low_part[c * rows : (c + 1) * rows]


def across_y(y_taps, along, size):
    main = dot(y_taps[...], along[0, 0])
    more = dot(y_taps[size : 3 * size, :], along[1, 0])
    slope_y = main[size : 2 * size] + (main[:size] + more[:size])
    mean = main[2 * size : 3 * size] + (main[3 * size :] + more[size:])

    def plain(pair):
        main = dot(y_taps[2 * size :, :], along[0, pair])
        more = dot(y_taps[2 * size : 3 * size, :], along[1, pair])
        return main[:size] + (main[size:] + more)

    return slope_y, mean, plain(1), plain(2)


def pool(smooth, mask, pools):
    slope_y, mean, slope_x, flux = smooth
    count = mask.shape[0]
    mean_u = mean[:, :LANES]
    mean_v = mean[:, LANES:]
    block = iota((LANES, LANES), 0) // COARSE == iota((LANES, LANES), 1)
    gather = jnp.where(block, deriv_scale / (COARSE * COARSE), 0.0).astype(bf16)
    out = []
    for c in range(2):
        at = slice(c * LANES, (c + 1) * LANES)
        pools[c] = mask * (flux[:, at] - (mean_u * slope_x[:, at] + mean_v * slope_y[:, at]))
        rows = [
            pools[c, pl.ds(k, count // COARSE, stride=COARSE), :] for k in range(COARSE)
        ]
        high, low_part = split((rows[0] + rows[1]) + (rows[2] + rows[3]))
        out.append(dot(high, gather) + dot(low_part, gather))
    return out


def own_kernel(
    geom,
    field,
    rims,
    wet,
    x_source,
    y_source,
    tail_source,
    part,
    tail,
    tail_wet,
    x_taps,
    tail_taps,
    padded,
    columns,
    along,
    pools,
    y_taps,
    sems,
):
    n_rows, n_cols, depth, _ = geom
    row_at = lax.axis_index("row")
    copies = start_all(
        (
            (x_source, x_taps),
            (y_source.at[row_at], y_taps),
            (tail_source.at[row_at], tail_taps),
        ),
        sems,
    )
    size = up_to(n_rows, 2 * SUBLANES)
    blank = jnp.zeros((size - n_rows, LANES), f32)
    for half, source in enumerate((field, rims)):
        for c in range(2):
            value = source[c]
            if size > n_rows:
                value = jnp.concatenate([value, blank], axis=0)
            pad_rows(padded.at[half], c, size, value)
        channels(
            padded.at[half], columns.at[:, :, half * LANES : (half + 1) * LANES], size
        )
    for copy in copies:
        copy.wait()
    for pair, value in enumerate(across_x(columns, x_taps, size)):
        keep_along(along, pair, value, size)
    smooth = [value[:n_rows] for value in across_y(y_taps, along, size)]
    mask = wet[...]
    for i, value in enumerate(smooth):
        tail[i] = facing(row_at, value, depth)
    tail_wet[...] = facing(row_at, mask, depth)
    for c, value in enumerate(pool(smooth, mask, pools)):
        part[:, c, :] = value[:, : n_cols // COARSE]


def close_kernel(
    geom,
    edge,
    field,
    rims,
    part,
    tail,
    tail_wet,
    x_taps,
    tail_taps,
    forcing,
    padded,
    columns,
    along,
    pools,
):
    n_rows, n_cols, depth, near = geom
    row_at = lax.axis_index("row")
    size = near + depth
    corners = unpack_corners(edge[2 * depth :, :], depth)
    others = ([edge[c * depth : (c + 1) * depth, :] for c in range(2)], corners)
    for half, source in enumerate((field, rims)):
        for c in range(2):
            value = edge_rows(row_at, source[c], others[half][c], near)
            pad_rows(padded.at[half], c, size, value)
        channels(
            padded.at[half], columns.at[:, :, half * LANES : (half + 1) * LANES], size
        )
    for pair, value in enumerate(across_x(columns, x_taps, size)):
        keep_along(along, pair, value, size)
    smooth = across_y(tail_taps, along, up_to(depth, 2 * SUBLANES))
    smooth = [value[:depth] + tail[i] for i, value in enumerate(smooth)]
    forcing[...] = part[...]
    start = jnp.where(row_at == 0, (n_rows - depth) // COARSE, 0)
    for c, value in enumerate(pool(smooth, tail_wet[...], pools)):
        forcing[pl.ds(start, depth // COARSE), c, :] = value[:, : n_cols // COARSE]


VMEM_SPEC = pl.BlockSpec(memory_space=pltpu.VMEM)
SMEM_SPEC = pl.BlockSpec(memory_space=pltpu.SMEM)
HBM_SPEC = pl.BlockSpec(memory_space=pltpu.HBM)


def choose(index, branches, *operands):
    closed = jax.make_jaxpr(lambda i, *rest: lax.switch(i, branches, *rest))(index, *operands)
    values = dict(zip(closed.jaxpr.constvars, closed.consts))
    values.update(zip(closed.jaxpr.invars, jax.tree.leaves((index, *operands))))

    def read(atom):
        return atom.val if hasattr(atom, "val") else values[atom]

    for eqn in closed.jaxpr.eqns:
        taken = [read(atom) for atom in eqn.invars]
        if eqn.primitive is lax.clamp_p:
            given = taken[1]
        else:
            given = eqn.primitive.bind(*taken, **eqn.params)
        if not eqn.primitive.multiple_results:
            given = [given]
        values.update(zip(eqn.outvars, given))
    return [read(atom) for atom in closed.jaxpr.outvars]


def seam_pairs(order, subs):
    pairs = []
    for west, east in enumerate(order):
        pairs += [(west * subs + subs - 1, east * subs), (east * subs, west * subs + subs - 1)]
    return pairs


def beside_pairs(subs):
    return [(i, subs - 1 - i) for i in range(subs)]


def exchange(order, east_face, outer, inner, finish):
    faces = east_face.shape[0]
    subs = lax.axis_size("sub")
    beside = beside_pairs(subs)

    def swap(order, outer, inner):
        seam = lax.ppermute(outer, ("tile", "sub"), seam_pairs(order, subs))
        return finish(seam, lax.ppermute(inner, "sub", beside))

    if faces <= SWITCHED_FACES:
        orders = itertools.permutations(range(faces))
        branches = [functools.partial(swap, order) for order in orders]
        return lax.switch(order[0], branches, outer, inner)
    tile_at = lax.axis_index("tile")
    sub_at = lax.axis_index("sub")
    west = jnp.sum(jnp.where(east_face == tile_at, jnp.arange(faces, dtype=jnp.int32), 0))
    east = lax.dynamic_index_in_dim(east_face, tile_at, 0, keepdims=False)
    gathered = lax.all_gather(lax.ppermute(outer, "sub", beside), "tile")
    partner = jnp.where(sub_at == 0, west, east)
    seam = lax.dynamic_index_in_dim(gathered, partner, 0, keepdims=False)
    return finish(seam, lax.ppermute(inner, "sub", beside))


def in_hbm(value):
    return pltpu.with_memory_space_constraint(value, pltpu.HBM)


def paired(velocity, wet_bits, east_face, seam_turn):
    _, n_rows, n_cols = velocity.shape
    depth = up_to(RIM, SUBLANES)
    near = up_to(depth + SUBLANES, 2 * SUBLANES) + 2 * SUBLANES - depth
    geom = (n_rows, n_cols, depth, near)
    size = up_to(n_rows, 2 * SUBLANES)
    end = near + depth
    wide = 2 * LANES
    coarse = n_rows // COARSE
    params = pltpu.CompilerParams(vmem_limit_bytes=16 << 20)
    shape = jax.ShapeDtypeStruct
    kernel = lambda body, name, **rest: pl.pallas_call(
        functools.partial(body, geom), name=name, compiler_params=params, **rest
    )
    packed = shape((packed_rows(n_rows), LANES), f32)
    field, outer, inner, wet, turn, order = kernel(
        open_kernel,
        "open",
        out_shape=(
            shape((2, n_rows, LANES), f32),
            packed,
            packed,
            shape((n_rows, LANES), f32),
            shape((SUBLANES, LANES), f32),
            pltpu.SMEM((1,), jnp.int32),
        ),
        in_specs=[HBM_SPEC] * 4,
        out_specs=(VMEM_SPEC,) * 5 + (SMEM_SPEC,),
        scratch_shapes=[
            pltpu.VMEM(velocity.shape, f32),
            pltpu.VMEM(wet_bits.shape, jnp.int32),
            pltpu.SMEM(east_face.shape, jnp.int32),
            pltpu.SMEM(seam_turn.shape, jnp.int32),
            pltpu.SemaphoreType.DMA((4,)),
        ],
    )(in_hbm(velocity), in_hbm(wet_bits), in_hbm(east_face), in_hbm(seam_turn))
    subs = lax.axis_size("sub")

    def swap(order, outer, inner, field, turn):
        seam = lax.ppermute(outer, ("tile", "sub"), seam_pairs(order, subs))
        beside = lax.ppermute(inner, "sub", beside_pairs(subs))
        return kernel(
            rims_kernel,
            "rims",
            out_shape=(
                shape((2, n_rows, LANES), f32),
                shape((2 * depth + corner_rows(depth), LANES), f32),
            ),
            in_specs=[VMEM_SPEC] * 4,
            out_specs=(VMEM_SPEC,) * 2,
        )(seam, beside, field, turn)

    orders = itertools.permutations(range(east_face.shape[0]))
    branches = [functools.partial(swap, order) for order in orders]
    rims, edge = choose(order[0], branches, outer, inner, field, turn)
    edge = lax.ppermute(edge, "row", [(0, 1), (1, 0)])
    own_taps, tail_taps = y_constants(n_rows, depth, near)
    x_taps = x_constant(n_cols)
    part, tail, tail_wet, x_taps, tail_taps = kernel(
        own_kernel,
        "own",
        out_shape=(
            shape((coarse, 2, n_cols // COARSE), f32),
            shape((4, depth, wide), f32),
            shape((depth, LANES), f32),
            shape(x_taps.shape, bf16),
            shape(tail_taps.shape[1:], bf16),
        ),
        in_specs=[VMEM_SPEC] * 3 + [HBM_SPEC] * 3,
        out_specs=(VMEM_SPEC,) * 5,
        scratch_shapes=[
            pltpu.VMEM((2, 2, size + 2 * SUBLANES, LANES), f32),
            pltpu.VMEM((2, 4 * size, wide), bf16),
            pltpu.VMEM((2, 3, size, wide), bf16),
            pltpu.VMEM((2, n_rows, LANES), f32),
            pltpu.VMEM(own_taps.shape[1:], bf16),
            pltpu.SemaphoreType.DMA((3,)),
        ],
        cost_estimate=pl.CostEstimate(
            flops=1 << 30, bytes_accessed=1 << 22, transcendentals=0
        ),
    )(field, rims, wet, *(in_hbm(jnp.asarray(taps)) for taps in (x_taps, own_taps, tail_taps)))
    forcing = kernel(
        close_kernel,
        "close",
        out_shape=shape((coarse, 2, n_cols // COARSE), f32),
        in_specs=[VMEM_SPEC] * 8,
        out_specs=VMEM_SPEC,
        scratch_shapes=[
            pltpu.VMEM((2, 2, end + 2 * SUBLANES, LANES), f32),
            pltpu.VMEM((2, 4 * end, wide), bf16),
            pltpu.VMEM((2, 3, end, wide), bf16),
            pltpu.VMEM((2, depth, LANES), f32),
        ],
    )(edge, field, rims, part, tail, tail_wet, x_taps, tail_taps)
    return jnp.transpose(forcing, (1, 0, 2))


def on_device(velocity, wet_bits, east_face, seam_turn):
    _, n_rows, n_cols = velocity.shape
    row_count = lax.axis_size("row")
    if row_count == 2 and east_face.shape[0] <= SWITCHED_FACES:
        return paired(velocity, wet_bits, east_face, seam_turn)
    depth = up_to(RIM, SUBLANES)
    sides = min(row_count - 1, 2)
    window = n_rows + sides * depth
    geom = (n_rows, n_cols, depth, row_count, window)
    sent = depth * max(sides, 1)
    wide = 2 * LANES
    out_rows = up_to(n_rows, 2 * SUBLANES)
    params = pltpu.CompilerParams(vmem_limit_bytes=16 << 20)
    shape = jax.ShapeDtypeStruct
    field, rows, wet = pl.pallas_call(
        functools.partial(mask_kernel, geom),
        out_shape=(
            shape((2, n_rows, LANES), f32),
            shape((2, sent, LANES), f32),
            shape((n_rows, LANES), f32),
        ),
        in_specs=[HBM_SPEC] * 2,
        out_specs=(VMEM_SPEC,) * 3,
        scratch_shapes=[
            pltpu.VMEM(velocity.shape, f32),
            pltpu.VMEM(wet_bits.shape, jnp.int32),
            pltpu.SemaphoreType.DMA((2,)),
        ],
        compiler_params=params,
        name="mask",
    )(
        pltpu.with_memory_space_constraint(velocity, pltpu.HBM),
        pltpu.with_memory_space_constraint(wet_bits, pltpu.HBM),
    )
    order, turn, x_taps, y_taps = pl.pallas_call(
        functools.partial(prepare_kernel, geom),
        out_shape=(
            shape((1,), jnp.int32),
            shape((SUBLANES, LANES), f32),
            shape((wide, 2 * wide), bf16),
            shape((4 * out_rows, window), bf16),
        ),
        in_specs=[HBM_SPEC] * 2,
        out_specs=(SMEM_SPEC,) + (VMEM_SPEC,) * 3,
        scratch_shapes=[
            pltpu.SMEM(east_face.shape, jnp.int32),
            pltpu.SMEM(seam_turn.shape, jnp.int32),
            pltpu.SemaphoreType.DMA((2,)),
        ],
        compiler_params=params,
        name="prepare",
    )(
        pltpu.with_memory_space_constraint(east_face, pltpu.HBM),
        pltpu.with_memory_space_constraint(seam_turn, pltpu.HBM),
    )
    if row_count == 2:
        before = lax.ppermute(rows, "row", [(0, 1), (1, 0)])
        after = before
    elif row_count > 2:
        up = [(i, i + 1) for i in range(row_count - 1)]
        before = lax.ppermute(rows[:, depth:], "row", up)
        after = lax.ppermute(rows[:, :depth], "row", [(j, i) for i, j in up])
    else:
        before = after = rows
    extended, outer, inner = pl.pallas_call(
        functools.partial(extend_kernel, geom),
        out_shape=(
            shape((2, window, LANES), f32),
            shape((packed_rows(window), LANES), f32),
            shape((packed_rows(window), LANES), f32),
        ),
        in_specs=[VMEM_SPEC] * 3,
        out_specs=(VMEM_SPEC,) * 3,
        compiler_params=params,
        name="extend",
    )(field, before, after)

    def finish(seam, beside):
        partial, edges = pl.pallas_call(
            functools.partial(inner_kernel, geom),
            out_shape=(
                shape((3, 2 * window, LANES), f32),
                shape((2, window, LANES), f32),
            ),
            in_specs=[VMEM_SPEC] * 2,
            out_specs=(VMEM_SPEC,) * 2,
            scratch_shapes=[
                pltpu.VMEM((2, window + 2 * SUBLANES, LANES), f32),
                pltpu.VMEM((2, 4 * window, LANES), bf16),
            ],
            compiler_params=params,
            name="inner",
        )(extended, x_taps)
        return pl.pallas_call(
            functools.partial(filter_kernel, geom),
            out_shape=shape((n_rows // COARSE, 2, n_cols // COARSE), f32),
            in_specs=[VMEM_SPEC] * 8,
            out_specs=VMEM_SPEC,
            scratch_shapes=[
                pltpu.VMEM((2, window + 2 * SUBLANES, LANES), f32),
                pltpu.VMEM((2, 4 * window, LANES), bf16),
                pltpu.VMEM((2, 3, window, wide), bf16),
                pltpu.VMEM((2, n_rows, LANES), f32),
            ],
            compiler_params=params,
            name="filter",
        )(seam, beside, edges, partial, wet, turn, x_taps, y_taps)

    forcing = exchange(order, east_face, outer, inner, finish)
    return jnp.transpose(forcing, (1, 0, 2))


def solution(mesh):
    placed = (
        P(None, ("grp", "row"), ("tile", "sub")),
        P(("grp", "row"), ("tile", "sub")),
        P(),
        P(),
    )
    return jax.shard_map(
        on_device,
        mesh=mesh,
        in_specs=placed,
        out_specs=P(None, ("grp", "row"), ("tile", "sub")),
        check_vma=False,
    )
```

```python
import functools
import itertools

import jax
import jax.numpy as jnp
import numpy as np
from jax import lax
from jax.experimental import pallas as pl
from jax.experimental.pallas import tpu as pltpu
from jax.sharding import PartitionSpec as P

R = 32
RIM = R + 1
BITS = 30
COARSE = 4
LANES = 128
HALF = LANES // 2
GROUPS = 3
GROUP = 40
SUBLANES = 8
SWITCHED_FACES = 4

deriv_scale = 8.0

f32 = jnp.float32
bf16 = jnp.bfloat16


def up_to(value, step):
    return -(-value // step) * step


def iota(shape, dim):
    return lax.broadcasted_iota(jnp.int32, shape, dim)


def split(value):
    high = value.astype(bf16)
    return high, (value - high.astype(f32)).astype(bf16)


def dot(left, right):
    return jnp.dot(left, right, preferred_element_type=f32)


def taps_sum():
    taps = np.arange(-R, R + 1, dtype=np.float64)
    return float(np.sum(np.exp(-0.5 * (taps / R) ** 2)))


def gaussian(distance, inside):
    inside = inside & (distance >= -R) & (distance <= R)
    scaled = distance.astype(f32) * (1.0 / R)
    return jnp.where(inside, jnp.exp(-0.5 * scaled * scaled) * (1.0 / taps_sum()), 0.0)


def roll(value, shift):
    return pltpu.roll(value, shift % LANES, axis=1)


def fetch(pairs, sems):
    copies = [pltpu.make_async_copy(a, b, sems.at[i]) for i, (a, b) in enumerate(pairs)]
    for copy in copies:
        copy.start()
    for copy in copies:
        copy.wait()


def mask_kernel(geom, velocity, wet_bits, field, rows, wet, vel, packed, sems):
    n_rows, n_cols, depth, row_count, _ = geom
    fetch(((velocity, vel), (wet_bits, packed)), sems)
    at = iota((n_rows, n_cols), 0)
    word = jnp.broadcast_to(packed[0:1, :], (n_rows, n_cols))
    shift = at
    for j in range(1, n_rows // BITS):
        line = jnp.broadcast_to(packed[j : j + 1, :], (n_rows, n_cols))
        later = at >= j * BITS
        word = jnp.where(later, line, word)
        shift = jnp.where(later, at - j * BITS, shift)
    mask = (jnp.right_shift(word, shift) & 1).astype(f32)
    margin = jnp.zeros((n_rows, LANES - n_cols), f32)
    wet[:, :n_cols] = mask
    wet[:, n_cols:] = margin
    row_at = lax.axis_index("row")
    for c in range(2):
        value = jnp.concatenate([vel[c] * mask, margin], axis=1)
        field[c] = value
        if row_count == 2:
            rows[c] = jnp.where(row_at == 0, value[n_rows - depth :], value[:depth])
        elif row_count > 2:
            rows[c, :depth] = value[:depth]
            rows[c, depth:] = value[n_rows - depth :]


def seam_order(faces):
    count = faces.shape[0]
    order = jnp.int32(0)
    for i in range(count):
        smaller = jnp.int32(0)
        for j in range(i + 1, count):
            smaller = smaller + jnp.where(faces[j] < faces[i], 1, 0)
        order = order * (count - i) + smaller
    return order


def prepare_kernel(
    geom, east_face, seam_turn, order, turn, x_taps, y_taps, faces, turns, sems
):
    n_rows, n_cols, depth, row_count, window = geom
    copies = [
        pltpu.make_async_copy(east_face, faces, sems.at[0]),
        pltpu.make_async_copy(seam_turn, turns, sems.at[1]),
    ]
    for copy in copies:
        copy.start()
    row_at = lax.axis_index("row")
    lane = iota((2 * LANES, LANES), 0)
    target = iota((2 * LANES, LANES), 1)
    rim = lane - LANES
    column = jnp.where(
        lane < LANES, lane, jnp.where(rim < HALF - 1, rim - RIM, rim - HALF + n_cols)
    )
    inside = (
        ((lane >= 1) & (lane < n_cols - 1))
        | ((rim >= 0) & (rim <= RIM))
        | ((rim >= HALF - 1) & (rim < HALF + RIM))
    )
    inside = inside & (target < n_cols)
    away = column - target
    value = split(gaussian(away, inside))
    slope = split(gaussian(away - 1, inside) - gaussian(away + 1, inside))
    for i, taps in enumerate((slope[1], value[1], value[0], slope[0])):
        x_taps[:, i * LANES : (i + 1) * LANES] = taps
    out_rows = up_to(n_rows, 2 * SUBLANES)
    source = iota((out_rows, window), 1)
    target = iota((out_rows, window), 0)
    start = row_start(geom, row_at)
    world = source - start + row_at * n_rows
    last = row_count * n_rows

    def taps_at(step):
        at = world + step
        inside = (at >= 0) & (at < last) & (target < n_rows)
        return gaussian(source + step - start - target, inside)

    value = split(taps_at(0))
    slope = split(taps_at(-1) - taps_at(1))
    for i, taps in enumerate((slope[1], slope[0], value[0], value[1])):
        y_taps[i * out_rows : (i + 1) * out_rows, :] = taps
    for copy in copies:
        copy.wait()
    order[0] = seam_order(faces) if faces.shape[0] <= SWITCHED_FACES else jnp.int32(0)
    write_turn(faces, turns, turn)


def write_turn(faces, turns, turn):
    tile_at = lax.axis_index("tile")
    back = jnp.int32(0)
    for w in range(faces.shape[0]):
        back = jnp.where(faces[w] == tile_at, turns[w], back)
    sub_at = lax.axis_index("sub")
    quarter = jnp.where(sub_at == 0, (4 - back) % 4, turns[tile_at])
    cosine = jnp.where(quarter == 0, 1.0, jnp.where(quarter == 2, -1.0, 0.0)).astype(f32)
    sine = jnp.where(quarter == 1, 1.0, jnp.where(quarter == 3, -1.0, 0.0)).astype(f32)
    row = iota((SUBLANES, LANES), 0)
    lane = iota((SUBLANES, LANES), 1)
    seam_lane = seam_side(lane, sub_at)
    turn[...] = jnp.where(
        row == 0, jnp.where(seam_lane, cosine, 1.0), jnp.where(seam_lane, sine, 0.0)
    )


def seam_side(lane, sub_at):
    edge = jnp.where(sub_at == 0, RIM, LANES)
    start = jnp.where(sub_at == 0, 0, HALF)
    return (lane >= start) & (lane < edge)


def packed_rows(window):
    return up_to(-(-2 * window // GROUPS), SUBLANES)


def pieces(window):
    size = packed_rows(window)
    cuts = sorted({0, window, 2 * window, *(size * g for g in range(1, GROUPS))})
    return [
        (a // window, a % window, a // size, a % size, b - a) for a, b in zip(cuts, cuts[1:])
    ]


def row_start(geom, row_at):
    _, _, depth, row_count, _ = geom
    if row_count == 2:
        return jnp.where(row_at == 0, 0, depth)
    return jnp.int32(depth if row_count > 2 else 0)


def extend_kernel(geom, field, before, after, extended, outer, inner):
    n_rows, n_cols, depth, row_count, window = geom
    row_at = lax.axis_index("row")
    whole = []
    for c in range(2):
        mine = field[c]
        if row_count == 2:
            other = before[c]
            value = jnp.where(
                row_at == 0,
                jnp.concatenate([mine, other], axis=0),
                jnp.concatenate([other, mine], axis=0),
            )
        elif row_count > 2:
            value = jnp.concatenate([before[c], mine, after[c]], axis=0)
        else:
            value = mine
        extended[c] = value
        whole.append(value)
    first = lax.axis_index("sub") == 0
    far = RIM - n_cols
    pack(whole, window, jnp.where(first, 0, far), outer)
    pack(whole, window, jnp.where(first, far, 0), inner)


def pad_rows(padded, c, window, value):
    blank = jnp.zeros((SUBLANES, LANES), f32)
    padded[c, :SUBLANES, :] = blank
    padded[c, SUBLANES + window :, :] = blank
    padded[c, SUBLANES : SUBLANES + window, :] = value


def channels(padded, columns, window):
    vel = [padded[c, SUBLANES : SUBLANES + window, :] for c in range(2)]
    for c in range(2):
        grad_x = roll(vel[c], -1) - roll(vel[c], 1)
        grad_y = (
            padded[c, SUBLANES + 1 : SUBLANES + 1 + window, :]
            - padded[c, SUBLANES - 1 : SUBLANES - 1 + window, :]
        )
        advect = vel[0] * grad_x + vel[1] * grad_y
        for at, value in ((c, vel[c]), (2 + c, advect)):
            high, low_part = split(value)
            columns[0, at * window : (at + 1) * window, :] = high
            columns[1, at * window : (at + 1) * window, :] = low_part


def across_x(columns, x_taps, window):
    wide = 2 * LANES
    high = x_taps[:, wide:]
    low_part = x_taps[:, :wide]
    both = x_taps[:, LANES : LANES + wide]
    main = dot(columns[0, : 2 * window, :], high)
    more = dot(columns[1, : 2 * window, :], high)
    rest = dot(columns[0, : 2 * window, :], low_part)
    flux = dot(columns[0, 2 * window :, :], both)
    flux_more = dot(columns[1, 2 * window :, :], both[:, LANES:])
    means = main[:, :LANES] + (more[:, :LANES] + rest[:, LANES:])
    slopes = main[:, LANES:] + (more[:, LANES:] + rest[:, :LANES])
    fluxes = flux[:, LANES:] + (flux_more + flux[:, :LANES])
    return means, slopes, fluxes


def inner_kernel(geom, extended, x_taps, partial, edges, padded, columns):
    n_rows, n_cols, depth, row_count, window = geom
    lane = iota((window, LANES), 1)
    for c in range(2):
        own = extended[c]
        pad_rows(padded, c, window, own)
        near = jnp.where(lane < RIM + 2, roll(own, RIM), roll(own, HALF - n_cols))
        edges[c] = near
    channels(padded, columns, window)
    for pair, value in enumerate(across_x(columns, x_taps[:LANES, :], window)):
        partial[pair] = value


def filter_kernel(
    geom,
    seam,
    beside,
    edges,
    partial,
    wet,
    turn,
    x_taps,
    y_taps,
    forcing,
    padded,
    columns,
    along,
    pools,
):
    n_rows, n_cols, depth, row_count, window = geom
    sub_at = lax.axis_index("sub")
    out_rows = up_to(n_rows, 2 * SUBLANES)
    turned = unpack(seam, beside, window, turn, sub_at)
    lane = iota((window, LANES), 1)
    own = (lane >= RIM) & (lane < HALF)
    for c in range(2):
        pad_rows(padded, c, window, jnp.where(own, edges[c], turned[c]))
    channels(padded, columns, window)
    for pair, value in enumerate(across_x(columns, x_taps[LANES:, :], window)):
        value = value + partial[pair]
        high, low_part = split(value)
        for c in range(2):
            at = slice(c * LANES, (c + 1) * LANES)
            along[0, pair, :, at] = high[c * window : (c + 1) * window]
            along[1, pair, :, at] = low_part[c * window : (c + 1) * window]

    main = dot(y_taps[...], along[0, 0])
    more = dot(y_taps[out_rows : 3 * out_rows, :], along[1, 0])
    slope_y = main[out_rows : 2 * out_rows] + (main[:out_rows] + more[:out_rows])
    mean = main[2 * out_rows : 3 * out_rows] + (main[3 * out_rows :] + more[out_rows:])

    def across(pair):
        main = dot(y_taps[2 * out_rows :, :], along[0, pair])
        more = dot(y_taps[2 * out_rows : 3 * out_rows, :], along[1, pair])
        return main[:out_rows] + (main[out_rows:] + more)

    slope_x = across(1)
    flux = across(2)
    mean_u = mean[:n_rows, :LANES]
    mean_v = mean[:n_rows, LANES:]
    mask = wet[...]
    coarse = n_rows // COARSE
    for c in range(2):
        at = slice(c * LANES, (c + 1) * LANES)
        pools[c] = mask * (
            flux[:n_rows, at] - (mean_u * slope_x[:n_rows, at] + mean_v * slope_y[:n_rows, at])
        )
    block = iota((LANES, LANES), 0) // COARSE == iota((LANES, LANES), 1)
    gather = jnp.where(block, deriv_scale / (COARSE * COARSE), 0.0).astype(bf16)
    for c in range(2):
        rows = [pools[c, pl.ds(k, coarse, stride=COARSE), :] for k in range(COARSE)]
        high, low_part = split((rows[0] + rows[1]) + (rows[2] + rows[3]))
        value = dot(high, gather) + dot(low_part, gather)
        forcing[:, c, :] = value[:, : n_cols // COARSE]


EDGE = 4


def np_split(value):
    high = value.astype(bf16)
    return high, (value - high.astype(np.float64)).astype(bf16)


def np_gaussian(distance):
    inside = np.abs(distance) <= R
    return np.where(inside, np.exp(-0.5 * (distance / R) ** 2) / taps_sum(), 0.0)


def x_constant(n_cols):
    lane = np.arange(2 * LANES)[:, None]
    target = np.arange(LANES)[None, :]
    rim = lane - LANES
    column = np.where(
        lane < LANES, lane, np.where(rim < HALF - 1, rim - RIM, rim - HALF + n_cols)
    )
    inside = (
        ((lane >= 1) & (lane < n_cols - 1))
        | ((rim >= 0) & (rim <= RIM))
        | ((rim >= HALF - 1) & (rim < HALF + RIM))
    )
    inside = inside & (target < n_cols)
    away = column - target
    value = np_split(np.where(inside, np_gaussian(away), 0.0))
    slope = np_split(np.where(inside, np_gaussian(away - 1) - np_gaussian(away + 1), 0.0))
    return np.concatenate([slope[1], value[1], value[0], slope[0]], axis=1)


def y_constant(target, source, used, first_row, last_row):
    def step(by):
        at = source + by
        inside = used & (at >= first_row) & (at < last_row)
        return np.where(inside[None, :], np_gaussian(at[None, :] - target[:, None]), 0.0)

    value = np_split(step(0))
    slope = np_split(step(-1) - step(1))
    pad = ((0, up_to(target.shape[0], 2 * SUBLANES) - target.shape[0]), (0, 0))
    return np.concatenate(
        [np.pad(taps, pad) for taps in (slope[1], slope[0], value[0], value[1])], axis=0
    )


def y_constants(n_rows, depth, near):
    source = np.arange(up_to(n_rows, 2 * SUBLANES))
    own = y_constant(np.arange(n_rows), source, source < n_rows, 0, n_rows)
    tail = []
    for row_at in range(2):
        source = np.arange(near + depth)
        source = source + n_rows - near if row_at == 0 else source - depth
        late = source >= n_rows - EDGE if row_at == 0 else source < EDGE
        target = np.arange(depth) + (n_rows - depth if row_at == 0 else 0)
        tail.append(
            y_constant(target, source, late, -row_at * n_rows, (2 - row_at) * n_rows)
        )
    return own, np.stack(tail)


def start_all(pairs, sems):
    copies = [pltpu.make_async_copy(a, b, sems.at[i]) for i, (a, b) in enumerate(pairs)]
    for copy in copies:
        copy.start()
    return copies


def pack(whole, rows, base, to):
    size = packed_rows(rows)
    lane = iota((size, LANES), 1)
    groups = [[] for _ in range(GROUPS)]
    for c, row, group, _, count in pieces(rows):
        groups[group].append(whole[c][row : row + count])
    spare = GROUPS * size - 2 * rows
    if spare:
        groups[-1].append(jnp.zeros((spare, LANES), f32))
    groups = [jnp.concatenate(group, axis=0) for group in groups]
    value = roll(groups[-1], base + (GROUPS - 1) * GROUP)
    for g in reversed(range(GROUPS - 1)):
        value = jnp.where(lane < (g + 1) * GROUP, roll(groups[g], base + g * GROUP), value)
    to[...] = value


def unpack(seam, beside, rows, turn, sub_at, only=None):
    near = jnp.where(sub_at == 0, 0, HALF)
    parts = [[], []]
    start, stop = only or (0, rows)
    for c, first, group, row, count in pieces(rows):
        skip = max(start - first, 0)
        count = min(first + count, stop) - max(first, start)
        row = row + skip
        if count <= 0:
            continue
        lane = iota((count, LANES), 1)
        parts[c].append(
            jnp.where(
                seam_side(lane, sub_at),
                roll(seam[row : row + count, :], near - group * GROUP),
                roll(beside[row : row + count, :], HALF - near - group * GROUP),
            )
        )
    east, north = (jnp.concatenate(part, axis=0) for part in parts)
    cosine = turn[0:1, :]
    sine = turn[1:2, :]
    return cosine * east - sine * north, sine * east + cosine * north


def with_own(turned, mine, n_cols):
    lane = iota(mine.shape, 1)
    near = jnp.where(lane < RIM + 2, roll(mine, RIM), roll(mine, HALF - n_cols))
    return jnp.where((lane >= RIM) & (lane < HALF), near, turned)


def open_kernel(
    geom,
    velocity,
    wet_bits,
    east_face,
    seam_turn,
    x_source,
    y_source,
    tail_source,
    field,
    rows,
    outer,
    inner,
    wet,
    turn,
    x_taps,
    y_taps,
    tail_taps,
    order,
    vel,
    packed,
    faces,
    turns,
    sems,
):
    n_rows, n_cols, depth, _ = geom
    row_at = lax.axis_index("row")
    copies = start_all(
        (
            (east_face, faces),
            (seam_turn, turns),
            (wet_bits, packed),
            (velocity, vel),
            (x_source, x_taps),
            (y_source, y_taps),
            (tail_source.at[row_at], tail_taps),
        ),
        sems,
    )
    for copy in copies[:2]:
        copy.wait()
    order[0] = seam_order(faces)
    sub_at = lax.axis_index("sub")
    write_turn(faces, turns, turn)
    copies[2].wait()
    at = iota((n_rows, n_cols), 0)
    word = jnp.broadcast_to(packed[0:1, :], (n_rows, n_cols))
    shift = at
    for j in range(1, n_rows // BITS):
        line = jnp.broadcast_to(packed[j : j + 1, :], (n_rows, n_cols))
        later = at >= j * BITS
        word = jnp.where(later, line, word)
        shift = jnp.where(later, at - j * BITS, shift)
    mask = (jnp.right_shift(word, shift) & 1).astype(f32)
    margin = jnp.zeros((n_rows, LANES - n_cols), f32)
    wet[:, :n_cols] = mask
    wet[:, n_cols:] = margin
    copies[3].wait()
    whole = []
    for c in range(2):
        value = jnp.concatenate([vel[c] * mask, margin], axis=1)
        field[c] = value
        rows[c] = facing(row_at, value, depth)
        whole.append(value)
    far = RIM - n_cols
    pack(whole, n_rows, jnp.where(sub_at == 0, 0, far), outer)
    pack(whole, n_rows, jnp.where(sub_at == 0, far, 0), inner)
    for copy in copies[4:]:
        copy.wait()


def corner_pieces(depth):
    size = corner_rows(depth)
    cuts = sorted({*range(0, 5 * depth, depth), *(size * g for g in range(1, GROUPS))})
    return [
        (a // (2 * depth), a // depth % 2, a % depth, a // size, a % size, b - a)
        for a, b in zip(cuts, cuts[1:])
    ]


def corner_rows(depth):
    return up_to(-(-4 * depth // GROUPS), SUBLANES)


def pack_corners(rims, depth):
    size = corner_rows(depth)
    groups = [[] for _ in range(GROUPS)]
    for c, side, row, group, _, count in corner_pieces(depth):
        groups[group].append(roll(rims[c][row : row + count], group * GROUP - side * (HALF - 2)))
    spare = GROUPS * size - 4 * depth
    if spare:
        groups[-1].append(jnp.zeros((spare, LANES), f32))
    groups = [jnp.concatenate(group, axis=0) for group in groups]
    lane = iota((size, LANES), 1)
    value = groups[-1]
    for g in reversed(range(GROUPS - 1)):
        value = jnp.where(lane < (g + 1) * GROUP, groups[g], value)
    return value


def unpack_corners(value, depth):
    parts = {}
    for c, side, _, group, row, count in corner_pieces(depth):
        piece = roll(value[row : row + count, :], side * (HALF - 2) - group * GROUP)
        parts.setdefault((c, side), []).append(piece)
    lane = iota((depth, LANES), 1)
    sides = {key: jnp.concatenate(part, axis=0) for key, part in parts.items()}
    return [jnp.where(lane < RIM + 2, sides[c, 0], sides[c, 1]) for c in range(2)]


def corner_kernel(geom, seam, beside, field, turn, corner):
    n_rows, n_cols, depth, _ = geom
    sub_at = lax.axis_index("sub")
    row_at = lax.axis_index("row")
    ends = [
        unpack(seam, beside, n_rows, turn, sub_at, only)
        for only in ((n_rows - depth, n_rows), (0, depth))
    ]
    corner[...] = pack_corners(
        [
            with_own(
                jnp.where(row_at == 0, ends[0][c], ends[1][c]),
                facing(row_at, field[c], depth),
                n_cols,
            )
            for c in range(2)
        ],
        depth,
    )


def facing(row_at, value, depth):
    return jnp.where(row_at == 0, value[value.shape[0] - depth :], value[:depth])


def keep_along(along, pair, value, rows):
    high, low_part = split(value)
    for c in range(2):
        at = slice(c * LANES, (c + 1) * LANES)
        along[0, pair, :, at] = high[c * rows : (c + 1) * rows]
        along[1, pair, :, at] = low_part[c * rows : (c + 1) * rows]


def across_y(y_taps, along, size):
    main = dot(y_taps[...], along[0, 0])
    more = dot(y_taps[size : 3 * size, :], along[1, 0])
    slope_y = main[size : 2 * size] + (main[:size] + more[:size])
    mean = main[2 * size : 3 * size] + (main[3 * size :] + more[size:])

    def plain(pair):
        main = dot(y_taps[2 * size :, :], along[0, pair])
        more = dot(y_taps[2 * size : 3 * size, :], along[1, pair])
        return main[:size] + (main[size:] + more)

    return slope_y, mean, plain(1), plain(2)


def pool(smooth, mask, pools):
    slope_y, mean, slope_x, flux = smooth
    count = mask.shape[0]
    mean_u = mean[:, :LANES]
    mean_v = mean[:, LANES:]
    block = iota((LANES, LANES), 0) // COARSE == iota((LANES, LANES), 1)
    gather = jnp.where(block, deriv_scale / (COARSE * COARSE), 0.0).astype(bf16)
    out = []
    for c in range(2):
        at = slice(c * LANES, (c + 1) * LANES)
        pools[c] = mask * (flux[:, at] - (mean_u * slope_x[:, at] + mean_v * slope_y[:, at]))
        rows = [
            pools[c, pl.ds(k, count // COARSE, stride=COARSE), :] for k in range(COARSE)
        ]
        high, low_part = split((rows[0] + rows[1]) + (rows[2] + rows[3]))
        out.append(dot(high, gather) + dot(low_part, gather))
    return out


def own_kernel(
    geom,
    seam,
    beside,
    field,
    turn,
    wet,
    x_taps,
    y_taps,
    part,
    tail,
    tail_wet,
    tail_rims,
    padded,
    columns,
    along,
    pools,
):
    n_rows, n_cols, depth, near = geom
    row_at = lax.axis_index("row")
    size = up_to(n_rows, 2 * SUBLANES)
    blank = jnp.zeros((size - n_rows, LANES), f32)
    turned = unpack(seam, beside, n_rows, turn, lax.axis_index("sub"))
    for c in range(2):
        mine = field[c]
        rims = with_own(turned[c], mine, n_cols)
        tail_rims[c] = facing(row_at, rims, near)
        for half, value in enumerate((mine, rims)):
            if size > n_rows:
                value = jnp.concatenate([value, blank], axis=0)
            pad_rows(padded.at[half], c, size, value)
    for half in range(2):
        channels(
            padded.at[half], columns.at[:, :, half * LANES : (half + 1) * LANES], size
        )
    at = iota((2 * size, LANES), 0) % size
    early = jnp.where(row_at == 0, 0, EDGE)
    late = jnp.where(row_at == 0, n_rows - EDGE, n_rows)
    kept = (at >= early) & (at < late)
    for pair, value in enumerate(across_x(columns, x_taps, size)):
        keep_along(along, pair, jnp.where(kept, value, 0.0), size)
    smooth = [value[:n_rows] for value in across_y(y_taps, along, size)]
    mask = wet[...]
    for i, value in enumerate(smooth):
        tail[i] = facing(row_at, value, depth)
    tail_wet[...] = facing(row_at, mask, depth)
    for c, value in enumerate(pool(smooth, mask, pools)):
        part[:, c, :] = value[:, : n_cols // COARSE]


def join_kernel(geom, other, corner, field, tail_rims, tail_rows):
    n_rows, n_cols, depth, near = geom
    row_at = lax.axis_index("row")
    corners = unpack_corners(corner[...], depth)
    for c in range(2):
        mine = facing(row_at, field[c], near)
        for half, (own, far) in enumerate(
            ((mine, other[c]), (tail_rims[c], corners[c]))
        ):
            tail_rows[half, c] = jnp.where(
                row_at == 0,
                jnp.concatenate([own, far], axis=0),
                jnp.concatenate([far, own], axis=0),
            )


def close_kernel(
    geom,
    tail_rows,
    part,
    tail,
    tail_wet,
    x_taps,
    tail_taps,
    forcing,
    padded,
    columns,
    along,
    pools,
):
    n_rows, n_cols, depth, near = geom
    row_at = lax.axis_index("row")
    size = near + depth
    for half in range(2):
        for c in range(2):
            pad_rows(padded.at[half], c, size, tail_rows[half, c])
        channels(
            padded.at[half], columns.at[:, :, half * LANES : (half + 1) * LANES], size
        )
    for pair, value in enumerate(across_x(columns, x_taps, size)):
        keep_along(along, pair, value, size)
    smooth = across_y(tail_taps, along, up_to(depth, 2 * SUBLANES))
    smooth = [value[:depth] + tail[i] for i, value in enumerate(smooth)]
    forcing[...] = part[...]
    start = jnp.where(row_at == 0, (n_rows - depth) // COARSE, 0)
    for c, value in enumerate(pool(smooth, tail_wet[...], pools)):
        forcing[pl.ds(start, depth // COARSE), c, :] = value[:, : n_cols // COARSE]


VMEM_SPEC = pl.BlockSpec(memory_space=pltpu.VMEM)
SMEM_SPEC = pl.BlockSpec(memory_space=pltpu.SMEM)
HBM_SPEC = pl.BlockSpec(memory_space=pltpu.HBM)


def choose(index, branches, *operands):
    closed = jax.make_jaxpr(lambda i, *rest: lax.switch(i, branches, *rest))(index, *operands)
    values = dict(zip(closed.jaxpr.constvars, closed.consts))
    values.update(zip(closed.jaxpr.invars, jax.tree.leaves((index, *operands))))

    def read(atom):
        return atom.val if hasattr(atom, "val") else values[atom]

    for eqn in closed.jaxpr.eqns:
        taken = [read(atom) for atom in eqn.invars]
        if eqn.primitive is lax.clamp_p:
            given = taken[1]
        else:
            given = eqn.primitive.bind(*taken, **eqn.params)
        if not eqn.primitive.multiple_results:
            given = [given]
        values.update(zip(eqn.outvars, given))
    return [read(atom) for atom in closed.jaxpr.outvars]


def seam_pairs(order, subs):
    pairs = []
    for west, east in enumerate(order):
        pairs += [(west * subs + subs - 1, east * subs), (east * subs, west * subs + subs - 1)]
    return pairs


def beside_pairs(subs):
    return [(i, subs - 1 - i) for i in range(subs)]


def exchange(order, east_face, outer, inner, finish):
    faces = east_face.shape[0]
    subs = lax.axis_size("sub")
    beside = beside_pairs(subs)

    def swap(order, outer, inner):
        seam = lax.ppermute(outer, ("tile", "sub"), seam_pairs(order, subs))
        return finish(seam, lax.ppermute(inner, "sub", beside))

    if faces <= SWITCHED_FACES:
        orders = itertools.permutations(range(faces))
        branches = [functools.partial(swap, order) for order in orders]
        return lax.switch(order[0], branches, outer, inner)
    tile_at = lax.axis_index("tile")
    sub_at = lax.axis_index("sub")
    west = jnp.sum(jnp.where(east_face == tile_at, jnp.arange(faces, dtype=jnp.int32), 0))
    east = lax.dynamic_index_in_dim(east_face, tile_at, 0, keepdims=False)
    gathered = lax.all_gather(lax.ppermute(outer, "sub", beside), "tile")
    partner = jnp.where(sub_at == 0, west, east)
    seam = lax.dynamic_index_in_dim(gathered, partner, 0, keepdims=False)
    return finish(seam, lax.ppermute(inner, "sub", beside))


def in_hbm(value):
    return pltpu.with_memory_space_constraint(value, pltpu.HBM)


def paired(velocity, wet_bits, east_face, seam_turn):
    _, n_rows, n_cols = velocity.shape
    depth = up_to(RIM, SUBLANES)
    near = up_to(depth + SUBLANES, 2 * SUBLANES) + 2 * SUBLANES - depth
    geom = (n_rows, n_cols, depth, near)
    size = up_to(n_rows, 2 * SUBLANES)
    end = near + depth
    wide = 2 * LANES
    coarse = n_rows // COARSE
    params = pltpu.CompilerParams(vmem_limit_bytes=16 << 20)
    shape = jax.ShapeDtypeStruct
    kernel = lambda body, name, **rest: pl.pallas_call(
        functools.partial(body, geom), name=name, compiler_params=params, **rest
    )
    packed = shape((packed_rows(n_rows), LANES), f32)
    own_taps, tail_taps = y_constants(n_rows, depth, near)
    taps = (x_constant(n_cols), own_taps, tail_taps)
    field, rows, outer, inner, wet, turn, x_taps, y_taps, tail_taps, order = kernel(
        open_kernel,
        "open",
        out_shape=(
            shape((2, n_rows, LANES), f32),
            shape((2, depth, LANES), f32),
            packed,
            packed,
            shape((n_rows, LANES), f32),
            shape((SUBLANES, LANES), f32),
            shape(taps[0].shape, bf16),
            shape(taps[1].shape, bf16),
            shape(taps[2].shape[1:], bf16),
            pltpu.SMEM((1,), jnp.int32),
        ),
        in_specs=[HBM_SPEC] * 7,
        out_specs=(VMEM_SPEC,) * 9 + (SMEM_SPEC,),
        scratch_shapes=[
            pltpu.VMEM(velocity.shape, f32),
            pltpu.VMEM(wet_bits.shape, jnp.int32),
            pltpu.SMEM(east_face.shape, jnp.int32),
            pltpu.SMEM(seam_turn.shape, jnp.int32),
            pltpu.SemaphoreType.DMA((7,)),
        ],
    )(
        *(in_hbm(value) for value in (velocity, wet_bits, east_face, seam_turn)),
        *(in_hbm(jnp.asarray(value)) for value in taps),
    )
    subs = lax.axis_size("sub")
    across = [(0, 1), (1, 0)]
    part_shape = shape((coarse, 2, n_cols // COARSE), f32)

    def branch(order, outer, inner, rows, field, wet, turn, x_taps, y_taps):
        seam = lax.ppermute(outer, ("tile", "sub"), seam_pairs(order, subs))
        beside = lax.ppermute(inner, "sub", beside_pairs(subs))
        other = lax.ppermute(rows, "row", across)
        corner = kernel(
            corner_kernel,
            "corner",
            out_shape=shape((corner_rows(depth), LANES), f32),
            in_specs=[VMEM_SPEC] * 4,
            out_specs=VMEM_SPEC,
        )(seam, beside, field, turn)
        corner = lax.ppermute(corner, "row", across)
        part, tail, tail_wet, tail_rims = kernel(
            own_kernel,
            "own",
            out_shape=(
                part_shape,
                shape((4, depth, wide), f32),
                shape((depth, LANES), f32),
                shape((2, near, LANES), f32),
            ),
            in_specs=[VMEM_SPEC] * 7,
            out_specs=(VMEM_SPEC,) * 4,
            scratch_shapes=[
                pltpu.VMEM((2, 2, size + 2 * SUBLANES, LANES), f32),
                pltpu.VMEM((2, 4 * size, wide), bf16),
                pltpu.VMEM((2, 3, size, wide), bf16),
                pltpu.VMEM((2, n_rows, LANES), f32),
            ],
            cost_estimate=pl.CostEstimate(
                flops=1 << 30, bytes_accessed=1 << 22, transcendentals=0
            ),
        )(seam, beside, field, turn, wet, x_taps, y_taps)
        tail_rows = kernel(
            join_kernel,
            "join",
            out_shape=shape((2, 2, end, LANES), f32),
            in_specs=[VMEM_SPEC] * 4,
            out_specs=VMEM_SPEC,
        )(other, corner, field, tail_rims)
        return tail_rows, part, tail, tail_wet

    orders = itertools.permutations(range(east_face.shape[0]))
    branches = [functools.partial(branch, order) for order in orders]
    tail_rows, part, tail, tail_wet = choose(
        order[0], branches, outer, inner, rows, field, wet, turn, x_taps, y_taps
    )
    forcing = kernel(
        close_kernel,
        "close",
        out_shape=part_shape,
        in_specs=[VMEM_SPEC] * 6,
        out_specs=VMEM_SPEC,
        scratch_shapes=[
            pltpu.VMEM((2, 2, end + 2 * SUBLANES, LANES), f32),
            pltpu.VMEM((2, 4 * end, wide), bf16),
            pltpu.VMEM((2, 3, end, wide), bf16),
            pltpu.VMEM((2, depth, LANES), f32),
        ],
    )(tail_rows, part, tail, tail_wet, x_taps, tail_taps)
    return jnp.transpose(forcing, (1, 0, 2))


def on_device(velocity, wet_bits, east_face, seam_turn):
    _, n_rows, n_cols = velocity.shape
    row_count = lax.axis_size("row")
    if row_count == 2 and east_face.shape[0] <= SWITCHED_FACES:
        return paired(velocity, wet_bits, east_face, seam_turn)
    depth = up_to(RIM, SUBLANES)
    sides = min(row_count - 1, 2)
    window = n_rows + sides * depth
    geom = (n_rows, n_cols, depth, row_count, window)
    sent = depth * max(sides, 1)
    wide = 2 * LANES
    out_rows = up_to(n_rows, 2 * SUBLANES)
    params = pltpu.CompilerParams(vmem_limit_bytes=16 << 20)
    shape = jax.ShapeDtypeStruct
    field, rows, wet = pl.pallas_call(
        functools.partial(mask_kernel, geom),
        out_shape=(
            shape((2, n_rows, LANES), f32),
            shape((2, sent, LANES), f32),
            shape((n_rows, LANES), f32),
        ),
        in_specs=[HBM_SPEC] * 2,
        out_specs=(VMEM_SPEC,) * 3,
        scratch_shapes=[
            pltpu.VMEM(velocity.shape, f32),
            pltpu.VMEM(wet_bits.shape, jnp.int32),
            pltpu.SemaphoreType.DMA((2,)),
        ],
        compiler_params=params,
        name="mask",
    )(
        pltpu.with_memory_space_constraint(velocity, pltpu.HBM),
        pltpu.with_memory_space_constraint(wet_bits, pltpu.HBM),
    )
    order, turn, x_taps, y_taps = pl.pallas_call(
        functools.partial(prepare_kernel, geom),
        out_shape=(
            shape((1,), jnp.int32),
            shape((SUBLANES, LANES), f32),
            shape((wide, 2 * wide), bf16),
            shape((4 * out_rows, window), bf16),
        ),
        in_specs=[HBM_SPEC] * 2,
        out_specs=(SMEM_SPEC,) + (VMEM_SPEC,) * 3,
        scratch_shapes=[
            pltpu.SMEM(east_face.shape, jnp.int32),
            pltpu.SMEM(seam_turn.shape, jnp.int32),
            pltpu.SemaphoreType.DMA((2,)),
        ],
        compiler_params=params,
        name="prepare",
    )(
        pltpu.with_memory_space_constraint(east_face, pltpu.HBM),
        pltpu.with_memory_space_constraint(seam_turn, pltpu.HBM),
    )
    if row_count == 2:
        before = lax.ppermute(rows, "row", [(0, 1), (1, 0)])
        after = before
    elif row_count > 2:
        up = [(i, i + 1) for i in range(row_count - 1)]
        before = lax.ppermute(rows[:, depth:], "row", up)
        after = lax.ppermute(rows[:, :depth], "row", [(j, i) for i, j in up])
    else:
        before = after = rows
    extended, outer, inner = pl.pallas_call(
        functools.partial(extend_kernel, geom),
        out_shape=(
            shape((2, window, LANES), f32),
            shape((packed_rows(window), LANES), f32),
            shape((packed_rows(window), LANES), f32),
        ),
        in_specs=[VMEM_SPEC] * 3,
        out_specs=(VMEM_SPEC,) * 3,
        compiler_params=params,
        name="extend",
    )(field, before, after)

    def finish(seam, beside):
        partial, edges = pl.pallas_call(
            functools.partial(inner_kernel, geom),
            out_shape=(
                shape((3, 2 * window, LANES), f32),
                shape((2, window, LANES), f32),
            ),
            in_specs=[VMEM_SPEC] * 2,
            out_specs=(VMEM_SPEC,) * 2,
            scratch_shapes=[
                pltpu.VMEM((2, window + 2 * SUBLANES, LANES), f32),
                pltpu.VMEM((2, 4 * window, LANES), bf16),
            ],
            compiler_params=params,
            name="inner",
        )(extended, x_taps)
        return pl.pallas_call(
            functools.partial(filter_kernel, geom),
            out_shape=shape((n_rows // COARSE, 2, n_cols // COARSE), f32),
            in_specs=[VMEM_SPEC] * 8,
            out_specs=VMEM_SPEC,
            scratch_shapes=[
                pltpu.VMEM((2, window + 2 * SUBLANES, LANES), f32),
                pltpu.VMEM((2, 4 * window, LANES), bf16),
                pltpu.VMEM((2, 3, window, wide), bf16),
                pltpu.VMEM((2, n_rows, LANES), f32),
            ],
            compiler_params=params,
            name="filter",
        )(seam, beside, edges, partial, wet, turn, x_taps, y_taps)

    forcing = exchange(order, east_face, outer, inner, finish)
    return jnp.transpose(forcing, (1, 0, 2))


def solution(mesh):
    placed = (
        P(None, ("grp", "row"), ("tile", "sub")),
        P(("grp", "row"), ("tile", "sub")),
        P(),
        P(),
    )
    return jax.shard_map(
        on_device,
        mesh=mesh,
        in_specs=placed,
        out_specs=P(None, ("grp", "row"), ("tile", "sub")),
        check_vma=False,
    )
```

```python
import functools
import itertools

import jax
import jax.numpy as jnp
import numpy as np
from jax import lax
from jax.experimental import pallas as pl
from jax.experimental.pallas import tpu as pltpu
from jax.sharding import PartitionSpec as P

R = 32
RIM = R + 1
BITS = 30
COARSE = 4
LANES = 128
HALF = LANES // 2
GROUPS = 3
GROUP = 40
SUBLANES = 8
SWITCHED_FACES = 4

deriv_scale = 8.0

f32 = jnp.float32
bf16 = jnp.bfloat16


def up_to(value, step):
    return -(-value // step) * step


def iota(shape, dim):
    return lax.broadcasted_iota(jnp.int32, shape, dim)


def split(value):
    high = value.astype(bf16)
    return high, (value - high.astype(f32)).astype(bf16)


def dot(left, right):
    return jnp.dot(left, right, preferred_element_type=f32)


def taps_sum():
    taps = np.arange(-R, R + 1, dtype=np.float64)
    return float(np.sum(np.exp(-0.5 * (taps / R) ** 2)))


def gaussian(distance, inside):
    inside = inside & (distance >= -R) & (distance <= R)
    scaled = distance.astype(f32) * (1.0 / R)
    return jnp.where(inside, jnp.exp(-0.5 * scaled * scaled) * (1.0 / taps_sum()), 0.0)


def roll(value, shift):
    shift = shift % LANES
    return pltpu.roll(value, shift, axis=1) if shift else value


def fetch(pairs, sems):
    copies = [pltpu.make_async_copy(a, b, sems.at[i]) for i, (a, b) in enumerate(pairs)]
    for copy in copies:
        copy.start()
    for copy in copies:
        copy.wait()


def mask_kernel(geom, velocity, wet_bits, field, rows, wet, vel, packed, sems):
    n_rows, n_cols, depth, row_count, _ = geom
    fetch(((velocity, vel), (wet_bits, packed)), sems)
    at = iota((n_rows, n_cols), 0)
    word = jnp.broadcast_to(packed[0:1, :], (n_rows, n_cols))
    shift = at
    for j in range(1, n_rows // BITS):
        line = jnp.broadcast_to(packed[j : j + 1, :], (n_rows, n_cols))
        later = at >= j * BITS
        word = jnp.where(later, line, word)
        shift = jnp.where(later, at - j * BITS, shift)
    mask = (jnp.right_shift(word, shift) & 1).astype(f32)
    margin = jnp.zeros((n_rows, LANES - n_cols), f32)
    wet[:, :n_cols] = mask
    wet[:, n_cols:] = margin
    row_at = lax.axis_index("row")
    for c in range(2):
        value = jnp.concatenate([vel[c] * mask, margin], axis=1)
        field[c] = value
        if row_count == 2:
            rows[c] = jnp.where(row_at == 0, value[n_rows - depth :], value[:depth])
        elif row_count > 2:
            rows[c, :depth] = value[:depth]
            rows[c, depth:] = value[n_rows - depth :]


def seam_order(faces):
    count = faces.shape[0]
    order = jnp.int32(0)
    for i in range(count):
        smaller = jnp.int32(0)
        for j in range(i + 1, count):
            smaller = smaller + jnp.where(faces[j] < faces[i], 1, 0)
        order = order * (count - i) + smaller
    return order


def prepare_kernel(
    geom, east_face, seam_turn, order, turn, x_taps, y_taps, faces, turns, sems
):
    n_rows, n_cols, depth, row_count, window = geom
    copies = [
        pltpu.make_async_copy(east_face, faces, sems.at[0]),
        pltpu.make_async_copy(seam_turn, turns, sems.at[1]),
    ]
    for copy in copies:
        copy.start()
    row_at = lax.axis_index("row")
    lane = iota((2 * LANES, LANES), 0)
    target = iota((2 * LANES, LANES), 1)
    rim = lane - LANES
    column = jnp.where(
        lane < LANES, lane, jnp.where(rim < HALF - 1, rim - RIM, rim - HALF + n_cols)
    )
    inside = (
        ((lane >= 1) & (lane < n_cols - 1))
        | ((rim >= 0) & (rim <= RIM))
        | ((rim >= HALF - 1) & (rim < HALF + RIM))
    )
    inside = inside & (target < n_cols)
    away = column - target
    value = split(gaussian(away, inside))
    slope = split(gaussian(away - 1, inside) - gaussian(away + 1, inside))
    for i, taps in enumerate((slope[1], value[1], value[0], slope[0])):
        x_taps[:, i * LANES : (i + 1) * LANES] = taps
    out_rows = up_to(n_rows, 2 * SUBLANES)
    source = iota((out_rows, window), 1)
    target = iota((out_rows, window), 0)
    start = row_start(geom, row_at)
    world = source - start + row_at * n_rows
    last = row_count * n_rows

    def taps_at(step):
        at = world + step
        inside = (at >= 0) & (at < last) & (target < n_rows)
        return gaussian(source + step - start - target, inside)

    value = split(taps_at(0))
    slope = split(taps_at(-1) - taps_at(1))
    for i, taps in enumerate((slope[1], slope[0], value[0], value[1])):
        y_taps[i * out_rows : (i + 1) * out_rows, :] = taps
    for copy in copies:
        copy.wait()
    order[0] = seam_order(faces) if faces.shape[0] <= SWITCHED_FACES else jnp.int32(0)
    write_turn(faces, turns, turn)


def write_turn(faces, turns, turn):
    tile_at = lax.axis_index("tile")
    back = jnp.int32(0)
    for w in range(faces.shape[0]):
        back = jnp.where(faces[w] == tile_at, turns[w], back)
    sub_at = lax.axis_index("sub")
    quarter = jnp.where(sub_at == 0, (4 - back) % 4, turns[tile_at])
    cosine = jnp.where(quarter == 0, 1.0, jnp.where(quarter == 2, -1.0, 0.0)).astype(f32)
    sine = jnp.where(quarter == 1, 1.0, jnp.where(quarter == 3, -1.0, 0.0)).astype(f32)
    row = iota((SUBLANES, LANES), 0)
    lane = iota((SUBLANES, LANES), 1)
    seam_lane = seam_side(lane, sub_at)
    turn[...] = jnp.where(
        row == 0, jnp.where(seam_lane, cosine, 1.0), jnp.where(seam_lane, sine, 0.0)
    )


def seam_side(lane, sub_at):
    edge = jnp.where(sub_at == 0, RIM, LANES)
    start = jnp.where(sub_at == 0, 0, HALF)
    return (lane >= start) & (lane < edge)


def packed_rows(window):
    return up_to(-(-2 * window // GROUPS), SUBLANES)


def pieces(window):
    size = packed_rows(window)
    cuts = sorted({0, window, 2 * window, *(size * g for g in range(1, GROUPS))})
    return [
        (a // window, a % window, a // size, a % size, b - a) for a, b in zip(cuts, cuts[1:])
    ]


def row_start(geom, row_at):
    _, _, depth, row_count, _ = geom
    if row_count == 2:
        return jnp.where(row_at == 0, 0, depth)
    return jnp.int32(depth if row_count > 2 else 0)


def extend_kernel(geom, field, before, after, extended, outer, inner):
    n_rows, n_cols, depth, row_count, window = geom
    row_at = lax.axis_index("row")
    whole = []
    for c in range(2):
        mine = field[c]
        if row_count == 2:
            other = before[c]
            value = jnp.where(
                row_at == 0,
                jnp.concatenate([mine, other], axis=0),
                jnp.concatenate([other, mine], axis=0),
            )
        elif row_count > 2:
            value = jnp.concatenate([before[c], mine, after[c]], axis=0)
        else:
            value = mine
        extended[c] = value
        whole.append(value)
    first = lax.axis_index("sub") == 0
    west, east = pack(whole, window, (0, n_cols - RIM))
    outer[...] = jnp.where(first, west, east)
    inner[...] = jnp.where(first, east, west)


def pad_rows(padded, c, window, value):
    blank = jnp.zeros((SUBLANES, LANES), f32)
    padded[c, :SUBLANES, :] = blank
    padded[c, SUBLANES + window :, :] = blank
    padded[c, SUBLANES : SUBLANES + window, :] = value


def channels(padded, columns, window):
    vel = [padded[c, SUBLANES : SUBLANES + window, :] for c in range(2)]
    for c in range(2):
        grad_x = roll(vel[c], -1) - roll(vel[c], 1)
        grad_y = (
            padded[c, SUBLANES + 1 : SUBLANES + 1 + window, :]
            - padded[c, SUBLANES - 1 : SUBLANES - 1 + window, :]
        )
        advect = vel[0] * grad_x + vel[1] * grad_y
        for at, value in ((c, vel[c]), (2 + c, advect)):
            high, low_part = split(value)
            columns[0, at * window : (at + 1) * window, :] = high
            columns[1, at * window : (at + 1) * window, :] = low_part


def across_x(columns, x_taps, window):
    wide = 2 * LANES
    high = x_taps[:, wide:]
    low_part = x_taps[:, :wide]
    both = x_taps[:, LANES : LANES + wide]
    main = dot(columns[0, : 2 * window, :], high)
    more = dot(columns[1, : 2 * window, :], high)
    rest = dot(columns[0, : 2 * window, :], low_part)
    flux = dot(columns[0, 2 * window :, :], both)
    flux_more = dot(columns[1, 2 * window :, :], both[:, LANES:])
    means = main[:, :LANES] + (more[:, :LANES] + rest[:, LANES:])
    slopes = main[:, LANES:] + (more[:, LANES:] + rest[:, :LANES])
    fluxes = flux[:, LANES:] + (flux_more + flux[:, :LANES])
    return means, slopes, fluxes


def inner_kernel(geom, extended, x_taps, partial, edges, padded, columns):
    n_rows, n_cols, depth, row_count, window = geom
    lane = iota((window, LANES), 1)
    for c in range(2):
        own = extended[c]
        pad_rows(padded, c, window, own)
        near = jnp.where(lane < RIM + 2, roll(own, RIM), roll(own, HALF - n_cols))
        edges[c] = near
    channels(padded, columns, window)
    for pair, value in enumerate(across_x(columns, x_taps[:LANES, :], window)):
        partial[pair] = value


def filter_kernel(
    geom,
    seam,
    beside,
    edges,
    partial,
    wet,
    turn,
    x_taps,
    y_taps,
    forcing,
    padded,
    columns,
    along,
    pools,
):
    n_rows, n_cols, depth, row_count, window = geom
    sub_at = lax.axis_index("sub")
    out_rows = up_to(n_rows, 2 * SUBLANES)
    west = jnp.where(sub_at == 0, seam[...], beside[...])
    east = jnp.where(sub_at == 0, beside[...], seam[...])
    turned = unpack(west, east, window, turn)
    lane = iota((window, LANES), 1)
    own = (lane >= RIM) & (lane < HALF)
    for c in range(2):
        pad_rows(padded, c, window, jnp.where(own, edges[c], turned[c]))
    channels(padded, columns, window)
    for pair, value in enumerate(across_x(columns, x_taps[LANES:, :], window)):
        value = value + partial[pair]
        high, low_part = split(value)
        for c in range(2):
            at = slice(c * LANES, (c + 1) * LANES)
            along[0, pair, :, at] = high[c * window : (c + 1) * window]
            along[1, pair, :, at] = low_part[c * window : (c + 1) * window]

    main = dot(y_taps[...], along[0, 0])
    more = dot(y_taps[out_rows : 3 * out_rows, :], along[1, 0])
    slope_y = main[out_rows : 2 * out_rows] + (main[:out_rows] + more[:out_rows])
    mean = main[2 * out_rows : 3 * out_rows] + (main[3 * out_rows :] + more[out_rows:])

    def across(pair):
        main = dot(y_taps[2 * out_rows :, :], along[0, pair])
        more = dot(y_taps[2 * out_rows : 3 * out_rows, :], along[1, pair])
        return main[:out_rows] + (main[out_rows:] + more)

    slope_x = across(1)
    flux = across(2)
    mean_u = mean[:n_rows, :LANES]
    mean_v = mean[:n_rows, LANES:]
    mask = wet[...]
    coarse = n_rows // COARSE
    for c in range(2):
        at = slice(c * LANES, (c + 1) * LANES)
        pools[c] = mask * (
            flux[:n_rows, at] - (mean_u * slope_x[:n_rows, at] + mean_v * slope_y[:n_rows, at])
        )
    block = iota((LANES, LANES), 0) // COARSE == iota((LANES, LANES), 1)
    gather = jnp.where(block, deriv_scale / (COARSE * COARSE), 0.0).astype(bf16)
    for c in range(2):
        rows = [pools[c, pl.ds(k, coarse, stride=COARSE), :] for k in range(COARSE)]
        high, low_part = split((rows[0] + rows[1]) + (rows[2] + rows[3]))
        value = dot(high, gather) + dot(low_part, gather)
        forcing[:, c, :] = value[:, : n_cols // COARSE]


EDGE = 4


def np_split(value):
    high = value.astype(bf16)
    return high, (value - high.astype(np.float64)).astype(bf16)


def np_gaussian(distance):
    inside = np.abs(distance) <= R
    return np.where(inside, np.exp(-0.5 * (distance / R) ** 2) / taps_sum(), 0.0)


def x_constant(n_cols):
    lane = np.arange(2 * LANES)[:, None]
    target = np.arange(LANES)[None, :]
    rim = lane - LANES
    column = np.where(
        lane < LANES, lane, np.where(rim < HALF - 1, rim - RIM, rim - HALF + n_cols)
    )
    inside = (
        ((lane >= 1) & (lane < n_cols - 1))
        | ((rim >= 0) & (rim <= RIM))
        | ((rim >= HALF - 1) & (rim < HALF + RIM))
    )
    inside = inside & (target < n_cols)
    away = column - target
    value = np_split(np.where(inside, np_gaussian(away), 0.0))
    slope = np_split(np.where(inside, np_gaussian(away - 1) - np_gaussian(away + 1), 0.0))
    return np.concatenate([slope[1], value[1], value[0], slope[0]], axis=1)


def y_constant(target, source, used, first_row, last_row):
    def step(by):
        at = source + by
        inside = used & (at >= first_row) & (at < last_row)
        return np.where(inside[None, :], np_gaussian(at[None, :] - target[:, None]), 0.0)

    value = np_split(step(0))
    slope = np_split(step(-1) - step(1))
    pad = ((0, up_to(target.shape[0], 2 * SUBLANES) - target.shape[0]), (0, 0))
    return np.concatenate(
        [np.pad(taps, pad) for taps in (slope[1], slope[0], value[0], value[1])], axis=0
    )


def y_constants(n_rows, depth, near):
    source = np.arange(up_to(n_rows, 2 * SUBLANES))
    own = y_constant(np.arange(n_rows), source, source < n_rows, 0, n_rows)
    tail = []
    for row_at in range(2):
        source = np.arange(near + depth)
        source = source + n_rows - near if row_at == 0 else source - depth
        late = source >= n_rows - EDGE if row_at == 0 else source < EDGE
        target = np.arange(depth) + (n_rows - depth if row_at == 0 else 0)
        tail.append(
            y_constant(target, source, late, -row_at * n_rows, (2 - row_at) * n_rows)
        )
    return own, np.stack(tail)


def start_all(pairs, sems):
    copies = [pltpu.make_async_copy(a, b, sems.at[i]) for i, (a, b) in enumerate(pairs)]
    for copy in copies:
        copy.start()
    return copies


def pack(whole, rows, bases):
    size = packed_rows(rows)
    lane = iota((size, LANES), 1)
    groups = [[] for _ in range(GROUPS)]
    for c, row, group, _, count in pieces(rows):
        groups[group].append(whole[c][row : row + count])
    spare = GROUPS * size - 2 * rows
    if spare:
        groups[-1].append(jnp.zeros((spare, LANES), f32))
    groups = [jnp.concatenate(group, axis=0) for group in groups]
    out = []
    for base in bases:
        value = roll(groups[-1], (GROUPS - 1) * GROUP - base)
        for g in reversed(range(GROUPS - 1)):
            value = jnp.where(lane < (g + 1) * GROUP, roll(groups[g], g * GROUP - base), value)
        out.append(value)
    return out


def unpack(west, east, rows, turn, only=None):
    parts = [[], []]
    start, stop = only or (0, rows)
    for c, first, group, row, count in pieces(rows):
        row = row + max(start - first, 0)
        count = min(first + count, stop) - max(first, start)
        if count <= 0:
            continue
        low = iota((count, LANES), 1) < HALF
        parts[c].append(
            jnp.where(
                low,
                roll(west[row : row + count, :], -group * GROUP),
                roll(east[row : row + count, :], HALF - group * GROUP),
            )
        )
    u, v = (jnp.concatenate(part, axis=0) for part in parts)
    cosine = turn[0:1, :]
    sine = turn[1:2, :]
    return cosine * u - sine * v, sine * u + cosine * v


def with_own(turned, mine, n_cols):
    lane = iota(mine.shape, 1)
    near = jnp.where(lane < RIM + 2, roll(mine, RIM), roll(mine, HALF - n_cols))
    return jnp.where((lane >= RIM) & (lane < HALF), near, turned)


def open_kernel(
    geom,
    velocity,
    wet_bits,
    east_face,
    seam_turn,
    x_source,
    y_source,
    tail_source,
    field,
    outer,
    inner,
    wet,
    turn,
    x_taps,
    y_taps,
    tail_taps,
    order,
    vel,
    packed,
    faces,
    turns,
    sems,
):
    n_rows, n_cols, _, _ = geom
    copies = start_all(
        (
            (wet_bits, packed),
            (velocity, vel),
            (east_face, faces),
            (seam_turn, turns),
            (x_source, x_taps),
            (y_source, y_taps),
            (tail_source.at[lax.axis_index("row")], tail_taps),
        ),
        sems,
    )
    copies[0].wait()
    at = iota((n_rows, n_cols), 0)
    word = jnp.broadcast_to(packed[0:1, :], (n_rows, n_cols))
    shift = at
    for j in range(1, n_rows // BITS):
        line = jnp.broadcast_to(packed[j : j + 1, :], (n_rows, n_cols))
        later = at >= j * BITS
        word = jnp.where(later, line, word)
        shift = jnp.where(later, at - j * BITS, shift)
    mask = (jnp.right_shift(word, shift) & 1).astype(f32)
    margin = jnp.zeros((n_rows, LANES - n_cols), f32)
    wet[:, :n_cols] = mask
    wet[:, n_cols:] = margin
    for copy in copies[1:4]:
        copy.wait()
    order[0] = seam_order(faces)
    whole = []
    for c in range(2):
        value = jnp.concatenate([vel[c] * mask, margin], axis=1)
        field[c] = value
        whole.append(value)
    west, east = pack(whole, n_rows, (0, n_cols - RIM))
    first = lax.axis_index("sub") == 0
    outer[...] = jnp.where(first, west, east)
    inner[...] = jnp.where(first, east, west)
    write_turn(faces, turns, turn)
    for copy in copies[4:]:
        copy.wait()


def corner_pieces(depth):
    size = corner_rows(depth)
    cuts = sorted({*range(0, 5 * depth, depth), *(size * g for g in range(1, GROUPS))})
    return [
        (a // (2 * depth), a // depth % 2, a % depth, a // size, a % size, b - a)
        for a, b in zip(cuts, cuts[1:])
    ]


def corner_rows(depth):
    return up_to(-(-4 * depth // GROUPS), SUBLANES)


def pack_corners(rims, depth):
    size = corner_rows(depth)
    groups = [[] for _ in range(GROUPS)]
    for c, side, row, group, _, count in corner_pieces(depth):
        groups[group].append(roll(rims[c][row : row + count], group * GROUP - side * (HALF - 2)))
    spare = GROUPS * size - 4 * depth
    if spare:
        groups[-1].append(jnp.zeros((spare, LANES), f32))
    groups = [jnp.concatenate(group, axis=0) for group in groups]
    lane = iota((size, LANES), 1)
    value = groups[-1]
    for g in reversed(range(GROUPS - 1)):
        value = jnp.where(lane < (g + 1) * GROUP, groups[g], value)
    return value


def unpack_corners(value, depth):
    parts = {}
    for c, side, _, group, row, count in corner_pieces(depth):
        piece = roll(value[row : row + count, :], side * (HALF - 2) - group * GROUP)
        parts.setdefault((c, side), []).append(piece)
    lane = iota((depth, LANES), 1)
    sides = {key: jnp.concatenate(part, axis=0) for key, part in parts.items()}
    return [jnp.where(lane < RIM + 2, sides[c, 0], sides[c, 1]) for c in range(2)]


def edge_kernel(geom, seam, beside, field, turn, edge, west, east):
    n_rows, n_cols, depth, _ = geom
    row_at = lax.axis_index("row")
    first = lax.axis_index("sub") == 0
    west[...] = jnp.where(first, seam[...], beside[...])
    east[...] = jnp.where(first, beside[...], seam[...])
    ends = [
        unpack(west, east, n_rows, turn, only)
        for only in ((n_rows - depth, n_rows), (0, depth))
    ]
    corners = []
    for c in range(2):
        mine = facing(row_at, field[c], depth)
        edge[c * depth : (c + 1) * depth, :] = mine
        corners.append(with_own(jnp.where(row_at == 0, ends[0][c], ends[1][c]), mine, n_cols))
    edge[2 * depth :, :] = pack_corners(corners, depth)


def facing(row_at, value, depth):
    return jnp.where(row_at == 0, value[value.shape[0] - depth :], value[:depth])


def keep_along(along, pair, value, rows):
    high, low_part = split(value)
    for c in range(2):
        at = slice(c * LANES, (c + 1) * LANES)
        along[0, pair, :, at] = high[c * rows : (c + 1) * rows]
        along[1, pair, :, at] = low_part[c * rows : (c + 1) * rows]


def across_y(y_taps, along, size):
    main = dot(y_taps[...], along[0, 0])
    more = dot(y_taps[size : 3 * size, :], along[1, 0])
    slope_y = main[size : 2 * size] + (main[:size] + more[:size])
    mean = main[2 * size : 3 * size] + (main[3 * size :] + more[size:])

    def plain(pair):
        main = dot(y_taps[2 * size :, :], along[0, pair])
        more = dot(y_taps[2 * size : 3 * size, :], along[1, pair])
        return main[:size] + (main[size:] + more)

    return slope_y, mean, plain(1), plain(2)


def pool(smooth, mask, pools):
    slope_y, mean, slope_x, flux = smooth
    count = mask.shape[0]
    mean_u = mean[:, :LANES]
    mean_v = mean[:, LANES:]
    block = iota((LANES, LANES), 0) // COARSE == iota((LANES, LANES), 1)
    gather = jnp.where(block, deriv_scale / (COARSE * COARSE), 0.0).astype(bf16)
    out = []
    for c in range(2):
        at = slice(c * LANES, (c + 1) * LANES)
        pools[c] = mask * (flux[:, at] - (mean_u * slope_x[:, at] + mean_v * slope_y[:, at]))
        rows = [
            pools[c, pl.ds(k, count // COARSE, stride=COARSE), :] for k in range(COARSE)
        ]
        high, low_part = split((rows[0] + rows[1]) + (rows[2] + rows[3]))
        out.append(dot(high, gather) + dot(low_part, gather))
    return out


def own_kernel(
    geom,
    west,
    east,
    field,
    turn,
    wet,
    x_taps,
    y_taps,
    part,
    tail,
    tail_wet,
    tail_rims,
    padded,
    columns,
    along,
    pools,
):
    n_rows, n_cols, depth, near = geom
    row_at = lax.axis_index("row")
    size = up_to(n_rows, 2 * SUBLANES)
    blank = jnp.zeros((size - n_rows, LANES), f32)
    turned = unpack(west, east, n_rows, turn)
    for c in range(2):
        mine = field[c]
        rims = with_own(turned[c], mine, n_cols)
        tail_rims[c] = facing(row_at, rims, near)
        for half, value in enumerate((mine, rims)):
            if size > n_rows:
                value = jnp.concatenate([value, blank], axis=0)
            pad_rows(padded.at[half], c, size, value)
    for half in range(2):
        channels(
            padded.at[half], columns.at[:, :, half * LANES : (half + 1) * LANES], size
        )
    at = iota((2 * size, LANES), 0) % size
    early = jnp.where(row_at == 0, 0, EDGE)
    late = jnp.where(row_at == 0, n_rows - EDGE, n_rows)
    kept = (at >= early) & (at < late)
    for pair, value in enumerate(across_x(columns, x_taps, size)):
        keep_along(along, pair, jnp.where(kept, value, 0.0), size)
    smooth = [value[:n_rows] for value in across_y(y_taps, along, size)]
    mask = wet[...]
    for i, value in enumerate(smooth):
        tail[i] = facing(row_at, value, depth)
    tail_wet[...] = facing(row_at, mask, depth)
    for c, value in enumerate(pool(smooth, mask, pools)):
        part[:, c, :] = value[:, : n_cols // COARSE]


def close_kernel(
    geom,
    edge,
    field,
    part,
    tail,
    tail_wet,
    tail_rims,
    x_taps,
    tail_taps,
    forcing,
    padded,
    columns,
    along,
    pools,
):
    n_rows, n_cols, depth, near = geom
    row_at = lax.axis_index("row")
    size = near + depth
    corners = unpack_corners(edge[2 * depth :, :], depth)
    for half in range(2):
        for c in range(2):
            if half == 0:
                own = facing(row_at, field[c], near)
                far = edge[c * depth : (c + 1) * depth, :]
            else:
                own = tail_rims[c]
                far = corners[c]
            value = jnp.where(
                row_at == 0,
                jnp.concatenate([own, far], axis=0),
                jnp.concatenate([far, own], axis=0),
            )
            pad_rows(padded.at[half], c, size, value)
        channels(
            padded.at[half], columns.at[:, :, half * LANES : (half + 1) * LANES], size
        )
    for pair, value in enumerate(across_x(columns, x_taps, size)):
        keep_along(along, pair, value, size)
    smooth = across_y(tail_taps, along, up_to(depth, 2 * SUBLANES))
    smooth = [value[:depth] + tail[i] for i, value in enumerate(smooth)]
    forcing[...] = part[...]
    start = jnp.where(row_at == 0, (n_rows - depth) // COARSE, 0)
    for c, value in enumerate(pool(smooth, tail_wet[...], pools)):
        forcing[pl.ds(start, depth // COARSE), c, :] = value[:, : n_cols // COARSE]


VMEM_SPEC = pl.BlockSpec(memory_space=pltpu.VMEM)
SMEM_SPEC = pl.BlockSpec(memory_space=pltpu.SMEM)
HBM_SPEC = pl.BlockSpec(memory_space=pltpu.HBM)


def choose(index, branches, *operands):
    closed = jax.make_jaxpr(lambda i, *rest: lax.switch(i, branches, *rest))(index, *operands)
    values = dict(zip(closed.jaxpr.constvars, closed.consts))
    values.update(zip(closed.jaxpr.invars, jax.tree.leaves((index, *operands))))

    def read(atom):
        return atom.val if hasattr(atom, "val") else values[atom]

    for eqn in closed.jaxpr.eqns:
        taken = [read(atom) for atom in eqn.invars]
        if eqn.primitive is lax.clamp_p:
            given = taken[1]
        else:
            given = eqn.primitive.bind(*taken, **eqn.params)
        if not eqn.primitive.multiple_results:
            given = [given]
        values.update(zip(eqn.outvars, given))
    return [read(atom) for atom in closed.jaxpr.outvars]


def seam_pairs(order, subs):
    pairs = []
    for west, east in enumerate(order):
        pairs += [(west * subs + subs - 1, east * subs), (east * subs, west * subs + subs - 1)]
    return pairs


def beside_pairs(subs):
    return [(i, subs - 1 - i) for i in range(subs)]


def exchange(order, east_face, outer, inner, finish):
    faces = east_face.shape[0]
    subs = lax.axis_size("sub")
    beside = beside_pairs(subs)

    def swap(order, outer, inner):
        seam = lax.ppermute(outer, ("tile", "sub"), seam_pairs(order, subs))
        return finish(seam, lax.ppermute(inner, "sub", beside))

    if faces <= SWITCHED_FACES:
        orders = itertools.permutations(range(faces))
        branches = [functools.partial(swap, order) for order in orders]
        return lax.switch(order[0], branches, outer, inner)
    tile_at = lax.axis_index("tile")
    sub_at = lax.axis_index("sub")
    west = jnp.sum(jnp.where(east_face == tile_at, jnp.arange(faces, dtype=jnp.int32), 0))
    east = lax.dynamic_index_in_dim(east_face, tile_at, 0, keepdims=False)
    gathered = lax.all_gather(lax.ppermute(outer, "sub", beside), "tile")
    partner = jnp.where(sub_at == 0, west, east)
    seam = lax.dynamic_index_in_dim(gathered, partner, 0, keepdims=False)
    return finish(seam, lax.ppermute(inner, "sub", beside))


def in_hbm(value):
    return pltpu.with_memory_space_constraint(value, pltpu.HBM)


def paired(velocity, wet_bits, east_face, seam_turn):
    _, n_rows, n_cols = velocity.shape
    depth = up_to(RIM, SUBLANES)
    near = up_to(depth + SUBLANES, 2 * SUBLANES) - depth
    geom = (n_rows, n_cols, depth, near)
    size = up_to(n_rows, 2 * SUBLANES)
    end = near + depth
    wide = 2 * LANES
    coarse = n_rows // COARSE
    params = pltpu.CompilerParams(vmem_limit_bytes=16 << 20)
    shape = jax.ShapeDtypeStruct
    kernel = lambda body, name, **rest: pl.pallas_call(
        functools.partial(body, geom), name=name, compiler_params=params, **rest
    )
    packed = shape((packed_rows(n_rows), LANES), f32)
    own_taps, tail_taps = y_constants(n_rows, depth, near)
    taps = (x_constant(n_cols), own_taps, tail_taps)
    field, outer, inner, wet, turn, x_taps, y_taps, tail_taps, order = kernel(
        open_kernel,
        "open",
        out_shape=(
            shape((2, n_rows, LANES), f32),
            packed,
            packed,
            shape((n_rows, LANES), f32),
            shape((SUBLANES, LANES), f32),
            shape(taps[0].shape, bf16),
            shape(taps[1].shape, bf16),
            shape(taps[2].shape[1:], bf16),
            pltpu.SMEM((1,), jnp.int32),
        ),
        in_specs=[HBM_SPEC] * 7,
        out_specs=(VMEM_SPEC,) * 8 + (SMEM_SPEC,),
        scratch_shapes=[
            pltpu.VMEM(velocity.shape, f32),
            pltpu.VMEM(wet_bits.shape, jnp.int32),
            pltpu.SMEM(east_face.shape, jnp.int32),
            pltpu.SMEM(seam_turn.shape, jnp.int32),
            pltpu.SemaphoreType.DMA((7,)),
        ],
    )(
        *(in_hbm(value) for value in (velocity, wet_bits, east_face, seam_turn)),
        *(in_hbm(jnp.asarray(value)) for value in taps),
    )
    subs = lax.axis_size("sub")
    part_shape = shape((coarse, 2, n_cols // COARSE), f32)

    def branch(order, outer, inner, field, turn):
        seam = lax.ppermute(outer, ("tile", "sub"), seam_pairs(order, subs))
        beside = lax.ppermute(inner, "sub", beside_pairs(subs))
        return kernel(
            edge_kernel,
            "edge",
            out_shape=(
                shape((2 * depth + corner_rows(depth), LANES), f32),
                packed,
                packed,
            ),
            in_specs=[VMEM_SPEC] * 4,
            out_specs=(VMEM_SPEC,) * 3,
        )(seam, beside, field, turn)

    orders = itertools.permutations(range(east_face.shape[0]))
    branches = [functools.partial(branch, order) for order in orders]
    edge, west, east = choose(order[0], branches, outer, inner, field, turn)
    edge = lax.ppermute(edge, "row", [(0, 1), (1, 0)])
    part, tail, tail_wet, tail_rims = kernel(
        own_kernel,
        "own",
        out_shape=(
            part_shape,
            shape((4, depth, wide), f32),
            shape((depth, LANES), f32),
            shape((2, near, LANES), f32),
        ),
        in_specs=[VMEM_SPEC] * 7,
        out_specs=(VMEM_SPEC,) * 4,
        scratch_shapes=[
            pltpu.VMEM((2, 2, size + 2 * SUBLANES, LANES), f32),
            pltpu.VMEM((2, 4 * size, wide), bf16),
            pltpu.VMEM((2, 3, size, wide), bf16),
            pltpu.VMEM((2, n_rows, LANES), f32),
        ],
        cost_estimate=pl.CostEstimate(
            flops=1 << 30, bytes_accessed=1 << 22, transcendentals=0
        ),
    )(west, east, field, turn, wet, x_taps, y_taps)
    forcing = kernel(
        close_kernel,
        "close",
        out_shape=part_shape,
        in_specs=[VMEM_SPEC] * 8,
        out_specs=VMEM_SPEC,
        scratch_shapes=[
            pltpu.VMEM((2, 2, end + 2 * SUBLANES, LANES), f32),
            pltpu.VMEM((2, 4 * end, wide), bf16),
            pltpu.VMEM((2, 3, end, wide), bf16),
            pltpu.VMEM((2, depth, LANES), f32),
        ],
    )(edge, field, part, tail, tail_wet, tail_rims, x_taps, tail_taps)
    return jnp.transpose(forcing, (1, 0, 2))


def on_device(velocity, wet_bits, east_face, seam_turn):
    _, n_rows, n_cols = velocity.shape
    row_count = lax.axis_size("row")
    if row_count == 2 and east_face.shape[0] <= SWITCHED_FACES:
        return paired(velocity, wet_bits, east_face, seam_turn)
    depth = up_to(RIM, SUBLANES)
    sides = min(row_count - 1, 2)
    window = n_rows + sides * depth
    geom = (n_rows, n_cols, depth, row_count, window)
    sent = depth * max(sides, 1)
    wide = 2 * LANES
    out_rows = up_to(n_rows, 2 * SUBLANES)
    params = pltpu.CompilerParams(vmem_limit_bytes=16 << 20)
    shape = jax.ShapeDtypeStruct
    field, rows, wet = pl.pallas_call(
        functools.partial(mask_kernel, geom),
        out_shape=(
            shape((2, n_rows, LANES), f32),
            shape((2, sent, LANES), f32),
            shape((n_rows, LANES), f32),
        ),
        in_specs=[HBM_SPEC] * 2,
        out_specs=(VMEM_SPEC,) * 3,
        scratch_shapes=[
            pltpu.VMEM(velocity.shape, f32),
            pltpu.VMEM(wet_bits.shape, jnp.int32),
            pltpu.SemaphoreType.DMA((2,)),
        ],
        compiler_params=params,
        name="mask",
    )(
        pltpu.with_memory_space_constraint(velocity, pltpu.HBM),
        pltpu.with_memory_space_constraint(wet_bits, pltpu.HBM),
    )
    order, turn, x_taps, y_taps = pl.pallas_call(
        functools.partial(prepare_kernel, geom),
        out_shape=(
            shape((1,), jnp.int32),
            shape((SUBLANES, LANES), f32),
            shape((wide, 2 * wide), bf16),
            shape((4 * out_rows, window), bf16),
        ),
        in_specs=[HBM_SPEC] * 2,
        out_specs=(SMEM_SPEC,) + (VMEM_SPEC,) * 3,
        scratch_shapes=[
            pltpu.SMEM(east_face.shape, jnp.int32),
            pltpu.SMEM(seam_turn.shape, jnp.int32),
            pltpu.SemaphoreType.DMA((2,)),
        ],
        compiler_params=params,
        name="prepare",
    )(
        pltpu.with_memory_space_constraint(east_face, pltpu.HBM),
        pltpu.with_memory_space_constraint(seam_turn, pltpu.HBM),
    )
    if row_count == 2:
        before = lax.ppermute(rows, "row", [(0, 1), (1, 0)])
        after = before
    elif row_count > 2:
        up = [(i, i + 1) for i in range(row_count - 1)]
        before = lax.ppermute(rows[:, depth:], "row", up)
        after = lax.ppermute(rows[:, :depth], "row", [(j, i) for i, j in up])
    else:
        before = after = rows
    extended, outer, inner = pl.pallas_call(
        functools.partial(extend_kernel, geom),
        out_shape=(
            shape((2, window, LANES), f32),
            shape((packed_rows(window), LANES), f32),
            shape((packed_rows(window), LANES), f32),
        ),
        in_specs=[VMEM_SPEC] * 3,
        out_specs=(VMEM_SPEC,) * 3,
        compiler_params=params,
        name="extend",
    )(field, before, after)

    def finish(seam, beside):
        partial, edges = pl.pallas_call(
            functools.partial(inner_kernel, geom),
            out_shape=(
                shape((3, 2 * window, LANES), f32),
                shape((2, window, LANES), f32),
            ),
            in_specs=[VMEM_SPEC] * 2,
            out_specs=(VMEM_SPEC,) * 2,
            scratch_shapes=[
                pltpu.VMEM((2, window + 2 * SUBLANES, LANES), f32),
                pltpu.VMEM((2, 4 * window, LANES), bf16),
            ],
            compiler_params=params,
            name="inner",
        )(extended, x_taps)
        return pl.pallas_call(
            functools.partial(filter_kernel, geom),
            out_shape=shape((n_rows // COARSE, 2, n_cols // COARSE), f32),
            in_specs=[VMEM_SPEC] * 8,
            out_specs=VMEM_SPEC,
            scratch_shapes=[
                pltpu.VMEM((2, window + 2 * SUBLANES, LANES), f32),
                pltpu.VMEM((2, 4 * window, LANES), bf16),
                pltpu.VMEM((2, 3, window, wide), bf16),
                pltpu.VMEM((2, n_rows, LANES), f32),
            ],
            compiler_params=params,
            name="filter",
        )(seam, beside, edges, partial, wet, turn, x_taps, y_taps)

    forcing = exchange(order, east_face, outer, inner, finish)
    return jnp.transpose(forcing, (1, 0, 2))


def solution(mesh):
    placed = (
        P(None, ("grp", "row"), ("tile", "sub")),
        P(("grp", "row"), ("tile", "sub")),
        P(),
        P(),
    )
    return jax.shard_map(
        on_device,
        mesh=mesh,
        in_specs=placed,
        out_specs=P(None, ("grp", "row"), ("tile", "sub")),
        check_vma=False,
    )
```

```python
import functools
import itertools

import jax
import jax.numpy as jnp
import numpy as np
from jax import lax
from jax.experimental import pallas as pl
from jax.experimental.pallas import tpu as pltpu
from jax.sharding import PartitionSpec as P

R = 32
RIM = R + 1
BITS = 30
COARSE = 4
LANES = 128
HALF = LANES // 2
GROUPS = 3
GROUP = 40
SUBLANES = 8
SWITCHED_FACES = 4

deriv_scale = 8.0

f32 = jnp.float32
bf16 = jnp.bfloat16


def up_to(value, step):
    return -(-value // step) * step


def iota(shape, dim):
    return lax.broadcasted_iota(jnp.int32, shape, dim)


def split(value):
    high = value.astype(bf16)
    return high, (value - high.astype(f32)).astype(bf16)


def dot(left, right):
    return jnp.dot(left, right, preferred_element_type=f32)


def taps_sum():
    taps = np.arange(-R, R + 1, dtype=np.float64)
    return float(np.sum(np.exp(-0.5 * (taps / R) ** 2)))


def gaussian(distance, inside):
    inside = inside & (distance >= -R) & (distance <= R)
    scaled = distance.astype(f32) * (1.0 / R)
    return jnp.where(inside, jnp.exp(-0.5 * scaled * scaled) * (1.0 / taps_sum()), 0.0)


def roll(value, shift):
    shift = shift % LANES
    return pltpu.roll(value, shift, axis=1) if shift else value


def fetch(pairs, sems):
    copies = [pltpu.make_async_copy(a, b, sems.at[i]) for i, (a, b) in enumerate(pairs)]
    for copy in copies:
        copy.start()
    for copy in copies:
        copy.wait()


def mask_kernel(geom, velocity, wet_bits, field, rows, wet, vel, packed, sems):
    n_rows, n_cols, depth, row_count, _ = geom
    fetch(((velocity, vel), (wet_bits, packed)), sems)
    at = iota((n_rows, n_cols), 0)
    word = jnp.broadcast_to(packed[0:1, :], (n_rows, n_cols))
    shift = at
    for j in range(1, n_rows // BITS):
        line = jnp.broadcast_to(packed[j : j + 1, :], (n_rows, n_cols))
        later = at >= j * BITS
        word = jnp.where(later, line, word)
        shift = jnp.where(later, at - j * BITS, shift)
    mask = (jnp.right_shift(word, shift) & 1).astype(f32)
    margin = jnp.zeros((n_rows, LANES - n_cols), f32)
    wet[:, :n_cols] = mask
    wet[:, n_cols:] = margin
    row_at = lax.axis_index("row")
    for c in range(2):
        value = jnp.concatenate([vel[c] * mask, margin], axis=1)
        field[c] = value
        if row_count == 2:
            rows[c] = jnp.where(row_at == 0, value[n_rows - depth :], value[:depth])
        elif row_count > 2:
            rows[c, :depth] = value[:depth]
            rows[c, depth:] = value[n_rows - depth :]


def seam_order(faces):
    count = faces.shape[0]
    order = jnp.int32(0)
    for i in range(count):
        smaller = jnp.int32(0)
        for j in range(i + 1, count):
            smaller = smaller + jnp.where(faces[j] < faces[i], 1, 0)
        order = order * (count - i) + smaller
    return order


def prepare_kernel(
    geom, east_face, seam_turn, order, turn, x_taps, y_taps, faces, turns, sems
):
    n_rows, n_cols, depth, row_count, window = geom
    copies = [
        pltpu.make_async_copy(east_face, faces, sems.at[0]),
        pltpu.make_async_copy(seam_turn, turns, sems.at[1]),
    ]
    for copy in copies:
        copy.start()
    row_at = lax.axis_index("row")
    lane = iota((2 * LANES, LANES), 0)
    target = iota((2 * LANES, LANES), 1)
    rim = lane - LANES
    column = jnp.where(
        lane < LANES, lane, jnp.where(rim < HALF - 1, rim - RIM, rim - HALF + n_cols)
    )
    inside = (
        ((lane >= 1) & (lane < n_cols - 1))
        | ((rim >= 0) & (rim <= RIM))
        | ((rim >= HALF - 1) & (rim < HALF + RIM))
    )
    inside = inside & (target < n_cols)
    away = column - target
    value = split(gaussian(away, inside))
    slope = split(gaussian(away - 1, inside) - gaussian(away + 1, inside))
    for i, taps in enumerate((slope[1], value[1], value[0], slope[0])):
        x_taps[:, i * LANES : (i + 1) * LANES] = taps
    out_rows = up_to(n_rows, 2 * SUBLANES)
    source = iota((out_rows, window), 1)
    target = iota((out_rows, window), 0)
    start = row_start(geom, row_at)
    world = source - start + row_at * n_rows
    last = row_count * n_rows

    def taps_at(step):
        at = world + step
        inside = (at >= 0) & (at < last) & (target < n_rows)
        return gaussian(source + step - start - target, inside)

    value = split(taps_at(0))
    slope = split(taps_at(-1) - taps_at(1))
    for i, taps in enumerate((slope[1], slope[0], value[0], value[1])):
        y_taps[i * out_rows : (i + 1) * out_rows, :] = taps
    for copy in copies:
        copy.wait()
    order[0] = seam_order(faces) if faces.shape[0] <= SWITCHED_FACES else jnp.int32(0)
    write_turn(faces, turns, turn)


def write_turn(faces, turns, turn):
    tile_at = lax.axis_index("tile")
    back = jnp.int32(0)
    for w in range(faces.shape[0]):
        back = jnp.where(faces[w] == tile_at, turns[w], back)
    sub_at = lax.axis_index("sub")
    quarter = jnp.where(sub_at == 0, (4 - back) % 4, turns[tile_at])
    cosine = jnp.where(quarter == 0, 1.0, jnp.where(quarter == 2, -1.0, 0.0)).astype(f32)
    sine = jnp.where(quarter == 1, 1.0, jnp.where(quarter == 3, -1.0, 0.0)).astype(f32)
    row = iota((SUBLANES, LANES), 0)
    lane = iota((SUBLANES, LANES), 1)
    seam_lane = seam_side(lane, sub_at)
    turn[...] = jnp.where(
        row == 0, jnp.where(seam_lane, cosine, 1.0), jnp.where(seam_lane, sine, 0.0)
    )


def seam_side(lane, sub_at):
    edge = jnp.where(sub_at == 0, RIM, LANES)
    start = jnp.where(sub_at == 0, 0, HALF)
    return (lane >= start) & (lane < edge)


def packed_rows(window):
    return up_to(-(-2 * window // GROUPS), SUBLANES)


def pieces(window):
    size = packed_rows(window)
    cuts = sorted({0, window, 2 * window, *(size * g for g in range(1, GROUPS))})
    return [
        (a // window, a % window, a // size, a % size, b - a) for a, b in zip(cuts, cuts[1:])
    ]


def row_start(geom, row_at):
    _, _, depth, row_count, _ = geom
    if row_count == 2:
        return jnp.where(row_at == 0, 0, depth)
    return jnp.int32(depth if row_count > 2 else 0)


def extend_kernel(geom, field, before, after, extended, outer, inner):
    n_rows, n_cols, depth, row_count, window = geom
    row_at = lax.axis_index("row")
    whole = []
    for c in range(2):
        mine = field[c]
        if row_count == 2:
            other = before[c]
            value = jnp.where(
                row_at == 0,
                jnp.concatenate([mine, other], axis=0),
                jnp.concatenate([other, mine], axis=0),
            )
        elif row_count > 2:
            value = jnp.concatenate([before[c], mine, after[c]], axis=0)
        else:
            value = mine
        extended[c] = value
        whole.append(value)
    first = lax.axis_index("sub") == 0
    west, east = pack(whole, window, (0, n_cols - RIM))
    outer[...] = jnp.where(first, west, east)
    inner[...] = jnp.where(first, east, west)


def pad_rows(padded, c, window, value):
    blank = jnp.zeros((SUBLANES, LANES), f32)
    padded[c, :SUBLANES, :] = blank
    padded[c, SUBLANES + window :, :] = blank
    padded[c, SUBLANES : SUBLANES + window, :] = value


def channels(padded, columns, window):
    vel = [padded[c, SUBLANES : SUBLANES + window, :] for c in range(2)]
    for c in range(2):
        grad_x = roll(vel[c], -1) - roll(vel[c], 1)
        grad_y = (
            padded[c, SUBLANES + 1 : SUBLANES + 1 + window, :]
            - padded[c, SUBLANES - 1 : SUBLANES - 1 + window, :]
        )
        advect = vel[0] * grad_x + vel[1] * grad_y
        for at, value in ((c, vel[c]), (2 + c, advect)):
            high, low_part = split(value)
            columns[0, at * window : (at + 1) * window, :] = high
            columns[1, at * window : (at + 1) * window, :] = low_part


def across_x(columns, x_taps, window):
    wide = 2 * LANES
    high = x_taps[:, wide:]
    low_part = x_taps[:, :wide]
    both = x_taps[:, LANES : LANES + wide]
    main = dot(columns[0, : 2 * window, :], high)
    more = dot(columns[1, : 2 * window, :], high)
    rest = dot(columns[0, : 2 * window, :], low_part)
    flux = dot(columns[0, 2 * window :, :], both)
    flux_more = dot(columns[1, 2 * window :, :], both[:, LANES:])
    means = main[:, :LANES] + (more[:, :LANES] + rest[:, LANES:])
    slopes = main[:, LANES:] + (more[:, LANES:] + rest[:, :LANES])
    fluxes = flux[:, LANES:] + (flux_more + flux[:, :LANES])
    return means, slopes, fluxes


def inner_kernel(geom, extended, x_taps, partial, edges, padded, columns):
    n_rows, n_cols, depth, row_count, window = geom
    lane = iota((window, LANES), 1)
    for c in range(2):
        own = extended[c]
        pad_rows(padded, c, window, own)
        near = jnp.where(lane < RIM + 2, roll(own, RIM), roll(own, HALF - n_cols))
        edges[c] = near
    channels(padded, columns, window)
    for pair, value in enumerate(across_x(columns, x_taps[:LANES, :], window)):
        partial[pair] = value


def filter_kernel(
    geom,
    seam,
    beside,
    edges,
    partial,
    wet,
    turn,
    x_taps,
    y_taps,
    forcing,
    padded,
    columns,
    along,
    pools,
):
    n_rows, n_cols, depth, row_count, window = geom
    sub_at = lax.axis_index("sub")
    out_rows = up_to(n_rows, 2 * SUBLANES)
    west = jnp.where(sub_at == 0, seam[...], beside[...])
    east = jnp.where(sub_at == 0, beside[...], seam[...])
    turned = unpack(west, east, window, turn)
    lane = iota((window, LANES), 1)
    own = (lane >= RIM) & (lane < HALF)
    for c in range(2):
        pad_rows(padded, c, window, jnp.where(own, edges[c], turned[c]))
    channels(padded, columns, window)
    for pair, value in enumerate(across_x(columns, x_taps[LANES:, :], window)):
        value = value + partial[pair]
        high, low_part = split(value)
        for c in range(2):
            at = slice(c * LANES, (c + 1) * LANES)
            along[0, pair, :, at] = high[c * window : (c + 1) * window]
            along[1, pair, :, at] = low_part[c * window : (c + 1) * window]

    main = dot(y_taps[...], along[0, 0])
    more = dot(y_taps[out_rows : 3 * out_rows, :], along[1, 0])
    slope_y = main[out_rows : 2 * out_rows] + (main[:out_rows] + more[:out_rows])
    mean = main[2 * out_rows : 3 * out_rows] + (main[3 * out_rows :] + more[out_rows:])

    def across(pair):
        main = dot(y_taps[2 * out_rows :, :], along[0, pair])
        more = dot(y_taps[2 * out_rows : 3 * out_rows, :], along[1, pair])
        return main[:out_rows] + (main[out_rows:] + more)

    slope_x = across(1)
    flux = across(2)
    mean_u = mean[:n_rows, :LANES]
    mean_v = mean[:n_rows, LANES:]
    mask = wet[...]
    coarse = n_rows // COARSE
    for c in range(2):
        at = slice(c * LANES, (c + 1) * LANES)
        pools[c] = mask * (
            flux[:n_rows, at] - (mean_u * slope_x[:n_rows, at] + mean_v * slope_y[:n_rows, at])
        )
    block = iota((LANES, LANES), 0) // COARSE == iota((LANES, LANES), 1)
    gather = jnp.where(block, deriv_scale / (COARSE * COARSE), 0.0).astype(bf16)
    for c in range(2):
        rows = [pools[c, pl.ds(k, coarse, stride=COARSE), :] for k in range(COARSE)]
        high, low_part = split((rows[0] + rows[1]) + (rows[2] + rows[3]))
        value = dot(high, gather) + dot(low_part, gather)
        forcing[:, c, :] = value[:, : n_cols // COARSE]


EDGE = 4


def np_split(value):
    high = value.astype(bf16)
    return high, (value - high.astype(np.float64)).astype(bf16)


def np_gaussian(distance):
    inside = np.abs(distance) <= R
    return np.where(inside, np.exp(-0.5 * (distance / R) ** 2) / taps_sum(), 0.0)


def x_constant(n_cols):
    lane = np.arange(2 * LANES)[:, None]
    target = np.arange(LANES)[None, :]
    rim = lane - LANES
    column = np.where(
        lane < LANES, lane, np.where(rim < HALF - 1, rim - RIM, rim - HALF + n_cols)
    )
    inside = (
        ((lane >= 1) & (lane < n_cols - 1))
        | ((rim >= 0) & (rim <= RIM))
        | ((rim >= HALF - 1) & (rim < HALF + RIM))
    )
    inside = inside & (target < n_cols)
    away = column - target
    value = np_split(np.where(inside, np_gaussian(away), 0.0))
    slope = np_split(np.where(inside, np_gaussian(away - 1) - np_gaussian(away + 1), 0.0))
    high, low_part = (np.concatenate([value[k], slope[k]], axis=1) for k in range(2))
    return np.concatenate([high, high, low_part], axis=0)


def y_constant(target, source, used, first_row, last_row):
    def step(by):
        at = source + by
        inside = used & (at >= first_row) & (at < last_row)
        return np.where(inside[None, :], np_gaussian(at[None, :] - target[:, None]), 0.0)

    value = np_split(step(0))
    slope = np_split(step(-1) - step(1))
    pad = ((0, up_to(target.shape[0], 2 * SUBLANES) - target.shape[0]), (0, 0))
    high, low_part = (
        np.concatenate([np.pad(slope[k], pad), np.pad(value[k], pad)], axis=0)
        for k in range(2)
    )
    return np.concatenate([high, high, low_part], axis=1)


def y_constants(n_rows, depth, near):
    source = np.arange(up_to(n_rows, 2 * SUBLANES))
    own = y_constant(np.arange(n_rows), source, source < n_rows, 0, n_rows)
    tail = []
    for row_at in range(2):
        source = np.arange(near + depth)
        source = source + n_rows - near if row_at == 0 else source - depth
        late = source >= n_rows - EDGE if row_at == 0 else source < EDGE
        target = np.arange(depth) + (n_rows - depth if row_at == 0 else 0)
        tail.append(
            y_constant(target, source, late, -row_at * n_rows, (2 - row_at) * n_rows)
        )
    return own, np.stack(tail)


def start_all(pairs, sems):
    copies = [pltpu.make_async_copy(a, b, sems.at[i]) for i, (a, b) in enumerate(pairs)]
    for copy in copies:
        copy.start()
    return copies


def pack(whole, rows, bases):
    size = packed_rows(rows)
    lane = iota((size, LANES), 1)
    groups = [[] for _ in range(GROUPS)]
    for c, row, group, _, count in pieces(rows):
        groups[group].append(whole[c][row : row + count])
    spare = GROUPS * size - 2 * rows
    if spare:
        groups[-1].append(jnp.zeros((spare, LANES), f32))
    groups = [jnp.concatenate(group, axis=0) for group in groups]
    out = []
    for base in bases:
        value = roll(groups[-1], (GROUPS - 1) * GROUP - base)
        for g in reversed(range(GROUPS - 1)):
            value = jnp.where(lane < (g + 1) * GROUP, roll(groups[g], g * GROUP - base), value)
        out.append(value)
    return out


def unpack(west, east, rows, turn, only=None):
    parts = [[], []]
    start, stop = only or (0, rows)
    for c, first, group, row, count in pieces(rows):
        row = row + max(start - first, 0)
        count = min(first + count, stop) - max(first, start)
        if count <= 0:
            continue
        low = iota((count, LANES), 1) < HALF
        parts[c].append(
            jnp.where(
                low,
                roll(west[row : row + count, :], -group * GROUP),
                roll(east[row : row + count, :], HALF - group * GROUP),
            )
        )
    u, v = (jnp.concatenate(part, axis=0) for part in parts)
    cosine = turn[0:1, :]
    sine = turn[1:2, :]
    return cosine * u - sine * v, sine * u + cosine * v


def with_own(turned, mine, n_cols):
    lane = iota(mine.shape, 1)
    near = jnp.where(lane < RIM + 2, roll(mine, RIM), roll(mine, HALF - n_cols))
    return jnp.where((lane >= RIM) & (lane < HALF), near, turned)


def open_kernel(
    geom,
    velocity,
    wet_bits,
    east_face,
    seam_turn,
    field,
    outer,
    inner,
    wet,
    turn,
    order,
    vel,
    packed,
    faces,
    turns,
    sems,
):
    n_rows, n_cols, _, _ = geom
    copies = start_all(
        (
            (wet_bits, packed),
            (velocity, vel),
            (east_face, faces),
            (seam_turn, turns),
        ),
        sems,
    )
    copies[0].wait()
    at = iota((n_rows, n_cols), 0)
    word = jnp.broadcast_to(packed[0:1, :], (n_rows, n_cols))
    shift = at
    for j in range(1, n_rows // BITS):
        line = jnp.broadcast_to(packed[j : j + 1, :], (n_rows, n_cols))
        later = at >= j * BITS
        word = jnp.where(later, line, word)
        shift = jnp.where(later, at - j * BITS, shift)
    mask = (jnp.right_shift(word, shift) & 1).astype(f32)
    margin = jnp.zeros((n_rows, LANES - n_cols), f32)
    wet[:, :n_cols] = mask
    wet[:, n_cols:] = margin
    for copy in copies[1:]:
        copy.wait()
    order[0] = seam_order(faces)
    whole = []
    for c in range(2):
        value = jnp.concatenate([vel[c] * mask, margin], axis=1)
        field[c] = value
        whole.append(value)
    west, east = pack(whole, n_rows, (0, n_cols - RIM))
    first = lax.axis_index("sub") == 0
    outer[...] = jnp.where(first, west, east)
    inner[...] = jnp.where(first, east, west)
    write_turn(faces, turns, turn)


def corner_pieces():
    size = corner_rows()
    cuts = sorted({*range(0, 5 * RIM, RIM), *(size * g for g in range(1, GROUPS))})
    return [
        (a // (2 * RIM), a // RIM % 2, a % RIM, a // size, a % size, b - a)
        for a, b in zip(cuts, cuts[1:])
    ]


def corner_rows():
    return -(-4 * RIM // GROUPS)


def edge_size():
    return up_to(2 * RIM + corner_rows(), SUBLANES)


def edge_kernel(geom, seam, beside, field, turn, edge, west, east, groups):
    n_rows, n_cols, depth, _ = geom
    row_at = lax.axis_index("row")
    first = lax.axis_index("sub") == 0
    west[...] = jnp.where(first, seam[...], beside[...])
    east[...] = jnp.where(first, beside[...], seam[...])
    ends = [
        unpack(west, east, n_rows, turn, only)
        for only in ((n_rows - depth, n_rows), (0, depth))
    ]
    corners = []
    for c in range(2):
        mine = facing(row_at, field[c], depth)
        rims = with_own(jnp.where(row_at == 0, ends[0][c], ends[1][c]), mine, n_cols)
        mine, rims = (
            jnp.where(row_at == 0, value[depth - RIM :], value[:RIM]) for value in (mine, rims)
        )
        edge[c * RIM : (c + 1) * RIM, :] = mine
        corners.append(rims)
    for c, side, row, group, at, count in corner_pieces():
        groups[group, at : at + count, :] = roll(
            corners[c][row : row + count], group * GROUP - side * (HALF - 2)
        )
    size = corner_rows()
    lane = iota((size, LANES), 1)
    value = groups[GROUPS - 1, :size, :]
    for g in reversed(range(GROUPS - 1)):
        value = jnp.where(lane < (g + 1) * GROUP, groups[g, :size, :], value)
    edge[2 * RIM : 2 * RIM + size, :] = value


def facing(row_at, value, depth):
    return jnp.where(row_at == 0, value[value.shape[0] - depth :], value[:depth])


def lay_columns(padded, columns, half, size):
    wide = 2 * LANES
    vel = [padded[c, SUBLANES : SUBLANES + size, :] for c in range(2)]
    for c in range(2):
        grad_x = roll(vel[c], -1) - roll(vel[c], 1)
        grad_y = (
            padded[c, SUBLANES + 1 : SUBLANES + 1 + size, :]
            - padded[c, SUBLANES - 1 : SUBLANES - 1 + size, :]
        )
        advect = vel[0] * grad_x + vel[1] * grad_y
        for at, value in ((c, vel[c]), (2 + c, advect)):
            high, low_part = split(value)
            rows = slice(at * size, (at + 1) * size)
            for k, part in enumerate((high, low_part, high)):
                start = k * wide + half * LANES
                columns[rows, start : start + LANES] = part


def sum_columns(columns, x_taps, size):
    both = dot(columns[: 2 * size, :], x_taps[...])
    flux = dot(columns[2 * size :, :], x_taps[:, :LANES])
    return both[:, :LANES], both[:, LANES:], flux


def keep_along(along, pair, value, size):
    high, low_part = split(value)
    for c in range(2):
        at = slice(c * LANES, (c + 1) * LANES)
        rows = slice(c * size, (c + 1) * size)
        for k, part in enumerate((high, low_part, high)):
            along[pair, k * size : (k + 1) * size, at] = part[rows]


def across_y(y_taps, along, size):
    both = dot(y_taps[...], along[0])
    slope_x = dot(y_taps[size:, :], along[1])
    flux = dot(y_taps[size:, :], along[2])
    return both[:size], both[size:], slope_x, flux


def pool(smooth, mask, pools):
    slope_y, mean, slope_x, flux = smooth
    count = mask.shape[0]
    mean_u = mean[:, :LANES]
    mean_v = mean[:, LANES:]
    block = iota((LANES, LANES), 0) // COARSE == iota((LANES, LANES), 1)
    gather = jnp.where(block, deriv_scale / (COARSE * COARSE), 0.0).astype(bf16)
    out = []
    for c in range(2):
        at = slice(c * LANES, (c + 1) * LANES)
        pools[c] = mask * (flux[:, at] - (mean_u * slope_x[:, at] + mean_v * slope_y[:, at]))
        rows = [
            pools[c, pl.ds(k, count // COARSE, stride=COARSE), :] for k in range(COARSE)
        ]
        high, low_part = split((rows[0] + rows[1]) + (rows[2] + rows[3]))
        out.append(dot(high, gather) + dot(low_part, gather))
    return out


def own_kernel(
    geom,
    west,
    east,
    field,
    turn,
    wet,
    x_source,
    y_source,
    tail_source,
    part,
    tail,
    tail_wet,
    tail_rims,
    x_taps,
    tail_taps,
    padded,
    columns,
    along,
    pools,
    y_taps,
    sems,
):
    n_rows, n_cols, depth, near = geom
    row_at = lax.axis_index("row")
    copies = start_all(
        ((x_source, x_taps), (y_source, y_taps), (tail_source.at[row_at], tail_taps)), sems
    )
    size = up_to(n_rows, 2 * SUBLANES)
    blank = jnp.zeros((size - n_rows, LANES), f32)
    turned = unpack(west, east, n_rows, turn)
    for c in range(2):
        mine = field[c]
        rims = with_own(turned[c], mine, n_cols)
        tail_rims[c] = facing(row_at, rims, near)
        for half, value in enumerate((mine, rims)):
            if size > n_rows:
                value = jnp.concatenate([value, blank], axis=0)
            pad_rows(padded.at[half], c, size, value)
    for half in range(2):
        lay_columns(padded.at[half], columns, half, size)
    for copy in copies:
        copy.wait()
    at = iota((2 * size, LANES), 0) % size
    early = jnp.where(row_at == 0, 0, EDGE)
    late = jnp.where(row_at == 0, n_rows - EDGE, n_rows)
    kept = (at >= early) & (at < late)
    for pair, value in enumerate(sum_columns(columns, x_taps, size)):
        keep_along(along, pair, jnp.where(kept, value, 0.0), size)
    smooth = [value[:n_rows] for value in across_y(y_taps, along, size)]
    mask = wet[...]
    for i, value in enumerate(smooth):
        tail[i] = facing(row_at, value, depth)
    tail_wet[...] = facing(row_at, mask, depth)
    for c, value in enumerate(pool(smooth, mask, pools)):
        part[:, c, :] = value[:, : n_cols // COARSE]


def close_kernel(
    geom,
    edge,
    field,
    part,
    tail,
    tail_wet,
    tail_rims,
    x_taps,
    tail_taps,
    forcing,
    padded,
    columns,
    along,
    pools,
):
    n_rows, n_cols, depth, near = geom
    row_at = lax.axis_index("row")
    size = near + depth
    sides = {}
    for c, side, _, group, at, count in corner_pieces():
        at = at + 2 * RIM
        piece = roll(edge[at : at + count, :], side * (HALF - 2) - group * GROUP)
        sides.setdefault((c, side), []).append(piece)
    for c in range(2):
        ones = [jnp.concatenate(sides[c, side], axis=0) for side in range(2)]
        low = iota((RIM, LANES), 1) < RIM + 2
        for half, (own, far) in enumerate(
            (
                (facing(row_at, field[c], near), edge[c * RIM : (c + 1) * RIM, :]),
                (tail_rims[c], jnp.where(low, ones[0], ones[1])),
            )
        ):
            spare = jnp.zeros((depth - RIM, LANES), f32)
            value = jnp.where(
                row_at == 0,
                jnp.concatenate([own, far, spare], axis=0),
                jnp.concatenate([spare, far, own], axis=0),
            )
            pad_rows(padded.at[half], c, size, value)
    for half in range(2):
        lay_columns(padded.at[half], columns, half, size)
    for pair, value in enumerate(sum_columns(columns, x_taps, size)):
        keep_along(along, pair, value, size)
    smooth = across_y(tail_taps, along, up_to(depth, 2 * SUBLANES))
    smooth = [value[:depth] + tail[i] for i, value in enumerate(smooth)]
    forcing[...] = part[...]
    start = jnp.where(row_at == 0, (n_rows - depth) // COARSE, 0)
    for c, value in enumerate(pool(smooth, tail_wet[...], pools)):
        forcing[pl.ds(start, depth // COARSE), c, :] = value[:, : n_cols // COARSE]


VMEM_SPEC = pl.BlockSpec(memory_space=pltpu.VMEM)
SMEM_SPEC = pl.BlockSpec(memory_space=pltpu.SMEM)
HBM_SPEC = pl.BlockSpec(memory_space=pltpu.HBM)


def choose(index, branches, *operands):
    closed = jax.make_jaxpr(lambda i, *rest: lax.switch(i, branches, *rest))(index, *operands)
    values = dict(zip(closed.jaxpr.constvars, closed.consts))
    values.update(zip(closed.jaxpr.invars, jax.tree.leaves((index, *operands))))

    def read(atom):
        return atom.val if hasattr(atom, "val") else values[atom]

    for eqn in closed.jaxpr.eqns:
        taken = [read(atom) for atom in eqn.invars]
        if eqn.primitive is lax.clamp_p:
            given = taken[1]
        else:
            given = eqn.primitive.bind(*taken, **eqn.params)
        if not eqn.primitive.multiple_results:
            given = [given]
        values.update(zip(eqn.outvars, given))
    return [read(atom) for atom in closed.jaxpr.outvars]


def seam_pairs(order, subs):
    pairs = []
    for west, east in enumerate(order):
        pairs += [(west * subs + subs - 1, east * subs), (east * subs, west * subs + subs - 1)]
    return pairs


def beside_pairs(subs):
    return [(i, subs - 1 - i) for i in range(subs)]


def exchange(order, east_face, outer, inner, finish):
    faces = east_face.shape[0]
    subs = lax.axis_size("sub")
    beside = beside_pairs(subs)

    def swap(order, outer, inner):
        seam = lax.ppermute(outer, ("tile", "sub"), seam_pairs(order, subs))
        return finish(seam, lax.ppermute(inner, "sub", beside))

    if faces <= SWITCHED_FACES:
        orders = itertools.permutations(range(faces))
        branches = [functools.partial(swap, order) for order in orders]
        return lax.switch(order[0], branches, outer, inner)
    tile_at = lax.axis_index("tile")
    sub_at = lax.axis_index("sub")
    west = jnp.sum(jnp.where(east_face == tile_at, jnp.arange(faces, dtype=jnp.int32), 0))
    east = lax.dynamic_index_in_dim(east_face, tile_at, 0, keepdims=False)
    gathered = lax.all_gather(lax.ppermute(outer, "sub", beside), "tile")
    partner = jnp.where(sub_at == 0, west, east)
    seam = lax.dynamic_index_in_dim(gathered, partner, 0, keepdims=False)
    return finish(seam, lax.ppermute(inner, "sub", beside))


def in_hbm(value):
    return pltpu.with_memory_space_constraint(value, pltpu.HBM)


def paired(velocity, wet_bits, east_face, seam_turn):
    _, n_rows, n_cols = velocity.shape
    depth = up_to(RIM, SUBLANES)
    near = up_to(depth + SUBLANES, 2 * SUBLANES) - depth
    geom = (n_rows, n_cols, depth, near)
    size = up_to(n_rows, 2 * SUBLANES)
    end = near + depth
    wide = 2 * LANES
    coarse = n_rows // COARSE
    params = pltpu.CompilerParams(vmem_limit_bytes=16 << 20)
    shape = jax.ShapeDtypeStruct
    kernel = lambda body, name, **rest: pl.pallas_call(
        functools.partial(body, geom), name=name, compiler_params=params, **rest
    )
    packed = shape((packed_rows(n_rows), LANES), f32)
    own_taps, tail_taps = y_constants(n_rows, depth, near)
    taps = (x_constant(n_cols), own_taps, tail_taps)
    field, outer, inner, wet, turn, order = kernel(
        open_kernel,
        "open",
        out_shape=(
            shape((2, n_rows, LANES), f32),
            packed,
            packed,
            shape((n_rows, LANES), f32),
            shape((SUBLANES, LANES), f32),
            pltpu.SMEM((1,), jnp.int32),
        ),
        in_specs=[HBM_SPEC] * 4,
        out_specs=(VMEM_SPEC,) * 5 + (SMEM_SPEC,),
        scratch_shapes=[
            pltpu.VMEM(velocity.shape, f32),
            pltpu.VMEM(wet_bits.shape, jnp.int32),
            pltpu.SMEM(east_face.shape, jnp.int32),
            pltpu.SMEM(seam_turn.shape, jnp.int32),
            pltpu.SemaphoreType.DMA((4,)),
        ],
    )(*(in_hbm(value) for value in (velocity, wet_bits, east_face, seam_turn)))
    subs = lax.axis_size("sub")
    part_shape = shape((coarse, 2, n_cols // COARSE), f32)

    def branch(order, outer, inner, field, turn):
        seam = lax.ppermute(outer, ("tile", "sub"), seam_pairs(order, subs))
        beside = lax.ppermute(inner, "sub", beside_pairs(subs))
        return kernel(
            edge_kernel,
            "edge",
            out_shape=(
                shape((edge_size(), LANES), f32),
                packed,
                packed,
            ),
            in_specs=[VMEM_SPEC] * 4,
            out_specs=(VMEM_SPEC,) * 3,
            scratch_shapes=[
                pltpu.VMEM((GROUPS, up_to(corner_rows(), SUBLANES), LANES), f32)
            ],
        )(seam, beside, field, turn)

    orders = itertools.permutations(range(east_face.shape[0]))
    branches = [functools.partial(branch, order) for order in orders]
    edge, west, east = choose(order[0], branches, outer, inner, field, turn)
    edge = lax.ppermute(edge, "row", [(0, 1), (1, 0)])
    part, tail, tail_wet, tail_rims, x_taps, tail_taps = kernel(
        own_kernel,
        "own",
        out_shape=(
            part_shape,
            shape((4, depth, wide), f32),
            shape((depth, LANES), f32),
            shape((2, near, LANES), f32),
            shape(taps[0].shape, bf16),
            shape(taps[2].shape[1:], bf16),
        ),
        in_specs=[VMEM_SPEC] * 5 + [HBM_SPEC] * 3,
        out_specs=(VMEM_SPEC,) * 6,
        scratch_shapes=[
            pltpu.VMEM((2, 2, size + 2 * SUBLANES, LANES), f32),
            pltpu.VMEM((4 * size, 3 * wide), bf16),
            pltpu.VMEM((3, 3 * size, wide), bf16),
            pltpu.VMEM((2, n_rows, LANES), f32),
            pltpu.VMEM(taps[1].shape, bf16),
            pltpu.SemaphoreType.DMA((3,)),
        ],
        cost_estimate=pl.CostEstimate(
            flops=1 << 30, bytes_accessed=1 << 22, transcendentals=0
        ),
    )(west, east, field, turn, wet, *(in_hbm(jnp.asarray(value)) for value in taps))
    forcing = kernel(
        close_kernel,
        "close",
        out_shape=part_shape,
        in_specs=[VMEM_SPEC] * 8,
        out_specs=VMEM_SPEC,
        scratch_shapes=[
            pltpu.VMEM((2, 2, end + 2 * SUBLANES, LANES), f32),
            pltpu.VMEM((4 * end, 3 * wide), bf16),
            pltpu.VMEM((3, 3 * end, wide), bf16),
            pltpu.VMEM((2, depth, LANES), f32),
        ],
    )(edge, field, part, tail, tail_wet, tail_rims, x_taps, tail_taps)
    return jnp.transpose(forcing, (1, 0, 2))


def on_device(velocity, wet_bits, east_face, seam_turn):
    _, n_rows, n_cols = velocity.shape
    row_count = lax.axis_size("row")
    if row_count == 2 and east_face.shape[0] <= SWITCHED_FACES:
        return paired(velocity, wet_bits, east_face, seam_turn)
    depth = up_to(RIM, SUBLANES)
    sides = min(row_count - 1, 2)
    window = n_rows + sides * depth
    geom = (n_rows, n_cols, depth, row_count, window)
    sent = depth * max(sides, 1)
    wide = 2 * LANES
    out_rows = up_to(n_rows, 2 * SUBLANES)
    params = pltpu.CompilerParams(vmem_limit_bytes=16 << 20)
    shape = jax.ShapeDtypeStruct
    field, rows, wet = pl.pallas_call(
        functools.partial(mask_kernel, geom),
        out_shape=(
            shape((2, n_rows, LANES), f32),
            shape((2, sent, LANES), f32),
            shape((n_rows, LANES), f32),
        ),
        in_specs=[HBM_SPEC] * 2,
        out_specs=(VMEM_SPEC,) * 3,
        scratch_shapes=[
            pltpu.VMEM(velocity.shape, f32),
            pltpu.VMEM(wet_bits.shape, jnp.int32),
            pltpu.SemaphoreType.DMA((2,)),
        ],
        compiler_params=params,
        name="mask",
    )(
        pltpu.with_memory_space_constraint(velocity, pltpu.HBM),
        pltpu.with_memory_space_constraint(wet_bits, pltpu.HBM),
    )
    order, turn, x_taps, y_taps = pl.pallas_call(
        functools.partial(prepare_kernel, geom),
        out_shape=(
            shape((1,), jnp.int32),
            shape((SUBLANES, LANES), f32),
            shape((wide, 2 * wide), bf16),
            shape((4 * out_rows, window), bf16),
        ),
        in_specs=[HBM_SPEC] * 2,
        out_specs=(SMEM_SPEC,) + (VMEM_SPEC,) * 3,
        scratch_shapes=[
            pltpu.SMEM(east_face.shape, jnp.int32),
            pltpu.SMEM(seam_turn.shape, jnp.int32),
            pltpu.SemaphoreType.DMA((2,)),
        ],
        compiler_params=params,
        name="prepare",
    )(
        pltpu.with_memory_space_constraint(east_face, pltpu.HBM),
        pltpu.with_memory_space_constraint(seam_turn, pltpu.HBM),
    )
    if row_count == 2:
        before = lax.ppermute(rows, "row", [(0, 1), (1, 0)])
        after = before
    elif row_count > 2:
        up = [(i, i + 1) for i in range(row_count - 1)]
        before = lax.ppermute(rows[:, depth:], "row", up)
        after = lax.ppermute(rows[:, :depth], "row", [(j, i) for i, j in up])
    else:
        before = after = rows
    extended, outer, inner = pl.pallas_call(
        functools.partial(extend_kernel, geom),
        out_shape=(
            shape((2, window, LANES), f32),
            shape((packed_rows(window), LANES), f32),
            shape((packed_rows(window), LANES), f32),
        ),
        in_specs=[VMEM_SPEC] * 3,
        out_specs=(VMEM_SPEC,) * 3,
        compiler_params=params,
        name="extend",
    )(field, before, after)

    def finish(seam, beside):
        partial, edges = pl.pallas_call(
            functools.partial(inner_kernel, geom),
            out_shape=(
                shape((3, 2 * window, LANES), f32),
                shape((2, window, LANES), f32),
            ),
            in_specs=[VMEM_SPEC] * 2,
            out_specs=(VMEM_SPEC,) * 2,
            scratch_shapes=[
                pltpu.VMEM((2, window + 2 * SUBLANES, LANES), f32),
                pltpu.VMEM((2, 4 * window, LANES), bf16),
            ],
            compiler_params=params,
            name="inner",
        )(extended, x_taps)
        return pl.pallas_call(
            functools.partial(filter_kernel, geom),
            out_shape=shape((n_rows // COARSE, 2, n_cols // COARSE), f32),
            in_specs=[VMEM_SPEC] * 8,
            out_specs=VMEM_SPEC,
            scratch_shapes=[
                pltpu.VMEM((2, window + 2 * SUBLANES, LANES), f32),
                pltpu.VMEM((2, 4 * window, LANES), bf16),
                pltpu.VMEM((2, 3, window, wide), bf16),
                pltpu.VMEM((2, n_rows, LANES), f32),
            ],
            compiler_params=params,
            name="filter",
        )(seam, beside, edges, partial, wet, turn, x_taps, y_taps)

    forcing = exchange(order, east_face, outer, inner, finish)
    return jnp.transpose(forcing, (1, 0, 2))


def solution(mesh):
    placed = (
        P(None, ("grp", "row"), ("tile", "sub")),
        P(("grp", "row"), ("tile", "sub")),
        P(),
        P(),
    )
    return jax.shard_map(
        on_device,
        mesh=mesh,
        in_specs=placed,
        out_specs=P(None, ("grp", "row"), ("tile", "sub")),
        check_vma=False,
    )
```

```python
import functools
import itertools

import jax
import jax.numpy as jnp
import numpy as np
from jax import lax
from jax.experimental import pallas as pl
from jax.experimental.pallas import tpu as pltpu
from jax.sharding import PartitionSpec as P

R = 32
RIM = R + 1
BITS = 30
COARSE = 4
LANES = 128
HALF = LANES // 2
GROUPS = 3
GROUP = 40
SUBLANES = 8
SWITCHED_FACES = 4

deriv_scale = 8.0

f32 = jnp.float32
bf16 = jnp.bfloat16


def up_to(value, step):
    return -(-value // step) * step


def iota(shape, dim):
    return lax.broadcasted_iota(jnp.int32, shape, dim)


def split(value):
    high = value.astype(bf16)
    return high, (value - high.astype(f32)).astype(bf16)


def dot(left, right):
    return jnp.dot(left, right, preferred_element_type=f32)


def taps_sum():
    taps = np.arange(-R, R + 1, dtype=np.float64)
    return float(np.sum(np.exp(-0.5 * (taps / R) ** 2)))


def gaussian(distance, inside):
    inside = inside & (distance >= -R) & (distance <= R)
    scaled = distance.astype(f32) * (1.0 / R)
    return jnp.where(inside, jnp.exp(-0.5 * scaled * scaled) * (1.0 / taps_sum()), 0.0)


def roll(value, shift):
    shift = shift % LANES
    return pltpu.roll(value, shift, axis=1) if shift else value


def fetch(pairs, sems):
    copies = [pltpu.make_async_copy(a, b, sems.at[i]) for i, (a, b) in enumerate(pairs)]
    for copy in copies:
        copy.start()
    for copy in copies:
        copy.wait()


def mask_kernel(geom, velocity, wet_bits, field, rows, wet, vel, packed, sems):
    n_rows, n_cols, depth, row_count, _ = geom
    fetch(((velocity, vel), (wet_bits, packed)), sems)
    at = iota((n_rows, n_cols), 0)
    word = jnp.broadcast_to(packed[0:1, :], (n_rows, n_cols))
    shift = at
    for j in range(1, n_rows // BITS):
        line = jnp.broadcast_to(packed[j : j + 1, :], (n_rows, n_cols))
        later = at >= j * BITS
        word = jnp.where(later, line, word)
        shift = jnp.where(later, at - j * BITS, shift)
    mask = (jnp.right_shift(word, shift) & 1).astype(f32)
    margin = jnp.zeros((n_rows, LANES - n_cols), f32)
    wet[:, :n_cols] = mask
    wet[:, n_cols:] = margin
    row_at = lax.axis_index("row")
    for c in range(2):
        value = jnp.concatenate([vel[c] * mask, margin], axis=1)
        field[c] = value
        if row_count == 2:
            rows[c] = jnp.where(row_at == 0, value[n_rows - depth :], value[:depth])
        elif row_count > 2:
            rows[c, :depth] = value[:depth]
            rows[c, depth:] = value[n_rows - depth :]


def seam_order(faces):
    count = faces.shape[0]
    order = jnp.int32(0)
    for i in range(count):
        smaller = jnp.int32(0)
        for j in range(i + 1, count):
            smaller = smaller + jnp.where(faces[j] < faces[i], 1, 0)
        order = order * (count - i) + smaller
    return order


def prepare_kernel(
    geom, east_face, seam_turn, order, turn, x_taps, y_taps, faces, turns, sems
):
    n_rows, n_cols, depth, row_count, window = geom
    copies = [
        pltpu.make_async_copy(east_face, faces, sems.at[0]),
        pltpu.make_async_copy(seam_turn, turns, sems.at[1]),
    ]
    for copy in copies:
        copy.start()
    row_at = lax.axis_index("row")
    lane = iota((2 * LANES, LANES), 0)
    target = iota((2 * LANES, LANES), 1)
    rim = lane - LANES
    column = jnp.where(
        lane < LANES, lane, jnp.where(rim < HALF - 1, rim - RIM, rim - HALF + n_cols)
    )
    inside = (
        ((lane >= 1) & (lane < n_cols - 1))
        | ((rim >= 0) & (rim <= RIM))
        | ((rim >= HALF - 1) & (rim < HALF + RIM))
    )
    inside = inside & (target < n_cols)
    away = column - target
    value = split(gaussian(away, inside))
    slope = split(gaussian(away - 1, inside) - gaussian(away + 1, inside))
    for i, taps in enumerate((slope[1], value[1], value[0], slope[0])):
        x_taps[:, i * LANES : (i + 1) * LANES] = taps
    out_rows = up_to(n_rows, 2 * SUBLANES)
    source = iota((out_rows, window), 1)
    target = iota((out_rows, window), 0)
    start = row_start(geom, row_at)
    world = source - start + row_at * n_rows
    last = row_count * n_rows

    def taps_at(step):
        at = world + step
        inside = (at >= 0) & (at < last) & (target < n_rows)
        return gaussian(source + step - start - target, inside)

    value = split(taps_at(0))
    slope = split(taps_at(-1) - taps_at(1))
    for i, taps in enumerate((slope[1], slope[0], value[0], value[1])):
        y_taps[i * out_rows : (i + 1) * out_rows, :] = taps
    for copy in copies:
        copy.wait()
    order[0] = seam_order(faces) if faces.shape[0] <= SWITCHED_FACES else jnp.int32(0)
    write_turn(faces, turns, turn)


def write_turn(faces, turns, turn):
    tile_at = lax.axis_index("tile")
    back = jnp.int32(0)
    for w in range(faces.shape[0]):
        back = jnp.where(faces[w] == tile_at, turns[w], back)
    sub_at = lax.axis_index("sub")
    quarter = jnp.where(sub_at == 0, (4 - back) % 4, turns[tile_at])
    cosine = jnp.where(quarter == 0, 1.0, jnp.where(quarter == 2, -1.0, 0.0)).astype(f32)
    sine = jnp.where(quarter == 1, 1.0, jnp.where(quarter == 3, -1.0, 0.0)).astype(f32)
    row = iota((SUBLANES, LANES), 0)
    lane = iota((SUBLANES, LANES), 1)
    seam_lane = seam_side(lane, sub_at)
    turn[...] = jnp.where(
        row == 0, jnp.where(seam_lane, cosine, 1.0), jnp.where(seam_lane, sine, 0.0)
    )


def seam_side(lane, sub_at):
    edge = jnp.where(sub_at == 0, RIM, LANES)
    start = jnp.where(sub_at == 0, 0, HALF)
    return (lane >= start) & (lane < edge)


def packed_rows(window):
    return up_to(-(-2 * window // GROUPS), SUBLANES)


def pieces(window):
    size = packed_rows(window)
    cuts = sorted({0, window, 2 * window, *(size * g for g in range(1, GROUPS))})
    return [
        (a // window, a % window, a // size, a % size, b - a) for a, b in zip(cuts, cuts[1:])
    ]


def row_start(geom, row_at):
    _, _, depth, row_count, _ = geom
    if row_count == 2:
        return jnp.where(row_at == 0, 0, depth)
    return jnp.int32(depth if row_count > 2 else 0)


def extend_kernel(geom, field, before, after, extended, outer, inner):
    n_rows, n_cols, depth, row_count, window = geom
    row_at = lax.axis_index("row")
    whole = []
    for c in range(2):
        mine = field[c]
        if row_count == 2:
            other = before[c]
            value = jnp.where(
                row_at == 0,
                jnp.concatenate([mine, other], axis=0),
                jnp.concatenate([other, mine], axis=0),
            )
        elif row_count > 2:
            value = jnp.concatenate([before[c], mine, after[c]], axis=0)
        else:
            value = mine
        extended[c] = value
        whole.append(value)
    first = lax.axis_index("sub") == 0
    west, east = pack(whole, window, (0, n_cols - RIM))
    outer[...] = jnp.where(first, west, east)
    inner[...] = jnp.where(first, east, west)


def pad_rows(padded, c, window, value):
    blank = jnp.zeros((SUBLANES, LANES), f32)
    padded[c, :SUBLANES, :] = blank
    padded[c, SUBLANES + window :, :] = blank
    padded[c, SUBLANES : SUBLANES + window, :] = value


def channels(padded, columns, window):
    vel = [padded[c, SUBLANES : SUBLANES + window, :] for c in range(2)]
    for c in range(2):
        grad_x = roll(vel[c], -1) - roll(vel[c], 1)
        grad_y = (
            padded[c, SUBLANES + 1 : SUBLANES + 1 + window, :]
            - padded[c, SUBLANES - 1 : SUBLANES - 1 + window, :]
        )
        advect = vel[0] * grad_x + vel[1] * grad_y
        for at, value in ((c, vel[c]), (2 + c, advect)):
            high, low_part = split(value)
            columns[0, at * window : (at + 1) * window, :] = high
            columns[1, at * window : (at + 1) * window, :] = low_part


def across_x(columns, x_taps, window):
    wide = 2 * LANES
    high = x_taps[:, wide:]
    low_part = x_taps[:, :wide]
    both = x_taps[:, LANES : LANES + wide]
    main = dot(columns[0, : 2 * window, :], high)
    more = dot(columns[1, : 2 * window, :], high)
    rest = dot(columns[0, : 2 * window, :], low_part)
    flux = dot(columns[0, 2 * window :, :], both)
    flux_more = dot(columns[1, 2 * window :, :], both[:, LANES:])
    means = main[:, :LANES] + (more[:, :LANES] + rest[:, LANES:])
    slopes = main[:, LANES:] + (more[:, LANES:] + rest[:, :LANES])
    fluxes = flux[:, LANES:] + (flux_more + flux[:, :LANES])
    return means, slopes, fluxes


def inner_kernel(geom, extended, x_taps, partial, edges, padded, columns):
    n_rows, n_cols, depth, row_count, window = geom
    lane = iota((window, LANES), 1)
    for c in range(2):
        own = extended[c]
        pad_rows(padded, c, window, own)
        near = jnp.where(lane < RIM + 2, roll(own, RIM), roll(own, HALF - n_cols))
        edges[c] = near
    channels(padded, columns, window)
    for pair, value in enumerate(across_x(columns, x_taps[:LANES, :], window)):
        partial[pair] = value


def filter_kernel(
    geom,
    seam,
    beside,
    edges,
    partial,
    wet,
    turn,
    x_taps,
    y_taps,
    forcing,
    padded,
    columns,
    along,
    pools,
):
    n_rows, n_cols, depth, row_count, window = geom
    sub_at = lax.axis_index("sub")
    out_rows = up_to(n_rows, 2 * SUBLANES)
    west = jnp.where(sub_at == 0, seam[...], beside[...])
    east = jnp.where(sub_at == 0, beside[...], seam[...])
    turned = unpack(west, east, window, turn)
    lane = iota((window, LANES), 1)
    own = (lane >= RIM) & (lane < HALF)
    for c in range(2):
        pad_rows(padded, c, window, jnp.where(own, edges[c], turned[c]))
    channels(padded, columns, window)
    for pair, value in enumerate(across_x(columns, x_taps[LANES:, :], window)):
        value = value + partial[pair]
        high, low_part = split(value)
        for c in range(2):
            at = slice(c * LANES, (c + 1) * LANES)
            along[0, pair, :, at] = high[c * window : (c + 1) * window]
            along[1, pair, :, at] = low_part[c * window : (c + 1) * window]

    main = dot(y_taps[...], along[0, 0])
    more = dot(y_taps[out_rows : 3 * out_rows, :], along[1, 0])
    slope_y = main[out_rows : 2 * out_rows] + (main[:out_rows] + more[:out_rows])
    mean = main[2 * out_rows : 3 * out_rows] + (main[3 * out_rows :] + more[out_rows:])

    def across(pair):
        main = dot(y_taps[2 * out_rows :, :], along[0, pair])
        more = dot(y_taps[2 * out_rows : 3 * out_rows, :], along[1, pair])
        return main[:out_rows] + (main[out_rows:] + more)

    slope_x = across(1)
    flux = across(2)
    mean_u = mean[:n_rows, :LANES]
    mean_v = mean[:n_rows, LANES:]
    mask = wet[...]
    coarse = n_rows // COARSE
    for c in range(2):
        at = slice(c * LANES, (c + 1) * LANES)
        pools[c] = mask * (
            flux[:n_rows, at] - (mean_u * slope_x[:n_rows, at] + mean_v * slope_y[:n_rows, at])
        )
    block = iota((LANES, LANES), 0) // COARSE == iota((LANES, LANES), 1)
    gather = jnp.where(block, deriv_scale / (COARSE * COARSE), 0.0).astype(bf16)
    for c in range(2):
        rows = [pools[c, pl.ds(k, coarse, stride=COARSE), :] for k in range(COARSE)]
        high, low_part = split((rows[0] + rows[1]) + (rows[2] + rows[3]))
        value = dot(high, gather) + dot(low_part, gather)
        forcing[:, c, :] = value[:, : n_cols // COARSE]


EDGE = 4


def np_split(value):
    high = value.astype(bf16)
    return high, (value - high.astype(np.float64)).astype(bf16)


def np_gaussian(distance):
    inside = np.abs(distance) <= R
    return np.where(inside, np.exp(-0.5 * (distance / R) ** 2) / taps_sum(), 0.0)


def x_constant(n_cols):
    lane = np.arange(2 * LANES)[:, None]
    target = np.arange(LANES)[None, :]
    rim = lane - LANES
    column = np.where(
        lane < LANES, lane, np.where(rim < HALF - 1, rim - RIM, rim - HALF + n_cols)
    )
    inside = (
        ((lane >= 1) & (lane < n_cols - 1))
        | ((rim >= 0) & (rim <= RIM))
        | ((rim >= HALF - 1) & (rim < HALF + RIM))
    )
    inside = inside & (target < n_cols)
    away = column - target
    value = np_split(np.where(inside, np_gaussian(away), 0.0))
    slope = np_split(np.where(inside, np_gaussian(away - 1) - np_gaussian(away + 1), 0.0))
    high, low_part = (np.concatenate([value[k], slope[k]], axis=1) for k in range(2))
    return np.concatenate([high, high, low_part], axis=0)


def y_constant(target, source, used, first_row, last_row):
    def step(by):
        at = source + by
        inside = used & (at >= first_row) & (at < last_row)
        return np.where(inside[None, :], np_gaussian(at[None, :] - target[:, None]), 0.0)

    value = np_split(step(0))
    slope = np_split(step(-1) - step(1))
    pad = ((0, up_to(target.shape[0], 2 * SUBLANES) - target.shape[0]), (0, 0))
    high, low_part = (
        np.concatenate([np.pad(slope[k], pad), np.pad(value[k], pad)], axis=0)
        for k in range(2)
    )
    return np.concatenate([high, high, low_part], axis=1)


def y_constants(n_rows, depth, near):
    source = np.arange(up_to(n_rows, 2 * SUBLANES))
    own = y_constant(np.arange(n_rows), source, source < n_rows, 0, n_rows)
    tail = []
    for row_at in range(2):
        source = np.arange(near + depth)
        source = source + n_rows - near if row_at == 0 else source - depth
        late = source >= n_rows - EDGE if row_at == 0 else source < EDGE
        target = np.arange(depth) + (n_rows - depth if row_at == 0 else 0)
        tail.append(
            y_constant(target, source, late, -row_at * n_rows, (2 - row_at) * n_rows)
        )
    return own, np.stack(tail)


def start_all(pairs, sems):
    copies = [pltpu.make_async_copy(a, b, sems.at[i]) for i, (a, b) in enumerate(pairs)]
    for copy in copies:
        copy.start()
    return copies


def pack(whole, rows, bases):
    size = packed_rows(rows)
    lane = iota((size, LANES), 1)
    groups = [[] for _ in range(GROUPS)]
    for c, row, group, _, count in pieces(rows):
        groups[group].append(whole[c][row : row + count])
    spare = GROUPS * size - 2 * rows
    if spare:
        groups[-1].append(jnp.zeros((spare, LANES), f32))
    groups = [jnp.concatenate(group, axis=0) for group in groups]
    out = []
    for base in bases:
        value = roll(groups[-1], (GROUPS - 1) * GROUP - base)
        for g in reversed(range(GROUPS - 1)):
            value = jnp.where(lane < (g + 1) * GROUP, roll(groups[g], g * GROUP - base), value)
        out.append(value)
    return out


def unpack(west, east, rows, turn, only=None):
    parts = [[], []]
    start, stop = only or (0, rows)
    for c, first, group, row, count in pieces(rows):
        row = row + max(start - first, 0)
        count = min(first + count, stop) - max(first, start)
        if count <= 0:
            continue
        low = iota((count, LANES), 1) < HALF
        parts[c].append(
            jnp.where(
                low,
                roll(west[row : row + count, :], -group * GROUP),
                roll(east[row : row + count, :], HALF - group * GROUP),
            )
        )
    u, v = (jnp.concatenate(part, axis=0) for part in parts)
    cosine = turn[0:1, :]
    sine = turn[1:2, :]
    return cosine * u - sine * v, sine * u + cosine * v


def with_own(turned, mine, n_cols):
    lane = iota(mine.shape, 1)
    near = jnp.where(lane < RIM + 2, roll(mine, RIM), roll(mine, HALF - n_cols))
    return jnp.where((lane >= RIM) & (lane < HALF), near, turned)


def open_kernel(
    geom,
    velocity,
    wet_bits,
    east_face,
    seam_turn,
    field,
    outer,
    inner,
    wet,
    turn,
    order,
    vel,
    packed,
    faces,
    turns,
    sems,
):
    n_rows, n_cols, _, _ = geom
    copies = start_all(
        (
            (velocity, vel),
            (wet_bits, packed),
            (east_face, faces),
            (seam_turn, turns),
        ),
        sems,
    )
    copies[1].wait()
    at = iota((n_rows, n_cols), 0)
    word = jnp.broadcast_to(packed[0:1, :], (n_rows, n_cols))
    shift = at
    for j in range(1, n_rows // BITS):
        line = jnp.broadcast_to(packed[j : j + 1, :], (n_rows, n_cols))
        later = at >= j * BITS
        word = jnp.where(later, line, word)
        shift = jnp.where(later, at - j * BITS, shift)
    mask = (jnp.right_shift(word, shift) & 1).astype(f32)
    margin = jnp.zeros((n_rows, LANES - n_cols), f32)
    wet[:, :n_cols] = mask
    wet[:, n_cols:] = margin
    for copy in (copies[0], *copies[2:]):
        copy.wait()
    order[0] = seam_order(faces)
    whole = []
    for c in range(2):
        value = jnp.concatenate([vel[c] * mask, margin], axis=1)
        field[c] = value
        whole.append(value)
    west, east = pack(whole, n_rows, (0, n_cols - RIM))
    first = lax.axis_index("sub") == 0
    outer[...] = jnp.where(first, west, east)
    inner[...] = jnp.where(first, east, west)
    write_turn(faces, turns, turn)


def corner_pieces():
    size = corner_rows()
    cuts = sorted({*range(0, 5 * RIM, RIM), *(size * g for g in range(1, GROUPS))})
    return [
        (a // (2 * RIM), a // RIM % 2, a % RIM, a // size, a % size, b - a)
        for a, b in zip(cuts, cuts[1:])
    ]


def corner_rows():
    return -(-4 * RIM // GROUPS)


def edge_size():
    return up_to(2 * RIM + corner_rows(), SUBLANES)


def edge_kernel(geom, seam, beside, field, turn, edge, west, east, groups):
    n_rows, n_cols, depth, _ = geom
    row_at = lax.axis_index("row")
    first = lax.axis_index("sub") == 0
    west[...] = jnp.where(first, seam[...], beside[...])
    east[...] = jnp.where(first, beside[...], seam[...])
    ends = [
        unpack(west, east, n_rows, turn, only)
        for only in ((n_rows - depth, n_rows), (0, depth))
    ]
    corners = []
    for c in range(2):
        mine = facing(row_at, field[c], depth)
        rims = with_own(jnp.where(row_at == 0, ends[0][c], ends[1][c]), mine, n_cols)
        mine, rims = (
            jnp.where(row_at == 0, value[depth - RIM :], value[:RIM]) for value in (mine, rims)
        )
        edge[c * RIM : (c + 1) * RIM, :] = mine
        corners.append(rims)
    for c, side, row, group, at, count in corner_pieces():
        groups[group, at : at + count, :] = roll(
            corners[c][row : row + count], group * GROUP - side * (HALF - 2)
        )
    size = corner_rows()
    lane = iota((size, LANES), 1)
    value = groups[GROUPS - 1, :size, :]
    for g in reversed(range(GROUPS - 1)):
        value = jnp.where(lane < (g + 1) * GROUP, groups[g, :size, :], value)
    edge[2 * RIM : 2 * RIM + size, :] = value


def facing(row_at, value, depth):
    return jnp.where(row_at == 0, value[value.shape[0] - depth :], value[:depth])


def lay_columns(padded, columns, half, size):
    wide = 2 * LANES
    vel = [padded[c, SUBLANES : SUBLANES + size, :] for c in range(2)]
    for c in range(2):
        grad_x = roll(vel[c], -1) - roll(vel[c], 1)
        grad_y = (
            padded[c, SUBLANES + 1 : SUBLANES + 1 + size, :]
            - padded[c, SUBLANES - 1 : SUBLANES - 1 + size, :]
        )
        advect = vel[0] * grad_x + vel[1] * grad_y
        for at, value in ((c, vel[c]), (2 + c, advect)):
            high, low_part = split(value)
            rows = slice(at * size, (at + 1) * size)
            for k, part in enumerate((high, low_part, high)):
                start = k * wide + half * LANES
                columns[rows, start : start + LANES] = part


def sum_columns(columns, x_taps, size):
    both = dot(columns[: 2 * size, :], x_taps[...])
    flux = dot(columns[2 * size :, :], x_taps[:, :LANES])
    return both[:, :LANES], both[:, LANES:], flux


def keep_along(along, pair, value, size):
    high, low_part = split(value)
    for c in range(2):
        at = slice(c * LANES, (c + 1) * LANES)
        rows = slice(c * size, (c + 1) * size)
        for k, part in enumerate((high, low_part, high)):
            along[pair, k * size : (k + 1) * size, at] = part[rows]


def across_y(y_taps, along, size):
    both = dot(y_taps[...], along[0])
    slope_x = dot(y_taps[size:, :], along[1])
    flux = dot(y_taps[size:, :], along[2])
    return both[:size], both[size:], slope_x, flux


def pool(smooth, mask, pools):
    slope_y, mean, slope_x, flux = smooth
    count = mask.shape[0]
    mean_u = mean[:, :LANES]
    mean_v = mean[:, LANES:]
    block = iota((LANES, LANES), 0) // COARSE == iota((LANES, LANES), 1)
    gather = jnp.where(block, deriv_scale / (COARSE * COARSE), 0.0).astype(bf16)
    out = []
    for c in range(2):
        at = slice(c * LANES, (c + 1) * LANES)
        pools[c] = mask * (flux[:, at] - (mean_u * slope_x[:, at] + mean_v * slope_y[:, at]))
        rows = [
            pools[c, pl.ds(k, count // COARSE, stride=COARSE), :] for k in range(COARSE)
        ]
        high, low_part = split((rows[0] + rows[1]) + (rows[2] + rows[3]))
        out.append(dot(high, gather) + dot(low_part, gather))
    return out


def own_kernel(
    geom,
    west,
    east,
    field,
    turn,
    wet,
    x_source,
    y_source,
    tail_source,
    part,
    tail,
    tail_wet,
    tail_rims,
    x_taps,
    tail_taps,
    padded,
    columns,
    along,
    pools,
    y_taps,
    sems,
):
    n_rows, n_cols, depth, near = geom
    row_at = lax.axis_index("row")
    copies = start_all(
        ((x_source, x_taps), (y_source, y_taps), (tail_source.at[row_at], tail_taps)), sems
    )
    size = up_to(n_rows, 2 * SUBLANES)
    blank = jnp.zeros((size - n_rows, LANES), f32)
    turned = unpack(west, east, n_rows, turn)
    for c in range(2):
        mine = field[c]
        rims = with_own(turned[c], mine, n_cols)
        tail_rims[c] = facing(row_at, rims, near)
        for half, value in enumerate((mine, rims)):
            if size > n_rows:
                value = jnp.concatenate([value, blank], axis=0)
            pad_rows(padded.at[half], c, size, value)
    for half in range(2):
        lay_columns(padded.at[half], columns, half, size)
    for copy in copies:
        copy.wait()
    at = iota((2 * size, LANES), 0) % size
    early = jnp.where(row_at == 0, 0, EDGE)
    late = jnp.where(row_at == 0, n_rows - EDGE, n_rows)
    kept = (at >= early) & (at < late)
    for pair, value in enumerate(sum_columns(columns, x_taps, size)):
        keep_along(along, pair, jnp.where(kept, value, 0.0), size)
    smooth = [value[:n_rows] for value in across_y(y_taps, along, size)]
    mask = wet[...]
    for i, value in enumerate(smooth):
        tail[i] = facing(row_at, value, depth)
    tail_wet[...] = facing(row_at, mask, depth)
    for c, value in enumerate(pool(smooth, mask, pools)):
        part[:, c, :] = value[:, : n_cols // COARSE]


def close_kernel(
    geom,
    edge,
    field,
    part,
    tail,
    tail_wet,
    tail_rims,
    x_taps,
    tail_taps,
    forcing,
    padded,
    columns,
    along,
    pools,
):
    n_rows, n_cols, depth, near = geom
    row_at = lax.axis_index("row")
    size = near + depth
    sides = {}
    for c, side, _, group, at, count in corner_pieces():
        at = at + 2 * RIM
        piece = roll(edge[at : at + count, :], side * (HALF - 2) - group * GROUP)
        sides.setdefault((c, side), []).append(piece)
    for c in range(2):
        ones = [jnp.concatenate(sides[c, side], axis=0) for side in range(2)]
        low = iota((RIM, LANES), 1) < RIM + 2
        for half, (own, far) in enumerate(
            (
                (facing(row_at, field[c], near), edge[c * RIM : (c + 1) * RIM, :]),
                (tail_rims[c], jnp.where(low, ones[0], ones[1])),
            )
        ):
            spare = jnp.zeros((depth - RIM, LANES), f32)
            value = jnp.where(
                row_at == 0,
                jnp.concatenate([own, far, spare], axis=0),
                jnp.concatenate([spare, far, own], axis=0),
            )
            pad_rows(padded.at[half], c, size, value)
    for half in range(2):
        lay_columns(padded.at[half], columns, half, size)
    for pair, value in enumerate(sum_columns(columns, x_taps, size)):
        keep_along(along, pair, value, size)
    smooth = across_y(tail_taps, along, up_to(depth, 2 * SUBLANES))
    smooth = [value[:depth] + tail[i] for i, value in enumerate(smooth)]
    forcing[...] = part[...]
    start = jnp.where(row_at == 0, (n_rows - depth) // COARSE, 0)
    for c, value in enumerate(pool(smooth, tail_wet[...], pools)):
        forcing[pl.ds(start, depth // COARSE), c, :] = value[:, : n_cols // COARSE]


VMEM_SPEC = pl.BlockSpec(memory_space=pltpu.VMEM)
SMEM_SPEC = pl.BlockSpec(memory_space=pltpu.SMEM)
HBM_SPEC = pl.BlockSpec(memory_space=pltpu.HBM)


def choose(index, branches, *operands):
    closed = jax.make_jaxpr(lambda i, *rest: lax.switch(i, branches, *rest))(index, *operands)
    values = dict(zip(closed.jaxpr.constvars, closed.consts))
    values.update(zip(closed.jaxpr.invars, jax.tree.leaves((index, *operands))))

    def read(atom):
        return atom.val if hasattr(atom, "val") else values[atom]

    for eqn in closed.jaxpr.eqns:
        taken = [read(atom) for atom in eqn.invars]
        if eqn.primitive is lax.clamp_p:
            given = taken[1]
        else:
            given = eqn.primitive.bind(*taken, **eqn.params)
        if not eqn.primitive.multiple_results:
            given = [given]
        values.update(zip(eqn.outvars, given))
    return [read(atom) for atom in closed.jaxpr.outvars]


def seam_pairs(order, subs):
    pairs = []
    for west, east in enumerate(order):
        pairs += [(west * subs + subs - 1, east * subs), (east * subs, west * subs + subs - 1)]
    return pairs


def beside_pairs(subs):
    return [(i, subs - 1 - i) for i in range(subs)]


def exchange(order, east_face, outer, inner, finish):
    faces = east_face.shape[0]
    subs = lax.axis_size("sub")
    beside = beside_pairs(subs)

    def swap(order, outer, inner):
        seam = lax.ppermute(outer, ("tile", "sub"), seam_pairs(order, subs))
        return finish(seam, lax.ppermute(inner, "sub", beside))

    if faces <= SWITCHED_FACES:
        orders = itertools.permutations(range(faces))
        branches = [functools.partial(swap, order) for order in orders]
        return lax.switch(order[0], branches, outer, inner)
    tile_at = lax.axis_index("tile")
    sub_at = lax.axis_index("sub")
    west = jnp.sum(jnp.where(east_face == tile_at, jnp.arange(faces, dtype=jnp.int32), 0))
    east = lax.dynamic_index_in_dim(east_face, tile_at, 0, keepdims=False)
    gathered = lax.all_gather(lax.ppermute(outer, "sub", beside), "tile")
    partner = jnp.where(sub_at == 0, west, east)
    seam = lax.dynamic_index_in_dim(gathered, partner, 0, keepdims=False)
    return finish(seam, lax.ppermute(inner, "sub", beside))


def in_hbm(value):
    return pltpu.with_memory_space_constraint(value, pltpu.HBM)


def paired(velocity, wet_bits, east_face, seam_turn):
    _, n_rows, n_cols = velocity.shape
    depth = up_to(RIM, SUBLANES)
    near = up_to(depth + SUBLANES, 2 * SUBLANES) - depth
    geom = (n_rows, n_cols, depth, near)
    size = up_to(n_rows, 2 * SUBLANES)
    end = near + depth
    wide = 2 * LANES
    coarse = n_rows // COARSE
    params = pltpu.CompilerParams(vmem_limit_bytes=16 << 20)
    shape = jax.ShapeDtypeStruct
    kernel = lambda body, name, **rest: pl.pallas_call(
        functools.partial(body, geom), name=name, compiler_params=params, **rest
    )
    packed = shape((packed_rows(n_rows), LANES), f32)
    own_taps, tail_taps = y_constants(n_rows, depth, near)
    taps = (x_constant(n_cols), own_taps, tail_taps)
    field, outer, inner, wet, turn, order = kernel(
        open_kernel,
        "open",
        out_shape=(
            shape((2, n_rows, LANES), f32),
            packed,
            packed,
            shape((n_rows, LANES), f32),
            shape((SUBLANES, LANES), f32),
            pltpu.SMEM((1,), jnp.int32),
        ),
        in_specs=[HBM_SPEC] * 4,
        out_specs=(VMEM_SPEC,) * 5 + (SMEM_SPEC,),
        scratch_shapes=[
            pltpu.VMEM(velocity.shape, f32),
            pltpu.VMEM(wet_bits.shape, jnp.int32),
            pltpu.SMEM(east_face.shape, jnp.int32),
            pltpu.SMEM(seam_turn.shape, jnp.int32),
            pltpu.SemaphoreType.DMA((4,)),
        ],
    )(*(in_hbm(value) for value in (velocity, wet_bits, east_face, seam_turn)))
    subs = lax.axis_size("sub")
    part_shape = shape((coarse, 2, n_cols // COARSE), f32)

    def branch(order, outer, inner, field, turn):
        seam = lax.ppermute(outer, ("tile", "sub"), seam_pairs(order, subs))
        beside = lax.ppermute(inner, "sub", beside_pairs(subs))
        return kernel(
            edge_kernel,
            "edge",
            out_shape=(
                shape((edge_size(), LANES), f32),
                packed,
                packed,
            ),
            in_specs=[VMEM_SPEC] * 4,
            out_specs=(VMEM_SPEC,) * 3,
            scratch_shapes=[
                pltpu.VMEM((GROUPS, up_to(corner_rows(), SUBLANES), LANES), f32)
            ],
        )(seam, beside, field, turn)

    orders = itertools.permutations(range(east_face.shape[0]))
    branches = [functools.partial(branch, order) for order in orders]
    edge, west, east = choose(order[0], branches, outer, inner, field, turn)
    edge = lax.ppermute(edge, "row", [(0, 1), (1, 0)])
    part, tail, tail_wet, tail_rims, x_taps, tail_taps = kernel(
        own_kernel,
        "own",
        out_shape=(
            part_shape,
            shape((4, depth, wide), f32),
            shape((depth, LANES), f32),
            shape((2, near, LANES), f32),
            shape(taps[0].shape, bf16),
            shape(taps[2].shape[1:], bf16),
        ),
        in_specs=[VMEM_SPEC] * 5 + [HBM_SPEC] * 3,
        out_specs=(VMEM_SPEC,) * 6,
        scratch_shapes=[
            pltpu.VMEM((2, 2, size + 2 * SUBLANES, LANES), f32),
            pltpu.VMEM((4 * size, 3 * wide), bf16),
            pltpu.VMEM((3, 3 * size, wide), bf16),
            pltpu.VMEM((2, n_rows, LANES), f32),
            pltpu.VMEM(taps[1].shape, bf16),
            pltpu.SemaphoreType.DMA((3,)),
        ],
        cost_estimate=pl.CostEstimate(
            flops=1 << 30, bytes_accessed=1 << 22, transcendentals=0
        ),
    )(west, east, field, turn, wet, *(in_hbm(jnp.asarray(value)) for value in taps))
    forcing = kernel(
        close_kernel,
        "close",
        out_shape=part_shape,
        in_specs=[VMEM_SPEC] * 8,
        out_specs=VMEM_SPEC,
        scratch_shapes=[
            pltpu.VMEM((2, 2, end + 2 * SUBLANES, LANES), f32),
            pltpu.VMEM((4 * end, 3 * wide), bf16),
            pltpu.VMEM((3, 3 * end, wide), bf16),
            pltpu.VMEM((2, depth, LANES), f32),
        ],
    )(edge, field, part, tail, tail_wet, tail_rims, x_taps, tail_taps)
    return jnp.transpose(forcing, (1, 0, 2))


def on_device(velocity, wet_bits, east_face, seam_turn):
    _, n_rows, n_cols = velocity.shape
    row_count = lax.axis_size("row")
    if row_count == 2 and east_face.shape[0] <= SWITCHED_FACES:
        return paired(velocity, wet_bits, east_face, seam_turn)
    depth = up_to(RIM, SUBLANES)
    sides = min(row_count - 1, 2)
    window = n_rows + sides * depth
    geom = (n_rows, n_cols, depth, row_count, window)
    sent = depth * max(sides, 1)
    wide = 2 * LANES
    out_rows = up_to(n_rows, 2 * SUBLANES)
    params = pltpu.CompilerParams(vmem_limit_bytes=16 << 20)
    shape = jax.ShapeDtypeStruct
    field, rows, wet = pl.pallas_call(
        functools.partial(mask_kernel, geom),
        out_shape=(
            shape((2, n_rows, LANES), f32),
            shape((2, sent, LANES), f32),
            shape((n_rows, LANES), f32),
        ),
        in_specs=[HBM_SPEC] * 2,
        out_specs=(VMEM_SPEC,) * 3,
        scratch_shapes=[
            pltpu.VMEM(velocity.shape, f32),
            pltpu.VMEM(wet_bits.shape, jnp.int32),
            pltpu.SemaphoreType.DMA((2,)),
        ],
        compiler_params=params,
        name="mask",
    )(
        pltpu.with_memory_space_constraint(velocity, pltpu.HBM),
        pltpu.with_memory_space_constraint(wet_bits, pltpu.HBM),
    )
    order, turn, x_taps, y_taps = pl.pallas_call(
        functools.partial(prepare_kernel, geom),
        out_shape=(
            shape((1,), jnp.int32),
            shape((SUBLANES, LANES), f32),
            shape((wide, 2 * wide), bf16),
            shape((4 * out_rows, window), bf16),
        ),
        in_specs=[HBM_SPEC] * 2,
        out_specs=(SMEM_SPEC,) + (VMEM_SPEC,) * 3,
        scratch_shapes=[
            pltpu.SMEM(east_face.shape, jnp.int32),
            pltpu.SMEM(seam_turn.shape, jnp.int32),
            pltpu.SemaphoreType.DMA((2,)),
        ],
        compiler_params=params,
        name="prepare",
    )(
        pltpu.with_memory_space_constraint(east_face, pltpu.HBM),
        pltpu.with_memory_space_constraint(seam_turn, pltpu.HBM),
    )
    if row_count == 2:
        before = lax.ppermute(rows, "row", [(0, 1), (1, 0)])
        after = before
    elif row_count > 2:
        up = [(i, i + 1) for i in range(row_count - 1)]
        before = lax.ppermute(rows[:, depth:], "row", up)
        after = lax.ppermute(rows[:, :depth], "row", [(j, i) for i, j in up])
    else:
        before = after = rows
    extended, outer, inner = pl.pallas_call(
        functools.partial(extend_kernel, geom),
        out_shape=(
            shape((2, window, LANES), f32),
            shape((packed_rows(window), LANES), f32),
            shape((packed_rows(window), LANES), f32),
        ),
        in_specs=[VMEM_SPEC] * 3,
        out_specs=(VMEM_SPEC,) * 3,
        compiler_params=params,
        name="extend",
    )(field, before, after)

    def finish(seam, beside):
        partial, edges = pl.pallas_call(
            functools.partial(inner_kernel, geom),
            out_shape=(
                shape((3, 2 * window, LANES), f32),
                shape((2, window, LANES), f32),
            ),
            in_specs=[VMEM_SPEC] * 2,
            out_specs=(VMEM_SPEC,) * 2,
            scratch_shapes=[
                pltpu.VMEM((2, window + 2 * SUBLANES, LANES), f32),
                pltpu.VMEM((2, 4 * window, LANES), bf16),
            ],
            compiler_params=params,
            name="inner",
        )(extended, x_taps)
        return pl.pallas_call(
            functools.partial(filter_kernel, geom),
            out_shape=shape((n_rows // COARSE, 2, n_cols // COARSE), f32),
            in_specs=[VMEM_SPEC] * 8,
            out_specs=VMEM_SPEC,
            scratch_shapes=[
                pltpu.VMEM((2, window + 2 * SUBLANES, LANES), f32),
                pltpu.VMEM((2, 4 * window, LANES), bf16),
                pltpu.VMEM((2, 3, window, wide), bf16),
                pltpu.VMEM((2, n_rows, LANES), f32),
            ],
            compiler_params=params,
            name="filter",
        )(seam, beside, edges, partial, wet, turn, x_taps, y_taps)

    forcing = exchange(order, east_face, outer, inner, finish)
    return jnp.transpose(forcing, (1, 0, 2))


def solution(mesh):
    placed = (
        P(None, ("grp", "row"), ("tile", "sub")),
        P(("grp", "row"), ("tile", "sub")),
        P(),
        P(),
    )
    return jax.shard_map(
        on_device,
        mesh=mesh,
        in_specs=placed,
        out_specs=P(None, ("grp", "row"), ("tile", "sub")),
        check_vma=False,
    )
```
